32 devices in a mesh: dp: 8 (over z, core), fsdp: 4 (over y, x).
Axes of the slice: x: 2, y: 2, z: 4, core: 2. Of those that a mesh axis runs over, the one named last changes fastest.
Arguments:
- inputs: bfloat16 [4, 800, 48, 256], P('fsdp', None, 'dp'), may hold values from -20 to 20, as said below
- out_grad: bfloat16 [4, 800, 48, 256], P('fsdp', None, 'dp'), may hold values from -6 to 6
- ocean_mask: int32 [48, 256], P('dp'), may hold values from 0 to 1, as said below
- rollout_lengths: int32 [4], replicated, may hold values from 1 to 8
- conv_weight: float32 [800, 49], P('fsdp'), may hold values from -0.875 to 0.875
- norm_gain: float32 [800], P('fsdp'), may hold values from 0.25 to 1.75
- norm_bias: float32 [800], P('fsdp'), may hold values from -3 to 3
- expand_weight: bfloat16 [800, 3200], P('fsdp'), may hold values from -0.21875 to 0.21875
- expand_bias: bfloat16 [3200], P('fsdp'), may hold values from -3 to 3
- project_weight: bfloat16 [800, 3200], P('fsdp'), may hold values from -0.21875 to 0.21875
- project_bias: bfloat16 [800], P('fsdp'), may hold values from -3 to 3
Outputs:
- block_out: bfloat16 [4, 800, 48, 256], P('fsdp', None, 'dp')
- input_grad: float32 [4, 800, 48, 256], P('fsdp', None, 'dp')
- conv_weight_grad: float32 [800, 49], P('fsdp')
- norm_gain_grad: float32 [800], P('fsdp')
- norm_bias_grad: float32 [800], P('fsdp')
- expand_weight_grad: float32 [800, 3200], P('fsdp')
- expand_bias_grad: float32 [3200], P('fsdp')
- project_weight_grad: float32 [800, 3200], P('fsdp')
- project_bias_grad: float32 [800], P('fsdp')
- chan_mean: float32 [800], replicated
- chan_std: float32 [800], replicated
The draws below stay inside these ranges and needn't reach their ends.
Inputs may be any that keep to these rules, and one draw needn't show every extreme that they name: `inputs`: fields whose spread and per-channel offset change with the row. `ocean_mask`: 1 marks ocean, 0 land; the first column of every row is ocean.
All inputs are finite; a program needn't handle non-finite values.
Results may differ from the reference program's by a relative error of at most 0.0058.
Values may be sent and summed in bfloat16 or wider, within the bound.
No kernel may reach another device: no remote copies, remote signals or barrier semaphores. Data moves between devices by JAX's collectives and lax.ppermute only.
A program may use at most 192 MiB of HBM per device.

```python
import jax
import jax.numpy as jnp
from jax import lax

C = 800
HID = 3200
KS = 7
ROLLOUT = 8
W = 256
SAMPLES = 4
H = 48


def draw_inputs(key, part):
    key_base, key_shift = jax.random.split(key, 2)
    rows = jnp.arange(H, dtype=jnp.float32) / max(H - 1, 1)
    spread = (1.0 + 2.0 * rows)[None, None, :, None]
    offset = jax.random.truncated_normal(key_shift, -4.0, 4.0, (1, C, 1, 1), jnp.float32) * (rows[None, None, :, None] - 0.5)
    base = jax.random.truncated_normal(key_base, -5.0, 5.0, (SAMPLES, C, H, W), jnp.float32)
    return (base * spread + offset).astype(jnp.bfloat16)


def draw_ocean_mask(key, part):
    levels = jax.random.randint(key, (H, W), 0, 4)
    columns = jnp.arange(W)[None, :]
    return jnp.where(columns == 0, 1, jnp.where(levels > 0, 1, 0)).astype(jnp.int32)


def plant(values, own_key, smallest, top_value):
    longest = values.shape.index(max(values.shape))
    spots = []
    for shift in (0, 1):
        where = [jax.random.randint(jax.random.fold_in(own_key, axis), (), 0, length) for axis, length in enumerate(values.shape)]
        where[longest] = (where[longest] + shift) % values.shape[longest]
        spots.append(tuple(where))
    return values.at[spots[0]].set(smallest).at[spots[1]].set(top_value)


def level_of(own_key, extent, cuts, smallest, largest):
    factor_of, own = 1.0, jax.random.fold_in(own_key, 6)
    for position, shards_of in cuts:
        steps = jnp.exp(jax.random.uniform(jax.random.fold_in(own, position), (shards_of,), jnp.float32, smallest / len(cuts), largest / len(cuts)))
        factor_of = factor_of * jnp.repeat(steps, extent[position] // shards_of).reshape([-1 if axis == position else 1 for axis in range(len(extent))])
    return factor_of


def scatter_about(key, extent, scale, most, cuts=(), kind=jnp.bfloat16):
    level = level_of(key, extent, cuts, -0.22, 0.18) if cuts else 1.0
    entries = jax.random.normal(key, extent, jnp.float32) * scale * level
    return jnp.minimum(jnp.maximum(entries, -most), most).astype(kind)


def setup_inputs(seed: int = 0) -> dict:
    streams_of = jax.random.split(jax.random.key(seed), 12)
    inputs = draw_inputs(jax.random.fold_in(streams_of[11], 71), 0)
    out_grad = scatter_about(streams_of[1], (SAMPLES, C, H, W), 1.0, 6.0, ((0, 4), (2, 8)))
    ocean_mask = draw_ocean_mask(jax.random.fold_in(streams_of[11], 71), 0)
    rollout_lengths = plant(jax.random.randint(streams_of[3], (SAMPLES,), 1, ROLLOUT + 1), jax.random.fold_in(streams_of[3], 1), 1, ROLLOUT).astype(jnp.int32)
    conv_weight = scatter_about(streams_of[4], (C, KS * KS), (KS * KS) ** -0.5, 0.875, ((0, 4),), jnp.float32)
    norm_gain = jnp.clip(1.0 + 0.15 * jax.random.normal(streams_of[5], (C,), jnp.float32), 0.25, 1.75)
    norm_bias = scatter_about(streams_of[6], (C,), 0.5, 3.0, ((0, 4),), jnp.float32)
    expand_weight = scatter_about(streams_of[7], (C, HID), C ** -0.5, 0.21875, ((0, 4),))
    expand_bias = scatter_about(streams_of[8], (HID,), 0.5, 3.0, ((0, 4),))
    project_weight = scatter_about(streams_of[9], (C, HID), (HID // 4) ** -0.5, 0.21875, ((0, 4),))
    project_bias = scatter_about(streams_of[10], (C,), 0.5, 3.0, ((0, 4),))
    return dict(inputs=inputs, out_grad=out_grad, ocean_mask=ocean_mask, rollout_lengths=rollout_lengths, conv_weight=conv_weight, norm_gain=norm_gain, norm_bias=norm_bias, expand_weight=expand_weight, expand_bias=expand_bias, project_weight=project_weight, project_bias=project_bias)


EPS = 1e-05

@jax.custom_vjp
def low(v):
    return lax.optimization_barrier(v.astype(jnp.bfloat16)).astype(jnp.float32)

@jax.custom_vjp
def low_back(v):
    return v

def low_keep(v):
    return (low(v), None)

def low_pass(kept, grad):
    return (grad,)

def back_keep(v):
    return (v, None)

def back_low(kept, grad):
    return (low(grad),)
low.defvjp(low_keep, low_pass)
low_back.defvjp(back_keep, back_low)

def conv_sample(field, conv_weight):
    reach = KS // 2
    padded = jnp.pad(field, ((0, 0), (reach, reach), (0, 0)))
    widened = jnp.concatenate([padded[:, :, -reach:], padded, padded[:, :, :reach]], axis=2)
    total = jnp.zeros(field.shape, jnp.float32)
    for row_step in range(KS):
        for col_step in range(KS):
            tap_weight = conv_weight[:, KS * row_step + col_step][:, None, None]
            total = total + tap_weight * widened[:, row_step:row_step + H, col_step:col_step + W]
    return total

def forward(inputs, conv_weight, norm_gain, norm_bias, expand_weight, expand_bias, project_weight, project_bias, weight, ocean_count):
    conv_out = lax.map(jax.checkpoint(lambda field: conv_sample(field, conv_weight)), inputs)
    conv_out = low_back(conv_out)
    weight_c = weight[:, None]
    chan_mean = lax.optimization_barrier(jnp.sum(weight_c * conv_out, axis=(0, 2, 3))) / ocean_count
    centered = conv_out - chan_mean[None, :, None, None]
    variance = lax.optimization_barrier(jnp.sum(weight_c * centered * centered, axis=(0, 2, 3))) / ocean_count
    inv_std = lax.rsqrt(variance + EPS)

    def one_sample(items):
        cen, field, mask_rows = items
        normalized = cen * inv_std[:, None, None]
        activation = low(normalized * norm_gain[:, None, None] + norm_bias[:, None, None]).reshape(C, H * W)
        hidden_pre = jnp.dot(expand_weight.T, activation, precision=lax.Precision.HIGHEST, preferred_element_type=jnp.float32) + expand_bias[:, None]
        hidden_pre = low_back(hidden_pre)
        hidden = low(jax.nn.gelu(hidden_pre))
        branch = jnp.dot(project_weight, hidden, precision=lax.Precision.HIGHEST, preferred_element_type=jnp.float32) + project_bias[:, None]
        branch = low_back(branch)
        return (field + branch.reshape(C, H, W)) * mask_rows[None]
    block_out = lax.map(jax.checkpoint(one_sample), (centered, inputs, weight))
    return (block_out, (chan_mean, jnp.sqrt(variance + EPS)))

def reference(inputs, out_grad, ocean_mask, rollout_lengths, conv_weight, norm_gain, norm_bias, expand_weight, expand_bias, project_weight, project_bias):
    sample_ids = jnp.arange(SAMPLES, dtype=jnp.int32)
    live_flag = jnp.where(sample_ids % ROLLOUT < rollout_lengths, 1.0, 0.0).astype(jnp.float32)
    weight = live_flag[:, None, None] * ocean_mask.astype(jnp.float32)[None]
    ocean_count = jnp.sum(weight)

    def wrapped(x_in, cw, gain, bias, ew, eb, pw, pb):
        return forward(x_in, cw, gain, bias, ew, eb, pw, pb, weight, ocean_count)
    block_out, pull, stats = jax.vjp(wrapped, inputs.astype(jnp.float32), conv_weight, norm_gain, norm_bias, expand_weight.astype(jnp.float32), expand_bias.astype(jnp.float32), project_weight.astype(jnp.float32), project_bias.astype(jnp.float32), has_aux=True)
    grads = pull(out_grad.astype(jnp.float32))
    return (block_out.astype(jnp.bfloat16), grads[0], grads[1], grads[2], grads[3], grads[4], grads[5], grads[6], grads[7], stats[0], stats[1])
```

```python
import functools

import jax
import jax.numpy as jnp
from jax import lax
from jax.experimental import pallas as pl
from jax.experimental.pallas import tpu as pltpu
from jax.sharding import PartitionSpec as P

KS = 7
REACH = KS // 2
TAPS = KS * KS
ROLLOUT = 8
EPS = 1e-05
F32, BF16 = jnp.float32, jnp.bfloat16
GRP = 16
TILE = 256
MIB = 2**20
GELU_A = 0.7978845608028654
GELU_B = 0.044715
NT = (((1,), (1,)), ((), ()))


def params(limit):
    return pltpu.CompilerParams(vmem_limit_bytes=limit * MIB)


def cost(flops, nbytes, trans=0):
    return pl.CostEstimate(flops=int(flops), bytes_accessed=int(nbytes), transcendentals=int(trans))


def whole(shape):
    zeros = (0,) * len(shape)
    return pl.BlockSpec(shape, lambda *g: zeros, pipeline_mode=pl.Buffered(1))


def roll_lanes(v, shift):
    shift %= v.shape[-1]
    return v if shift == 0 else pltpu.roll(v, shift, v.ndim - 1)


def columns_of(rows_ref):
    pieces = []
    for k in range(0, rows_ref.shape[1], 128):
        block = jnp.concatenate([rows_ref[:, k : k + 128], jnp.zeros((120, 128), F32)], axis=0)
        pieces.append(block.T)
    return jnp.concatenate(pieces, axis=0)


def rows_of(cols_ref, out_ref):
    for k in range(0, cols_ref.shape[0], 128):
        out_ref[:, k : k + 128] = cols_ref[k : k + 128, :].T[0:8]


def spread_taps(taps):
    channels = taps.shape[0]
    by_col = taps.reshape(channels, KS, KS).transpose(2, 0, 1)
    own = jnp.arange(channels)[:, None] % GRP == jnp.arange(GRP)[None, :]
    spread = jnp.where(own[None, :, None, :], by_col[..., None], 0.0)
    spread = spread.reshape(KS, channels, KS * GRP)
    spread = jnp.pad(spread, ((0, 0), (0, 0), (0, 128 - KS * GRP)))
    high = lax.reduce_precision(spread, 8, 7)
    return jnp.stack([high.astype(BF16), (spread - high).astype(BF16)])


def conv_rows(field_ref, taps_ref, s, rows, flip):
    x = field_ref[:, s, :].reshape((rows + 2 * REACH) * GRP, field_ref.shape[-1])
    parts = [taps_ref[h, :, s, :].reshape(KS * GRP, 128)[:, : KS * GRP] for h in range(2)]
    taps = jnp.concatenate(parts, axis=1)
    out = []
    for r in range(rows):
        src = rows - 1 - r if flip else r
        window = x[src * GRP : (src + KS) * GRP]
        sums = jnp.dot(taps, jnp.concatenate([window, window], axis=0), preferred_element_type=F32)
        acc = None
        for j in range(KS):
            moved = roll_lanes(sums[j * GRP : (j + 1) * GRP], j - REACH if flip else REACH - j)
            acc = moved if acc is None else acc + moved
        out.append(acc)
    return out


def conv_kernel(n_ref, x_ref, up_ref, dn_ref, e_ref, m_ref, out_ref, st_ref, field_ref, cols_ref):
    rows, block = x_ref.shape[0], x_ref.shape[1]
    step = pl.program_id(0)
    count = n_ref[0]
    inv_n = n_ref[1]
    field_ref[0:REACH] = up_ref[...]
    field_ref[REACH : REACH + rows] = x_ref[...]
    field_ref[REACH + rows :] = dn_ref[...]

    @pl.when(step == 0)
    def _():
        cols_ref[...] = jnp.full(cols_ref.shape, count, F32)

    lane = lax.broadcasted_iota(jnp.int32, (GRP, 128), 1)
    for g in range(block // GRP):
        s = pl.ds(g * GRP, GRP)
        acc = conv_rows(field_ref, e_ref, s, rows, False)
        total = None
        for r in range(rows):
            out_ref[r, s, :] = acc[r]
            v = acc[r] * m_ref[r]
            total = v if total is None else total + v
        mean = jnp.sum(total, axis=-1, keepdims=True) * inv_n
        total = None
        for r in range(rows):
            d = acc[r] - mean
            v = d * d * m_ref[r]
            total = v if total is None else total + v
        dev = jnp.sum(total, axis=-1, keepdims=True)
        at = pl.multiple_of(step * block + g * GRP, GRP)
        cols_ref[pl.ds(at, GRP), :] = jnp.where(lane == 0, mean, dev)

    @pl.when(step == pl.num_programs(0) - 1)
    def _():
        rows_of(cols_ref, st_ref)


def conv_forward(x, up, dn, spread, m16, counts, padded, block):
    rows, channels, width = x.shape
    return pl.pallas_call(
        conv_kernel,
        grid=(channels // block,),
        in_specs=[
            pl.BlockSpec(memory_space=pltpu.SMEM),
            pl.BlockSpec((rows, block, width), lambda g: (0, g, 0)),
            pl.BlockSpec((REACH, block, width), lambda g: (0, g, 0)),
            pl.BlockSpec((REACH, block, width), lambda g: (0, g, 0)),
            pl.BlockSpec((2, KS, block, 128), lambda g: (0, 0, g, 0)),
            whole((rows, GRP, width)),
        ],
        out_specs=[
            pl.BlockSpec((rows, block, width), lambda g: (0, g, 0)),
            pl.BlockSpec((8, padded), lambda g: (0, 0)),
        ],
        out_shape=[
            jax.ShapeDtypeStruct((rows, channels, width), F32),
            jax.ShapeDtypeStruct((8, padded), F32),
        ],
        scratch_shapes=[
            pltpu.VMEM((rows + 2 * REACH, block, width), BF16),
            pltpu.VMEM((padded, 128), F32),
        ],
        compiler_params=params(24),
        cost_estimate=cost(20e9, 12e6),
        name="conv_forward",
    )(counts, x, up, dn, spread, m16)


def input_grad_kernel(g_ref, up_ref, dn_ref, e_ref, og_ref, m_ref, out_ref, field_ref):
    rows, block = g_ref.shape[0], g_ref.shape[1]
    last = rows + 2 * REACH - 1
    for q in range(REACH):
        field_ref[last - q] = up_ref[q]
        field_ref[REACH - 1 - q] = dn_ref[q]
    for q in range(rows):
        field_ref[last - REACH - q] = g_ref[q]
    for g in range(block // GRP):
        s = pl.ds(g * GRP, GRP)
        acc = conv_rows(field_ref, e_ref, s, rows, True)
        for r in range(rows):
            out_ref[r, s, :] = og_ref[r, s, :].astype(F32) * m_ref[r] + acc[r]


def input_gradient(grad, up, dn, spread, og, m16, block):
    rows, channels, width = grad.shape
    return pl.pallas_call(
        input_grad_kernel,
        grid=(channels // block,),
        in_specs=[
            pl.BlockSpec((rows, block, width), lambda g: (0, g, 0)),
            pl.BlockSpec((REACH, block, width), lambda g: (0, g, 0)),
            pl.BlockSpec((REACH, block, width), lambda g: (0, g, 0)),
            pl.BlockSpec((2, KS, block, 128), lambda g: (0, 0, g, 0)),
            pl.BlockSpec((rows, block, width), lambda g: (0, g, 0)),
            whole((rows, GRP, width)),
        ],
        out_specs=pl.BlockSpec((rows, block, width), lambda g: (0, g, 0)),
        out_shape=jax.ShapeDtypeStruct((rows, channels, width), F32),
        scratch_shapes=[pltpu.VMEM((rows + 2 * REACH, block, width), BF16)],
        compiler_params=params(24),
        cost_estimate=cost(18e9, 15e6),
        name="input_gradient",
    )(grad, up, dn, spread, og, m16)


def tap_grad_kernel(x_ref, up_ref, dn_ref, g_ref, out_ref, field_ref):
    rows, block, width = x_ref.shape
    field_ref[0:REACH] = up_ref[...]
    field_ref[REACH : REACH + rows] = x_ref[...]
    field_ref[REACH + rows :] = dn_ref[...]
    lane = lax.broadcasted_iota(jnp.int32, (GRP, 128), 1)
    own = lax.broadcasted_iota(jnp.int32, (GRP, 128), 0) == lane % GRP
    for g in range(block // GRP):
        s = pl.ds(g * GRP, GRP)
        x = field_ref[:, s, :].reshape((rows + 2 * REACH) * GRP, width)
        fields = jnp.concatenate([x[r * GRP : (r + KS) * GRP] for r in range(rows)], axis=1)
        grads = []
        for j in range(KS):
            moved = [roll_lanes(g_ref[r, s, :], j - REACH) for r in range(rows)]
            grads.append(jnp.concatenate(moved, axis=1))
        grads = jnp.concatenate(grads, axis=0)
        sums = lax.dot_general(grads, fields, NT, preferred_element_type=F32)
        sums = jnp.concatenate([sums, jnp.zeros((KS * GRP, 128 - KS * GRP), F32)], axis=1)
        out = None
        for j in range(KS):
            acc = jnp.where(own, sums[j * GRP : (j + 1) * GRP], 0.0)
            for k in (8, 4, 2, 1):
                acc = acc + pltpu.roll(acc, 128 - k, 1)
            acc = roll_lanes(acc, j)
            out = acc if out is None else jnp.where(lane % GRP == j, acc, out)
        out_ref[s, :] = out


def tap_gradient(x, up, dn, grad, block):
    rows, channels, width = x.shape
    out = pl.pallas_call(
        tap_grad_kernel,
        grid=(channels // block,),
        in_specs=[
            pl.BlockSpec((rows, block, width), lambda g: (0, g, 0)),
            pl.BlockSpec((REACH, block, width), lambda g: (0, g, 0)),
            pl.BlockSpec((REACH, block, width), lambda g: (0, g, 0)),
            pl.BlockSpec((rows, block, width), lambda g: (0, g, 0)),
        ],
        out_specs=pl.BlockSpec((block, 128), lambda g: (g, 0)),
        out_shape=jax.ShapeDtypeStruct((channels, 128), F32),
        scratch_shapes=[pltpu.VMEM((rows + 2 * REACH, block, width), BF16)],
        compiler_params=params(24),
        cost_estimate=cost(18e9, 8e6),
        name="tap_gradient",
    )(x, up, dn, grad)
    return out.reshape(channels, 8, GRP)[:, :KS, :KS].reshape(channels, TAPS)


def mask_grad_kernel(og_ref, m_ref, by_chan_ref, by_pixel_ref, sum_ref, cols_ref):
    row = pl.program_id(0)
    channels = og_ref.shape[1]
    v = og_ref[0].astype(F32) * m_ref[0, 0:1]
    by_chan_ref[...] = v.astype(BF16)
    by_pixel_ref[...] = v.T.astype(BF16)
    part = v[:, 0:128]
    for k in range(128, v.shape[1], 128):
        part = part + v[:, k : k + 128]

    @pl.when(row == 0)
    def _():
        cols_ref[...] = jnp.zeros(cols_ref.shape, F32)

    cols_ref[0:channels, :] += part

    @pl.when(row == pl.num_programs(0) - 1)
    def _():
        cols_ref[...] = jnp.broadcast_to(
            jnp.sum(cols_ref[...], axis=1, keepdims=True), cols_ref.shape
        )
        rows_of(cols_ref, sum_ref)


def mask_gradient(og, m16, padded):
    rows, channels, width = og.shape
    pixels = rows * width
    return pl.pallas_call(
        mask_grad_kernel,
        grid=(rows,),
        in_specs=[
            pl.BlockSpec((1, channels, width), lambda r: (r, 0, 0)),
            pl.BlockSpec((1, GRP, width), lambda r: (r, 0, 0)),
        ],
        out_specs=[
            pl.BlockSpec((channels, width), lambda r: (0, r)),
            pl.BlockSpec((width, channels), lambda r: (r, 0)),
            pl.BlockSpec((8, padded), lambda r: (0, 0)),
        ],
        out_shape=[
            jax.ShapeDtypeStruct((channels, pixels), BF16),
            jax.ShapeDtypeStruct((pixels, channels), BF16),
            jax.ShapeDtypeStruct((8, padded), F32),
        ],
        scratch_shapes=[pltpu.VMEM((padded, 128), F32)],
        compiler_params=params(24),
        cost_estimate=cost(1e9, 8e6),
        name="mask_gradient",
    )(og, m16)


def activate_kernel(conv_ref, par_ref, by_chan_ref, by_pixel_ref, cols_ref):
    channels = conv_ref.shape[1]

    @pl.when(pl.program_id(0) == 0)
    def _():
        cols_ref[...] = columns_of(par_ref)

    c = cols_ref[0:channels, :]
    v = (conv_ref[0] - c[:, 0:1]) * c[:, 1:2] + c[:, 2:3]
    by_chan_ref[...] = v.astype(BF16)
    by_pixel_ref[...] = v.T.astype(BF16)


def activate(conv, par):
    rows, channels, width = conv.shape
    pixels = rows * width
    padded = par.shape[1]
    return pl.pallas_call(
        activate_kernel,
        grid=(rows,),
        in_specs=[pl.BlockSpec((1, channels, width), lambda r: (r, 0, 0)), whole((8, padded))],
        out_specs=[
            pl.BlockSpec((channels, width), lambda r: (0, r)),
            pl.BlockSpec((width, channels), lambda r: (r, 0)),
        ],
        out_shape=[
            jax.ShapeDtypeStruct((channels, pixels), BF16),
            jax.ShapeDtypeStruct((pixels, channels), BF16),
        ],
        scratch_shapes=[pltpu.VMEM((padded, 128), F32)],
        compiler_params=params(24),
        cost_estimate=cost(1e9, 10e6),
        name="activate",
    )(conv, par)


def gelu_parts(v):
    v2 = v * v
    t = jnp.tanh(v * (GELU_A + (GELU_A * GELU_B) * v2))
    s = 0.5 * t + 0.5
    h = v * s
    return h, s + h * (1.0 - s) * (2 * GELU_A + (6 * GELU_A * GELU_B) * v2)


def hidden_kernel(
    act_p, act_c, bg_p, bg_c, we_ref, wp_ref, eb_ref, h_ref, g_ref, dwp_ref, dwe_ref, ebg_ref, *, step
):
    we, wp, bias = we_ref[...], wp_ref[...], eb_ref[...]
    total = None
    for p in range(0, act_p.shape[0], step):
        pre = jnp.dot(act_p[p : p + step, :], we, preferred_element_type=F32) + bias
        pull = jnp.dot(bg_p[p : p + step, :], wp, preferred_element_type=F32)
        h, slope = gelu_parts(pre)
        grad = (pull * slope).astype(BF16)
        h_ref[p : p + step, :] = h.astype(BF16)
        g_ref[p : p + step, :] = grad
        part = jnp.sum(grad.astype(F32), axis=0, keepdims=True)
        total = part if total is None else total + part
    ebg_ref[...] = total
    dwp_ref[...] = jnp.dot(bg_c[...], h_ref[...], preferred_element_type=F32).astype(dwp_ref.dtype)
    dwe_ref[...] = jnp.dot(act_c[...], g_ref[...], preferred_element_type=F32).astype(dwe_ref.dtype)


def hidden_layer(act_p, act_c, bg_p, bg_c, we, wp, eb, first, units, dtype):
    pixels, channels = act_p.shape
    steps = pl.cdiv(units, TILE)
    off = first // TILE
    weight = pl.BlockSpec((channels, TILE), lambda g: (0, g + off))
    return pl.pallas_call(
        functools.partial(hidden_kernel, step=pixels // 3),
        grid=(steps,),
        in_specs=[
            whole((pixels, channels)),
            whole((channels, pixels)),
            whole((pixels, channels)),
            whole((channels, pixels)),
            weight,
            weight,
            pl.BlockSpec((1, TILE), lambda g: (0, g + off)),
        ],
        out_specs=[
            pl.BlockSpec((pixels, TILE), lambda g: (0, g)),
            pl.BlockSpec((pixels, TILE), lambda g: (0, g)),
            pl.BlockSpec((channels, TILE), lambda g: (0, g)),
            pl.BlockSpec((channels, TILE), lambda g: (0, g)),
            pl.BlockSpec((1, TILE), lambda g: (0, g)),
        ],
        out_shape=[
            jax.ShapeDtypeStruct((pixels, units), BF16),
            jax.ShapeDtypeStruct((pixels, units), BF16),
            jax.ShapeDtypeStruct((channels, units), dtype),
            jax.ShapeDtypeStruct((channels, units), dtype),
            jax.ShapeDtypeStruct((1, units), F32),
        ],
        compiler_params=params(40),
        cost_estimate=cost(8 * pixels * channels * units, 20e6, pixels * units),
        name="hidden_layer",
    )(act_p, act_c, bg_p, bg_c, we, wp, eb)


def contract(weights, hiddens):
    total = None
    for (w_ref, first, units), h_ref in zip(weights, hiddens, strict=True):
        part = lax.dot_general(
            w_ref[:, first : first + units], h_ref[...], NT, preferred_element_type=F32
        )
        total = part if total is None else total + part
    return total


def act_grad_kernel(*refs, cuts):
    n = len(cuts)
    w_refs, h_refs = refs[0:2], refs[2 : 2 + n]
    conv_ref, par_ref, out_ref, sum_ref, cols_ref, acc_ref = refs[2 + n :]
    channels = conv_ref.shape[1]
    row = pl.program_id(0)

    @pl.when(row == 0)
    def _():
        cols_ref[...] = columns_of(par_ref)
        acc_ref[...] = jnp.zeros(acc_ref.shape, F32)

    grad = contract([(w_refs[w], first, units) for w, first, units in cuts], h_refs)
    out_ref[0] = grad
    c = cols_ref[0:channels, :]
    scaled = grad * ((conv_ref[0] - c[:, 0:1]) * c[:, 3:4])
    plain, weighted = grad[:, 0:128], scaled[:, 0:128]
    for k in range(128, grad.shape[1], 128):
        plain = plain + grad[:, k : k + 128]
        weighted = weighted + scaled[:, k : k + 128]
    acc_ref[0, 0:channels, :] += plain
    acc_ref[1, 0:channels, :] += weighted

    @pl.when(row == pl.num_programs(0) - 1)
    def _():
        lane = lax.broadcasted_iota(jnp.int32, cols_ref.shape, 1)
        plain = jnp.sum(acc_ref[0], axis=1, keepdims=True)
        weighted = jnp.sum(acc_ref[1], axis=1, keepdims=True)
        cols_ref[...] = jnp.where(lane == 0, plain, weighted)
        rows_of(cols_ref, sum_ref)


def activation_gradient(weights, hiddens, cuts, conv, par):
    rows, channels, width = conv.shape
    padded = par.shape[1]
    return pl.pallas_call(
        functools.partial(act_grad_kernel, cuts=cuts),
        grid=(rows,),
        in_specs=[whole(w.shape) for w in weights]
        + [pl.BlockSpec((width, h.shape[1]), lambda r: (r, 0)) for h in hiddens]
        + [pl.BlockSpec((1, channels, width), lambda r: (r, 0, 0)), whole((8, padded))],
        out_specs=[
            pl.BlockSpec((1, channels, width), lambda r: (r, 0, 0)),
            pl.BlockSpec((8, padded), lambda r: (0, 0)),
        ],
        out_shape=[
            jax.ShapeDtypeStruct((rows, channels, width), F32),
            jax.ShapeDtypeStruct((8, padded), F32),
        ],
        scratch_shapes=[pltpu.VMEM((padded, 128), F32), pltpu.VMEM((2, padded, 128), F32)],
        compiler_params=params(40),
        cost_estimate=cost(8e9, 25e6),
        name="activation_gradient",
    )(*weights, *hiddens, conv, par)


def block_out_kernel(*refs, cuts):
    n = len(cuts)
    w_refs, h_refs = refs[0:2], refs[2 : 2 + n]
    x_ref, m_ref, par_ref, out_ref, cols_ref = refs[2 + n :]
    channels = x_ref.shape[1]

    @pl.when(pl.program_id(0) == 0)
    def _():
        cols_ref[...] = columns_of(par_ref)

    branch = contract([(w_refs[w], first, units) for w, first, units in cuts], h_refs)
    branch = branch + cols_ref[0:channels, 4:5]
    out_ref[0] = ((x_ref[0].astype(F32) + branch) * m_ref[0, 0:1]).astype(BF16)


def block_output(weights, hiddens, cuts, x, m16, par):
    rows, channels, width = x.shape
    padded = par.shape[1]
    return pl.pallas_call(
        functools.partial(block_out_kernel, cuts=cuts),
        grid=(rows,),
        in_specs=[whole(w.shape) for w in weights]
        + [pl.BlockSpec((width, h.shape[1]), lambda r: (r, 0)) for h in hiddens]
        + [
            pl.BlockSpec((1, channels, width), lambda r: (r, 0, 0)),
            pl.BlockSpec((1, GRP, width), lambda r: (r, 0, 0)),
            whole((8, padded)),
        ],
        out_specs=pl.BlockSpec((1, channels, width), lambda r: (r, 0, 0)),
        out_shape=jax.ShapeDtypeStruct((rows, channels, width), BF16),
        scratch_shapes=[pltpu.VMEM((padded, 128), F32)],
        compiler_params=params(40),
        cost_estimate=cost(8e9, 22e6),
        name="block_output",
    )(*weights, *hiddens, x, m16, par)


def conv_grad_kernel(da_ref, conv_ref, m_ref, par_ref, out_ref, cols_ref):
    channels = conv_ref.shape[1]

    @pl.when(pl.program_id(0) == 0)
    def _():
        cols_ref[...] = columns_of(par_ref)

    c = cols_ref[0:channels, :]
    normalized = (conv_ref[0] - c[:, 0:1]) * c[:, 1:2]
    correction = m_ref[0, 0:1] * (c[:, 3:4] + normalized * c[:, 4:5])
    out_ref[0] = (c[:, 2:3] * (da_ref[0] - correction)).astype(BF16)


def conv_gradient(da, conv, m16, par):
    rows, channels, width = conv.shape
    padded = par.shape[1]
    return pl.pallas_call(
        conv_grad_kernel,
        grid=(rows,),
        in_specs=[
            pl.BlockSpec((1, channels, width), lambda r: (r, 0, 0)),
            pl.BlockSpec((1, channels, width), lambda r: (r, 0, 0)),
            pl.BlockSpec((1, GRP, width), lambda r: (r, 0, 0)),
            whole((8, padded)),
        ],
        out_specs=pl.BlockSpec((1, channels, width), lambda r: (r, 0, 0)),
        out_shape=jax.ShapeDtypeStruct((rows, channels, width), BF16),
        scratch_shapes=[pltpu.VMEM((padded, 128), F32)],
        compiler_params=params(24),
        cost_estimate=cost(1e9, 12e6),
        name="conv_gradient",
    )(da, conv, m16, par)


def halo(field):
    size = lax.axis_size("dp")
    up = [(i, i + 1) for i in range(size - 1)]
    down = [(j, i) for i, j in up]
    return (
        lax.ppermute(field[-REACH:], "dp", up),
        lax.ppermute(field[:REACH], "dp", down),
    )


def from_all(values, axes):
    size = 1
    for axis in axes:
        size *= lax.axis_size(axis)
    copies = jnp.broadcast_to(values[None], (size,) + values.shape)
    return lax.all_to_all(copies, axes, 0, 0)


def flip_bit(values, axis, bit):
    size = lax.axis_size(axis)
    return lax.ppermute(values, axis, [(i, i ^ (1 << bit)) for i in range(size)])


def bit_of(axis, bit):
    return (lax.axis_index(axis) >> bit) & 1


def gather_rows(shard, order):
    bits = lax.axis_size("fsdp").bit_length() - 1
    rows, cols = shard.shape
    have = shard.reshape((1,) * bits + (rows, cols))
    for bit in order:
        other = flip_bit(have, "fsdp", bit)
        mine = bit_of("fsdp", bit) == 0
        dim = bits - 1 - bit
        first, second = jnp.where(mine, have, other), jnp.where(mine, other, have)
        have = jnp.concatenate([first, second], axis=dim)
    return have.reshape(-1, cols)


def scatter_rows(full, order):
    bits = lax.axis_size("fsdp").bit_length() - 1
    cols = full.shape[1]
    have = full.reshape((2,) * bits + (-1, cols))
    for bit in order:
        dim = bits - 1 - bit
        mine = bit_of("fsdp", bit)
        send = lax.dynamic_slice_in_dim(have, 1 - mine, 1, axis=dim).astype(BF16)
        keep = lax.dynamic_slice_in_dim(have, mine, 1, axis=dim)
        have = keep + flip_bit(send, "fsdp", bit).astype(F32)
    return have.reshape(-1, cols)


def per_device(
    inputs,
    out_grad,
    ocean_mask,
    rollout_lengths,
    conv_weight,
    norm_gain,
    norm_bias,
    expand_weight,
    expand_bias,
    project_weight,
    project_bias,
):
    channels, rows, width = inputs.shape[1:]
    n_fs, n_dp = lax.axis_size("fsdp"), lax.axis_size("dp")
    share = conv_weight.shape[0]
    units = expand_weight.shape[1]
    half = pl.cdiv(units // 128, 2) * 128
    padded = pl.cdiv(channels, 128) * 128
    bits = list(range(n_fs.bit_length() - 1))
    core = bit_of("dp", 0)
    x = inputs[0].transpose(1, 0, 2)
    og = out_grad[0].transpose(1, 0, 2)
    block = 5 * GRP

    ratio = expand_bias.shape[0] // share
    small = jnp.concatenate(
        [
            conv_weight,
            norm_gain[:, None],
            norm_bias[:, None],
            project_bias.astype(F32)[:, None],
            expand_bias.astype(F32).reshape(share, ratio),
        ],
        axis=1,
    )
    small = from_all(small, ("fsdp",)).reshape(channels, -1)
    taps, gain, bias = small[:, :TAPS], small[:, TAPS], small[:, TAPS + 1]
    p_bias = small[:, TAPS + 2]
    e_bias = jnp.pad(small[:, TAPS + 3 :].reshape(1, units), ((0, 0), (0, 2 * half - units)))
    spread = spread_taps(taps)
    x_up, x_dn = halo(x)

    def columns(weight):
        wide = jnp.pad(weight, ((0, 0), (0, 2 * half - units)))
        return lax.dynamic_slice_in_dim(wide, core * half, half, axis=1)

    we_own = gather_rows(columns(expand_weight), bits)
    wp_own = gather_rows(columns(project_weight), bits[::-1])
    we_peer = flip_bit(we_own, "dp", 0)
    wp_peer = flip_bit(wp_own, "dp", 0)
    eb_own = lax.dynamic_slice_in_dim(e_bias, core * half, half, axis=1)
    eb_peer = lax.dynamic_slice_in_dim(e_bias, (1 - core) * half, half, axis=1)

    sample = lax.axis_index("fsdp")
    length = lax.dynamic_index_in_dim(rollout_lengths, sample, keepdims=False)
    live = jnp.where(sample % ROLLOUT < length, 1.0, 0.0).astype(F32)
    weight = live * ocean_mask.astype(F32)
    m16 = jnp.broadcast_to(weight[:, None, :], (rows, GRP, width))
    count_here = jnp.sum(weight)
    counts = jnp.stack([count_here, 1.0 / jnp.maximum(count_here, 1.0)])

    bg_c, bg_p, bg_sum = mask_gradient(og, m16, padded)

    conv, stats = conv_forward(x, x_up, x_dn, spread, m16, counts, padded, block)
    stats = from_all(stats[:2], ("dp", "fsdp"))
    counts_all = stats[:, 0, padded - 1]
    count = jnp.sum(counts_all)
    mean = jnp.sum(counts_all[:, None] * stats[:, 0], axis=0) / count
    apart = stats[:, 0] - mean[None]
    squares = jnp.sum(stats[:, 1] + counts_all[:, None] * apart * apart, axis=0)
    variance = squares / count
    inv_std = lax.rsqrt(variance + EPS)
    pad_c = lambda v: jnp.pad(v, (0, padded - channels))
    gain_p = pad_c(gain)
    nothing = jnp.zeros_like(mean)
    par = jnp.stack(
        [mean, inv_std * gain_p, pad_c(bias), inv_std, pad_c(p_bias), nothing, nothing, nothing]
    )
    act_c, act_p = activate(conv, par)

    first = half // (2 * TILE) * TILE
    second = half - first
    common = (act_p, act_c, bg_p, bg_c)
    q1 = hidden_layer(*common, we_peer, wp_peer, eb_peer, 0, first, BF16)
    o1 = hidden_layer(*common, we_own, wp_own, eb_own, 0, first, F32)
    q2 = hidden_layer(*common, we_peer, wp_peer, eb_peer, first, second, BF16)
    o2 = hidden_layer(*common, we_own, wp_own, eb_own, first, second, F32)
    cuts = ((1, 0, first), (0, 0, first), (1, first, second), (0, first, second))
    parts = (q1, o1, q2, o2)
    da, sums = activation_gradient(
        (we_own, we_peer), [p[1] for p in parts], cuts, conv, par
    )
    sums = jnp.sum(from_all(sums[:2], ("dp", "fsdp")), axis=0)
    block_out = block_output(
        (wp_own, wp_peer), [p[0] for p in parts], cuts, x, m16, par
    )
    bias_total, gain_total = sums[0], sums[1]
    par_b = jnp.stack(
        [mean, inv_std, gain_p * inv_std, bias_total / count, gain_total / count]
        + [nothing] * 3
    )
    conv_grad = conv_gradient(da, conv, m16, par_b)
    g_up, g_dn = halo(conv_grad)
    tap_local = tap_gradient(x, x_up, x_dn, conv_grad, block)
    input_grad = input_gradient(conv_grad, g_up, g_dn, spread, og, m16, block)

    groups = [[i for i in range(n_dp) if i % 2 == c] for c in range(2)]

    def reduced(peer, own, order):
        total = own + flip_bit(peer, "dp", 0).astype(F32)
        mine = scatter_rows(total, order).astype(BF16)
        return lax.psum(mine, "dp", axis_index_groups=groups)

    def joined(which, order):
        mine = jnp.concatenate(
            [reduced(q1[which], o1[which], order), reduced(q2[which], o2[which], order)], axis=1
        )
        other = flip_bit(mine, "dp", 0)
        low, high = jnp.where(core == 0, mine, other), jnp.where(core == 0, other, mine)
        return jnp.concatenate([low, high], axis=1)[:, :units].astype(F32)

    project_grad = joined(2, bits[::-1])
    expand_grad = joined(3, bits)

    eb_o = jnp.concatenate([o1[4], o2[4]], axis=1)
    eb_q = jnp.concatenate([q1[4], q2[4]], axis=1)
    eb_all = jnp.concatenate(
        [jnp.where(core == 0, eb_o, eb_q), jnp.where(core == 0, eb_q, eb_o)], axis=1
    )[0, :units]
    local = jnp.concatenate(
        [
            tap_local.reshape(n_fs, share * TAPS),
            eb_all.reshape(n_fs, share * ratio),
            bg_sum[0, :channels].reshape(n_fs, share),
        ],
        axis=1,
    )
    local = jnp.sum(lax.all_to_all(local, "fsdp", 0, 0), axis=0)
    local = lax.psum(local, "dp")
    tap_grad = local[: share * TAPS].reshape(share, TAPS)
    eb_grad = local[share * TAPS : share * (TAPS + ratio)]
    pb_grad = local[share * (TAPS + ratio) :]

    start = lax.axis_index("fsdp") * share
    gain_grad = lax.dynamic_slice_in_dim(gain_total, start, share)
    bias_grad = lax.dynamic_slice_in_dim(bias_total, start, share)
    return (
        block_out.transpose(1, 0, 2)[None],
        input_grad.transpose(1, 0, 2)[None],
        tap_grad,
        gain_grad,
        bias_grad,
        expand_grad,
        eb_grad,
        project_grad,
        pb_grad,
        mean[:channels],
        jnp.sqrt(variance + EPS)[:channels],
    )


def solution(mesh):
    rows = P("fsdp", None, "dp", None)
    return jax.shard_map(
        per_device,
        mesh=mesh,
        in_specs=(
            rows,
            rows,
            P("dp", None),
            P(),
            P("fsdp", None),
            P("fsdp"),
            P("fsdp"),
            P("fsdp", None),
            P("fsdp"),
            P("fsdp", None),
            P("fsdp"),
        ),
        out_specs=(
            rows,
            rows,
            P("fsdp", None),
            P("fsdp"),
            P("fsdp"),
            P("fsdp", None),
            P("fsdp"),
            P("fsdp", None),
            P("fsdp"),
            P(),
            P(),
        ),
        check_vma=False,
    )
```

```python
import functools

import jax
import jax.numpy as jnp
from jax import lax
from jax.experimental import pallas as pl
from jax.experimental.pallas import tpu as pltpu
from jax.sharding import PartitionSpec as P

KS = 7
REACH = KS // 2
TAPS = KS * KS
ROLLOUT = 8
EPS = 1e-05
F32, BF16 = jnp.float32, jnp.bfloat16
GRP = 16
TILE = 256
MIB = 2**20
GELU_A = 0.7978845608028654
GELU_B = 0.044715
NT = (((1,), (1,)), ((), ()))


def params(limit=60):
    return pltpu.CompilerParams(vmem_limit_bytes=limit * MIB)


def cost(flops, nbytes, trans=0):
    return pl.CostEstimate(flops=int(flops), bytes_accessed=int(nbytes), transcendentals=int(trans))


def whole(shape):
    zeros = (0,) * len(shape)
    return pl.BlockSpec(shape, lambda *g: zeros, pipeline_mode=pl.Buffered(1))


def roll_lanes(v, shift):
    shift %= v.shape[-1]
    return v if shift == 0 else pltpu.roll(v, shift, v.ndim - 1)


def columns_of(*rows):
    pieces = []
    for k in range(rows[0].shape[0]):
        used = [v[k : k + 1, :] for v in rows]
        block = jnp.concatenate(used + [jnp.zeros((128 - len(rows), 128), F32)], axis=0)
        pieces.append(block.T)
    return jnp.concatenate(pieces, axis=0)


def copies_of(cols, out_ref):
    copies = out_ref.shape[0]
    for k in range(cols.shape[0] // 128):
        block = cols[k * 128 : (k + 1) * 128, :].T
        for q in range(2):
            row = jnp.broadcast_to(block[q : q + 1, :][None], (copies, 1, 128))
            out_ref[:, 8 * q + k : 8 * q + k + 1, :] = row


def spread_taps(cols, pick_ref, e_ref):
    count = cols.shape[0]
    lane = lax.broadcasted_iota(jnp.int32, (count, 128), 1)
    own = lax.broadcasted_iota(jnp.int32, (count, 128), 0) % GRP == lane % GRP
    high = cols.astype(BF16)
    low = (cols - high.astype(F32)).astype(BF16)
    for h, part in enumerate((high, low)):
        for j in range(KS):
            picked = jnp.dot(part, pick_ref[j], preferred_element_type=F32)
            e_ref[h, j] = jnp.where(own, picked, 0.0).astype(BF16)


def tap_picker():
    col, tap, lane = (lax.broadcasted_iota(jnp.int32, (KS, 128, 128), d) for d in range(3))
    return jnp.where((tap == KS * (lane // GRP) + col) & (lane < KS * GRP), 1.0, 0.0).astype(BF16)


def conv_rows(field_ref, taps_ref, s, rows, flip):
    x = field_ref[:, s, :].reshape((rows + 2 * REACH) * GRP, field_ref.shape[-1])
    parts = [taps_ref[h, :, s, :].reshape(KS * GRP, 128)[:, : KS * GRP] for h in range(2)]
    taps = jnp.concatenate(parts, axis=1)
    out = []
    for r in range(rows):
        src = rows - 1 - r if flip else r
        window = x[src * GRP : (src + KS) * GRP]
        sums = jnp.dot(taps, jnp.concatenate([window, window], axis=0), preferred_element_type=F32)
        acc = None
        for j in range(KS):
            moved = roll_lanes(sums[j * GRP : (j + 1) * GRP], j - REACH if flip else REACH - j)
            acc = moved if acc is None else acc + moved
        out.append(acc)
    return out


def conv_kernel(
    n_ref, x_ref, up_ref, dn_ref, small_ref, pick_ref, m_ref, out_ref, st_ref, par_ref,
    field_ref, cols_ref, e_ref, *, share
):
    rows, block = x_ref.shape[0], x_ref.shape[1]
    step = pl.program_id(0)
    count = n_ref[0]
    inv_n = n_ref[1]

    @pl.when(step == 0)
    def _():
        cols_ref[...] = jnp.full(cols_ref.shape, count, F32)
        given, wide = small_ref.shape[1], pl.cdiv(share, 128) * 128
        for f in range(small_ref.shape[0]):
            v = small_ref[f]
            v = jnp.concatenate([v, jnp.zeros((given, wide - share), F32)], axis=1)
            v = jnp.concatenate([v, jnp.zeros((128 - given, wide), F32)], axis=0)
            par_ref[f * share : (f + 1) * share, :] = v.T[:share]

    field_ref[0:REACH] = up_ref[...]
    field_ref[REACH : REACH + rows] = x_ref[...]
    field_ref[REACH + rows :] = dn_ref[...]
    here = pl.multiple_of(step * block, GRP)
    spread_taps(par_ref[pl.ds(here, block), :], pick_ref, e_ref)
    lane = lax.broadcasted_iota(jnp.int32, (GRP, 128), 1)
    for g in range(block // GRP):
        s = pl.ds(g * GRP, GRP)
        acc = conv_rows(field_ref, e_ref, s, rows, False)
        total = None
        for r in range(rows):
            out_ref[r, s, :] = acc[r]
            v = acc[r] * m_ref[r]
            total = v if total is None else total + v
        mean = jnp.sum(total, axis=-1, keepdims=True) * inv_n
        total = None
        for r in range(rows):
            d = acc[r] - mean
            v = d * d * m_ref[r]
            total = v if total is None else total + v
        dev = jnp.sum(total, axis=-1, keepdims=True)
        at = pl.multiple_of(step * block + g * GRP, GRP)
        cols_ref[pl.ds(at, GRP), :] = jnp.where(lane == 0, mean, dev)

    @pl.when(step == pl.num_programs(0) - 1)
    def _():
        st_ref[...] = jnp.full(st_ref.shape, count, F32)
        copies_of(cols_ref[...], st_ref)


def conv_forward(x, up, dn, small, pick, m16, counts, copies, block):
    rows, channels, width = x.shape
    n_fs, given, share = small.shape
    padded = pl.cdiv(channels, 128) * 128
    return pl.pallas_call(
        functools.partial(conv_kernel, share=share),
        grid=(channels // block,),
        in_specs=[
            pl.BlockSpec(memory_space=pltpu.SMEM),
            pl.BlockSpec((rows, block, width), lambda g: (0, g, 0)),
            pl.BlockSpec((REACH, block, width), lambda g: (0, g, 0)),
            pl.BlockSpec((REACH, block, width), lambda g: (0, g, 0)),
            whole((n_fs, given, share)),
            whole((KS, 128, 128)),
            whole((rows, GRP, width)),
        ],
        out_specs=[
            pl.BlockSpec((rows, block, width), lambda g: (0, g, 0)),
            pl.BlockSpec((copies, 16, 128), lambda g: (0, 0, 0)),
            pl.BlockSpec((channels, 128), lambda g: (0, 0)),
        ],
        out_shape=[
            jax.ShapeDtypeStruct((rows, channels, width), F32),
            jax.ShapeDtypeStruct((copies, 16, 128), F32),
            jax.ShapeDtypeStruct((channels, 128), F32),
        ],
        scratch_shapes=[
            pltpu.VMEM((rows + 2 * REACH, block, width), BF16),
            pltpu.VMEM((padded, 128), F32),
            pltpu.VMEM((2, KS, block, 128), BF16),
        ],
        compiler_params=params(),
        cost_estimate=cost(20e9, 12e6),
        name="conv_forward",
    )(counts, x, up, dn, small, pick, m16)


def input_grad_kernel(
    g_ref, up_ref, dn_ref, par_ref, pick_ref, og_ref, m_ref, out_ref, field_ref, e_ref
):
    rows, block = g_ref.shape[0], g_ref.shape[1]
    last = rows + 2 * REACH - 1
    for q in range(REACH):
        field_ref[last - q] = up_ref[q]
        field_ref[REACH - 1 - q] = dn_ref[q]
    for q in range(rows):
        field_ref[last - REACH - q] = g_ref[q]
    spread_taps(par_ref[...], pick_ref, e_ref)
    for g in range(block // GRP):
        s = pl.ds(g * GRP, GRP)
        acc = conv_rows(field_ref, e_ref, s, rows, True)
        for r in range(rows):
            out_ref[r, s, :] = og_ref[r, s, :].astype(F32) * m_ref[r] + acc[r]


def input_gradient(grad, up, dn, par, pick, og, m16, block):
    rows, channels, width = grad.shape
    return pl.pallas_call(
        input_grad_kernel,
        grid=(channels // block,),
        in_specs=[
            pl.BlockSpec((rows, block, width), lambda g: (0, g, 0)),
            pl.BlockSpec((REACH, block, width), lambda g: (0, g, 0)),
            pl.BlockSpec((REACH, block, width), lambda g: (0, g, 0)),
            pl.BlockSpec((block, 128), lambda g: (g, 0)),
            whole((KS, 128, 128)),
            pl.BlockSpec((rows, block, width), lambda g: (0, g, 0)),
            whole((rows, GRP, width)),
        ],
        out_specs=pl.BlockSpec((rows, block, width), lambda g: (0, g, 0)),
        out_shape=jax.ShapeDtypeStruct((rows, channels, width), F32),
        scratch_shapes=[
            pltpu.VMEM((rows + 2 * REACH, block, width), BF16),
            pltpu.VMEM((2, KS, block, 128), BF16),
        ],
        compiler_params=params(),
        cost_estimate=cost(18e9, 15e6),
        name="input_gradient",
    )(grad, up, dn, par, pick, og, m16)


def tap_grad_kernel(x_ref, up_ref, dn_ref, g_ref, out_ref, field_ref, cols_ref, *, share):
    rows, block, width = x_ref.shape
    field_ref[0:REACH] = up_ref[...]
    field_ref[REACH : REACH + rows] = x_ref[...]
    field_ref[REACH + rows :] = dn_ref[...]
    lane = lax.broadcasted_iota(jnp.int32, (GRP, 128), 1)
    own = lax.broadcasted_iota(jnp.int32, (GRP, 128), 0) == lane % GRP
    for g in range(block // GRP):
        s = pl.ds(g * GRP, GRP)
        x = field_ref[:, s, :].reshape((rows + 2 * REACH) * GRP, width)
        fields = jnp.concatenate([x[r * GRP : (r + KS) * GRP] for r in range(rows)], axis=1)
        grads = []
        for j in range(KS):
            moved = [roll_lanes(g_ref[r, s, :], j - REACH) for r in range(rows)]
            grads.append(jnp.concatenate(moved, axis=1))
        grads = jnp.concatenate(grads, axis=0)
        sums = lax.dot_general(grads, fields, NT, preferred_element_type=F32)
        sums = jnp.concatenate([sums, jnp.zeros((KS * GRP, 128 - KS * GRP), F32)], axis=1)
        out = None
        for j in range(KS):
            acc = jnp.where(own, sums[j * GRP : (j + 1) * GRP], 0.0)
            for k in (8, 4, 2, 1):
                acc = acc + pltpu.roll(acc, 128 - k, 1)
            acc = roll_lanes(acc, j)
            out = acc if out is None else jnp.where(lane % GRP == j, acc, out)
        at = pl.multiple_of(pl.program_id(0) * block + g * GRP, GRP)
        cols_ref[pl.ds(at, GRP), :] = out

    @pl.when(pl.program_id(0) == pl.num_programs(0) - 1)
    def _():
        blocks = [cols_ref[k : k + 128, :].T for k in range(0, cols_ref.shape[0], 128)]
        wide = jnp.concatenate(blocks, axis=1)
        taps = jnp.concatenate([wide[GRP * i : GRP * i + KS] for i in range(KS)], axis=0)
        for f in range(out_ref.shape[0]):
            out_ref[f] = taps[:, f * share : (f + 1) * share]


def tap_gradient(x, up, dn, grad, block, share):
    rows, channels, width = x.shape
    padded = pl.cdiv(channels, 128) * 128
    return pl.pallas_call(
        functools.partial(tap_grad_kernel, share=share),
        grid=(channels // block,),
        in_specs=[
            pl.BlockSpec((rows, block, width), lambda g: (0, g, 0)),
            pl.BlockSpec((REACH, block, width), lambda g: (0, g, 0)),
            pl.BlockSpec((REACH, block, width), lambda g: (0, g, 0)),
            pl.BlockSpec((rows, block, width), lambda g: (0, g, 0)),
        ],
        out_specs=pl.BlockSpec((channels // share, TAPS, share), lambda g: (0, 0, 0)),
        out_shape=jax.ShapeDtypeStruct((channels // share, TAPS, share), F32),
        scratch_shapes=[
            pltpu.VMEM((rows + 2 * REACH, block, width), BF16),
            pltpu.VMEM((padded, 128), F32),
        ],
        compiler_params=params(),
        cost_estimate=cost(18e9, 8e6),
        name="tap_gradient",
    )(x, up, dn, grad)


def mask_grad_kernel(og_ref, m_ref, by_chan_ref, by_pixel_ref, sum_ref, cols_ref):
    row = pl.program_id(0)
    channels = og_ref.shape[1]
    v = og_ref[0].astype(F32) * m_ref[0, 0:1]
    by_chan_ref[...] = v.astype(BF16)
    by_pixel_ref[...] = v.T.astype(BF16)
    part = v[:, 0:128]
    for k in range(128, v.shape[1], 128):
        part = part + v[:, k : k + 128]

    @pl.when(row == 0)
    def _():
        cols_ref[...] = jnp.zeros(cols_ref.shape, F32)

    cols_ref[0:channels, :] += part

    @pl.when(row == pl.num_programs(0) - 1)
    def _():
        sums = jnp.broadcast_to(jnp.sum(cols_ref[...], axis=1, keepdims=True), cols_ref.shape)
        copies_of(sums, sum_ref)


def mask_gradient(og, m16):
    rows, channels, width = og.shape
    padded = pl.cdiv(channels, 128) * 128
    pixels = rows * width
    return pl.pallas_call(
        mask_grad_kernel,
        grid=(rows,),
        in_specs=[
            pl.BlockSpec((1, channels, width), lambda r: (r, 0, 0)),
            pl.BlockSpec((1, GRP, width), lambda r: (r, 0, 0)),
        ],
        out_specs=[
            pl.BlockSpec((channels, width), lambda r: (0, r)),
            pl.BlockSpec((width, channels), lambda r: (r, 0)),
            pl.BlockSpec((1, 16, 128), lambda r: (0, 0, 0)),
        ],
        out_shape=[
            jax.ShapeDtypeStruct((channels, pixels), BF16),
            jax.ShapeDtypeStruct((pixels, channels), BF16),
            jax.ShapeDtypeStruct((1, 16, 128), F32),
        ],
        scratch_shapes=[pltpu.VMEM((padded, 128), F32)],
        compiler_params=params(),
        cost_estimate=cost(1e9, 8e6),
        name="mask_gradient",
    )(og, m16)


def activate_kernel(conv_ref, all_ref, par_ref, by_chan_ref, by_pixel_ref, stat_ref, cols_ref):
    channels = conv_ref.shape[1]

    @pl.when(pl.program_id(0) == 0)
    def _():
        means, squares = all_ref[:, 0:8, :], all_ref[:, 8:16, :]
        counts = all_ref[:, 7:8, :]
        count = jnp.sum(counts, axis=0)
        mean = jnp.sum(counts * means, axis=0) / count
        apart = means - mean[None]
        variance = jnp.sum(squares + counts * apart * apart, axis=0) / count
        inv_std = lax.rsqrt(variance + EPS)
        stat_ref[0:8] = mean
        stat_ref[8:16] = inv_std
        stat_ref[16:24] = jnp.sqrt(variance + EPS)
        stat_ref[24:32] = jnp.broadcast_to(count, (8, 128))
        cols_ref[...] = columns_of(mean[0:7], inv_std[0:7])[: cols_ref.shape[0]]

    c, p = cols_ref[0:channels, :], par_ref[...]
    v = (conv_ref[0] - c[:, 0:1]) * (c[:, 1:2] * p[:, TAPS : TAPS + 1]) + p[:, TAPS + 1 : TAPS + 2]
    by_chan_ref[...] = v.astype(BF16)
    by_pixel_ref[...] = v.T.astype(BF16)


def activate(conv, stats, par):
    rows, channels, width = conv.shape
    pixels = rows * width
    padded = pl.cdiv(channels, 128) * 128
    return pl.pallas_call(
        activate_kernel,
        grid=(rows,),
        in_specs=[
            pl.BlockSpec((1, channels, width), lambda r: (r, 0, 0)),
            whole(stats.shape),
            whole(par.shape),
        ],
        out_specs=[
            pl.BlockSpec((channels, width), lambda r: (0, r)),
            pl.BlockSpec((width, channels), lambda r: (r, 0)),
            pl.BlockSpec((32, 128), lambda r: (0, 0)),
        ],
        out_shape=[
            jax.ShapeDtypeStruct((channels, pixels), BF16),
            jax.ShapeDtypeStruct((pixels, channels), BF16),
            jax.ShapeDtypeStruct((32, 128), F32),
        ],
        scratch_shapes=[pltpu.VMEM((padded, 128), F32)],
        compiler_params=params(),
        cost_estimate=cost(1e9, 10e6),
        name="activate",
    )(conv, stats, par)


def gelu_parts(v):
    v2 = v * v
    t = jnp.tanh(v * (GELU_A + (GELU_A * GELU_B) * v2))
    s = 0.5 * t + 0.5
    h = v * s
    return h, s + h * (1.0 - s) * (2 * GELU_A + (6 * GELU_A * GELU_B) * v2)


def hidden_kernel(
    act_p, act_c, bg_p, bg_c, we_ref, wp_ref, eb_ref, h_ref, g_ref, dwp_ref, dwe_ref, ebg_ref, *, step
):
    we, wp, bias = we_ref[...], wp_ref[...], eb_ref[...]
    total = None
    for p in range(0, act_p.shape[0], step):
        pre = jnp.dot(act_p[p : p + step, :], we, preferred_element_type=F32) + bias
        pull = jnp.dot(bg_p[p : p + step, :], wp, preferred_element_type=F32)
        h, slope = gelu_parts(pre)
        grad = (pull * slope).astype(BF16)
        h_ref[p : p + step, :] = h.astype(BF16)
        g_ref[p : p + step, :] = grad
        part = jnp.sum(grad.astype(F32), axis=0, keepdims=True)
        total = part if total is None else total + part
    ebg_ref[...] = total
    dwp_ref[...] = jnp.dot(bg_c[...], h_ref[...], preferred_element_type=F32).astype(dwp_ref.dtype)
    dwe_ref[...] = jnp.dot(act_c[...], g_ref[...], preferred_element_type=F32).astype(dwe_ref.dtype)


def hidden_layer(act_p, act_c, bg_p, bg_c, we, wp, eb, first, units, dtype):
    pixels, channels = act_p.shape
    steps = pl.cdiv(units, TILE)
    off = first // TILE
    weight = pl.BlockSpec((channels, TILE), lambda g: (0, g + off))
    return pl.pallas_call(
        functools.partial(hidden_kernel, step=pixels // 3),
        grid=(steps,),
        in_specs=[
            whole((pixels, channels)),
            whole((channels, pixels)),
            whole((pixels, channels)),
            whole((channels, pixels)),
            weight,
            weight,
            pl.BlockSpec((1, TILE), lambda g: (0, g + off)),
        ],
        out_specs=[
            pl.BlockSpec((pixels, TILE), lambda g: (0, g)),
            pl.BlockSpec((pixels, TILE), lambda g: (0, g)),
            pl.BlockSpec((channels, TILE), lambda g: (0, g)),
            pl.BlockSpec((channels, TILE), lambda g: (0, g)),
            pl.BlockSpec((1, TILE), lambda g: (0, g)),
        ],
        out_shape=[
            jax.ShapeDtypeStruct((pixels, units), BF16),
            jax.ShapeDtypeStruct((pixels, units), BF16),
            jax.ShapeDtypeStruct((channels, units), dtype),
            jax.ShapeDtypeStruct((channels, units), dtype),
            jax.ShapeDtypeStruct((1, units), F32),
        ],
        compiler_params=params(),
        cost_estimate=cost(8 * pixels * channels * units, 20e6, pixels * units),
        name="hidden_layer",
    )(act_p, act_c, bg_p, bg_c, we, wp, eb)


def contract(weights, hiddens):
    total = None
    for (w_ref, first, units), h_ref in zip(weights, hiddens, strict=True):
        part = lax.dot_general(
            w_ref[:, first : first + units], h_ref[...], NT, preferred_element_type=F32
        )
        total = part if total is None else total + part
    return total


def act_grad_kernel(*refs, cuts):
    n = len(cuts)
    w_refs, h_refs = refs[0:2], refs[2 : 2 + n]
    conv_ref, stat_ref, out_ref, sum_ref, cols_ref, acc_ref = refs[2 + n :]
    channels = conv_ref.shape[1]
    row = pl.program_id(0)

    @pl.when(row == 0)
    def _():
        cols_ref[...] = columns_of(stat_ref[0:7], stat_ref[8:15])[: cols_ref.shape[0]]
        acc_ref[...] = jnp.zeros(acc_ref.shape, F32)

    grad = contract([(w_refs[w], first, units) for w, first, units in cuts], h_refs)
    out_ref[0] = grad
    c = cols_ref[0:channels, :]
    scaled = grad * ((conv_ref[0] - c[:, 0:1]) * c[:, 1:2])
    plain, weighted = grad[:, 0:128], scaled[:, 0:128]
    for k in range(128, grad.shape[1], 128):
        plain = plain + grad[:, k : k + 128]
        weighted = weighted + scaled[:, k : k + 128]
    acc_ref[0, 0:channels, :] += plain
    acc_ref[1, 0:channels, :] += weighted

    @pl.when(row == pl.num_programs(0) - 1)
    def _():
        lane = lax.broadcasted_iota(jnp.int32, cols_ref.shape, 1)
        plain = jnp.sum(acc_ref[0], axis=1, keepdims=True)
        weighted = jnp.sum(acc_ref[1], axis=1, keepdims=True)
        sum_ref[...] = jnp.zeros(sum_ref.shape, F32)
        copies_of(jnp.where(lane == 0, plain, weighted), sum_ref)


def activation_gradient(weights, hiddens, cuts, conv, stat, copies):
    rows, channels, width = conv.shape
    padded = pl.cdiv(channels, 128) * 128
    return pl.pallas_call(
        functools.partial(act_grad_kernel, cuts=cuts),
        grid=(rows,),
        in_specs=[whole(w.shape) for w in weights]
        + [pl.BlockSpec((width, h.shape[1]), lambda r: (r, 0)) for h in hiddens]
        + [pl.BlockSpec((1, channels, width), lambda r: (r, 0, 0)), whole(stat.shape)],
        out_specs=[
            pl.BlockSpec((1, channels, width), lambda r: (r, 0, 0)),
            pl.BlockSpec((copies, 16, 128), lambda r: (0, 0, 0)),
        ],
        out_shape=[
            jax.ShapeDtypeStruct((rows, channels, width), F32),
            jax.ShapeDtypeStruct((copies, 16, 128), F32),
        ],
        scratch_shapes=[pltpu.VMEM((padded, 128), F32), pltpu.VMEM((2, padded, 128), F32)],
        compiler_params=params(),
        cost_estimate=cost(8e9, 25e6),
        name="activation_gradient",
    )(*weights, *hiddens, conv, stat)


def block_out_kernel(*refs, cuts):
    n = len(cuts)
    w_refs, h_refs = refs[0:2], refs[2 : 2 + n]
    x_ref, m_ref, par_ref, out_ref = refs[2 + n :]
    branch = contract([(w_refs[w], first, units) for w, first, units in cuts], h_refs)
    branch = branch + par_ref[:, TAPS + 2 : TAPS + 3]
    out_ref[0] = ((x_ref[0].astype(F32) + branch) * m_ref[0, 0:1]).astype(BF16)


def block_output(weights, hiddens, cuts, x, m16, par):
    rows, channels, width = x.shape
    return pl.pallas_call(
        functools.partial(block_out_kernel, cuts=cuts),
        grid=(rows,),
        in_specs=[whole(w.shape) for w in weights]
        + [pl.BlockSpec((width, h.shape[1]), lambda r: (r, 0)) for h in hiddens]
        + [
            pl.BlockSpec((1, channels, width), lambda r: (r, 0, 0)),
            pl.BlockSpec((1, GRP, width), lambda r: (r, 0, 0)),
            whole(par.shape),
        ],
        out_specs=pl.BlockSpec((1, channels, width), lambda r: (r, 0, 0)),
        out_shape=jax.ShapeDtypeStruct((rows, channels, width), BF16),
        compiler_params=params(),
        cost_estimate=cost(8e9, 22e6),
        name="block_output",
    )(*weights, *hiddens, x, m16, par)


def conv_grad_kernel(da_ref, conv_ref, m_ref, all_ref, stat_ref, par_ref, out_ref, sum_ref, cols_ref):
    channels = conv_ref.shape[1]

    @pl.when(pl.program_id(0) == 0)
    def _():
        sums = jnp.sum(all_ref[...], axis=0)
        sum_ref[...] = sums
        count = stat_ref[24:32]
        cols_ref[...] = columns_of(
            stat_ref[0:7], stat_ref[8:15], (sums[0:8] / count)[0:7], (sums[8:16] / count)[0:7]
        )[: cols_ref.shape[0]]

    c = cols_ref[0:channels, :]
    normalized = (conv_ref[0] - c[:, 0:1]) * c[:, 1:2]
    correction = m_ref[0, 0:1] * (c[:, 2:3] + normalized * c[:, 3:4])
    factor = c[:, 1:2] * par_ref[:, TAPS : TAPS + 1]
    out_ref[0] = (factor * (da_ref[0] - correction)).astype(BF16)


def conv_gradient(da, conv, m16, sums, stat, par):
    rows, channels, width = conv.shape
    padded = pl.cdiv(channels, 128) * 128
    return pl.pallas_call(
        conv_grad_kernel,
        grid=(rows,),
        in_specs=[
            pl.BlockSpec((1, channels, width), lambda r: (r, 0, 0)),
            pl.BlockSpec((1, channels, width), lambda r: (r, 0, 0)),
            pl.BlockSpec((1, GRP, width), lambda r: (r, 0, 0)),
            whole(sums.shape),
            whole(stat.shape),
            whole(par.shape),
        ],
        out_specs=[
            pl.BlockSpec((1, channels, width), lambda r: (r, 0, 0)),
            pl.BlockSpec((16, 128), lambda r: (0, 0)),
        ],
        out_shape=[
            jax.ShapeDtypeStruct((rows, channels, width), BF16),
            jax.ShapeDtypeStruct((16, 128), F32),
        ],
        scratch_shapes=[pltpu.VMEM((padded, 128), F32)],
        compiler_params=params(),
        cost_estimate=cost(1e9, 12e6),
        name="conv_gradient",
    )(da, conv, m16, sums, stat, par)


def halo(field):
    size = lax.axis_size("dp")
    up = [(i, i + 1) for i in range(size - 1)]
    down = [(j, i) for i, j in up]
    return (
        lax.ppermute(field[-REACH:], "dp", up),
        lax.ppermute(field[:REACH], "dp", down),
    )


def after(value, *others):
    return lax.optimization_barrier((value,) + others)[0]


def from_all(values, axis):
    copies = jnp.broadcast_to(values[None], (lax.axis_size(axis),) + values.shape)
    return lax.all_to_all(copies, axis, 0, 0)


def flip_bit(values, axis, bit):
    size = lax.axis_size(axis)
    return lax.ppermute(values, axis, [(i, i ^ (1 << bit)) for i in range(size)])


def bit_of(axis, bit):
    return (lax.axis_index(axis) >> bit) & 1


def gather_step(have, bit, mine):
    other = flip_bit(have, "fsdp", bit)
    dim = lax.axis_size("fsdp").bit_length() - 2 - bit
    first, second = jnp.where(mine, have, other), jnp.where(mine, other, have)
    return jnp.concatenate([first, second], axis=dim)


def scatter_step(have, bit, done):
    bits = lax.axis_size("fsdp").bit_length() - 1
    cols = have.shape[-1]
    if done == 0:
        have = have.reshape((2,) * bits + (-1, cols))
    dim = bits - 1 - bit
    mine = bit_of("fsdp", bit)
    send = lax.dynamic_slice_in_dim(have, 1 - mine, 1, axis=dim).astype(BF16)
    keep = lax.dynamic_slice_in_dim(have, mine, 1, axis=dim)
    have = keep + flip_bit(send, "fsdp", bit).astype(F32)
    return have.reshape(-1, cols) if done == bits - 1 else have


def per_device(
    inputs,
    out_grad,
    ocean_mask,
    rollout_lengths,
    conv_weight,
    norm_gain,
    norm_bias,
    expand_weight,
    expand_bias,
    project_weight,
    project_bias,
):
    channels, rows, width = inputs.shape[1:]
    n_fs, n_dp = lax.axis_size("fsdp"), lax.axis_size("dp")
    devices = ("dp", "fsdp")
    share = conv_weight.shape[0]
    units = expand_weight.shape[1]
    half = pl.cdiv(units // 128, 2) * 128
    bits = list(range(n_fs.bit_length() - 1))
    core = bit_of("dp", 0)
    x = inputs[0].transpose(1, 0, 2)
    og = out_grad[0].transpose(1, 0, 2)
    block = 5 * GRP

    ratio = expand_bias.shape[0] // share
    small = jnp.concatenate(
        [
            conv_weight.T,
            norm_gain[None],
            norm_bias[None],
            project_bias.astype(F32)[None],
            expand_bias.astype(F32).reshape(ratio, share),
        ],
        axis=0,
    )
    small = from_all(small, "fsdp")
    e_bias = jnp.pad(small[:, TAPS + 3 :].reshape(1, units), ((0, 0), (0, 2 * half - units)))
    pick = tap_picker()
    x_up, x_dn = halo(x)

    def columns(weight):
        wide = jnp.pad(weight, ((0, 0), (0, 2 * half - units)))
        mine = lax.dynamic_slice_in_dim(wide, core * half, half, axis=1)
        return mine.reshape((1,) * len(bits) + (share, half))

    we_own, wp_own = columns(expand_weight), columns(project_weight)
    zeros = [bit_of("fsdp", bit) == 0 for bit in bits]
    for n in bits[:-1]:
        we_own = gather_step(we_own, n, zeros[n])
        wp_own = gather_step(wp_own, bits[-1 - n], zeros[-1 - n])
    eb_own = lax.dynamic_slice_in_dim(e_bias, core * half, half, axis=1)
    eb_peer = lax.dynamic_slice_in_dim(e_bias, (1 - core) * half, half, axis=1)

    sample = lax.axis_index("fsdp")
    length = lax.dynamic_index_in_dim(rollout_lengths, sample, keepdims=False)
    live = jnp.where(sample % ROLLOUT < length, 1.0, 0.0).astype(F32)
    weight = live * ocean_mask.astype(F32)
    m16 = jnp.broadcast_to(weight[:, None, :], (rows, GRP, width))
    count_here = jnp.sum(weight)
    counts = jnp.stack([count_here, 1.0 / jnp.maximum(count_here, 1.0)])

    bg_c, bg_p, bg_sum = mask_gradient(og, m16)

    copies = n_fs * n_dp
    ready = after(m16, bg_c, we_own, wp_own)
    conv, stats, par = conv_forward(x, x_up, x_dn, small, pick, ready, counts, copies, block)
    n = bits[-1]
    we_own = gather_step(we_own, n, after(zeros[n], conv)).reshape(channels, half)
    wp_own = gather_step(wp_own, bits[-1 - n], after(zeros[-1 - n], conv)).reshape(channels, half)
    we_peer = flip_bit(we_own, "dp", 0)
    wp_peer = flip_bit(wp_own, "dp", 0)
    stats = lax.all_to_all(stats, devices, 0, 0)
    act_c, act_p, stat = activate(conv, stats, par)

    groups = [[i for i in range(n_dp) if i % 2 == c] for c in range(2)]
    orders = {2: bits[::-1], 3: bits}
    first = half // (2 * TILE) * TILE
    second = half - first
    common = (act_p, act_c, bg_p, bg_c)

    def added(peer, own):
        return {k: own[k] + flip_bit(peer[k], "dp", 0).astype(F32) for k in orders}

    def stage(sums, n):
        return {k: scatter_step(v, orders[k][n], n) for k, v in sums.items()}

    def over_bands(sums):
        return {k: lax.psum(v.astype(BF16), "dp", axis_index_groups=groups) for k, v in sums.items()}

    q1 = hidden_layer(*common, we_peer, wp_peer, eb_peer, 0, first, BF16)
    o1 = hidden_layer(*common, we_own, wp_own, after(eb_own, q1[0]), 0, first, F32)
    s1 = added(q1, o1)
    q2 = hidden_layer(*common, we_peer, wp_peer, after(eb_peer, s1[2], s1[3]), first, second, BF16)
    for n in range(len(bits) - 1):
        s1 = stage(s1, n)
    o2 = hidden_layer(*common, we_own, wp_own, after(eb_own, q2[0], s1[2], s1[3]), first, second, F32)
    s1 = stage(s1, len(bits) - 1)
    s1 = {k: v.astype(BF16) for k, v in s1.items()}

    cuts = ((1, 0, first), (0, 0, first), (1, first, second), (0, first, second))
    parts = (q1, o1, q2, o2)
    s2 = added(q2, o2)
    ready = after(stat, s1[2], s1[3], s2[2], s2[3])
    da, sums = activation_gradient((we_own, we_peer), [p[1] for p in parts], cuts, conv, ready, copies)
    sums = lax.all_to_all(sums, devices, 0, 0)
    s1 = over_bands(s1)
    block_out = block_output(
        (wp_own, wp_peer), [p[0] for p in parts], cuts, x, m16, after(par, da, s2[2], s2[3])
    )
    for n in range(len(bits) - 1):
        s2 = stage(s2, n)
    conv_grad, totals = conv_gradient(da, conv, m16, sums, stat, after(par, block_out, s2[2], s2[3]))
    g_up, g_dn = halo(conv_grad)
    s2 = stage(s2, len(bits) - 1)
    s2 = {k: v.astype(BF16) for k, v in s2.items()}
    tap_local = tap_gradient(x, x_up, x_dn, after(conv_grad, s2[2], s2[3]), block, share)
    s2 = over_bands({k: after(v, s1[2], s1[3]) for k, v in s2.items()})

    eb_o = jnp.concatenate([o1[4], o2[4]], axis=1)
    eb_q = jnp.concatenate([q1[4], q2[4]], axis=1)
    eb_all = jnp.concatenate(
        [jnp.where(core == 0, eb_o, eb_q), jnp.where(core == 0, eb_q, eb_o)], axis=1
    )[0, :units]
    local = jnp.concatenate(
        [
            tap_local,
            bg_sum[0, :8].reshape(-1)[:channels].reshape(n_fs, 1, share),
            eb_all.reshape(n_fs, ratio, share),
        ],
        axis=1,
    )
    local = jnp.sum(lax.all_to_all(local, "fsdp", 0, 0), axis=0)
    input_grad = input_gradient(conv_grad, g_up, g_dn, after(par, tap_local), pick, og, m16, block)
    local = jnp.sum(from_all(local, "dp"), axis=0)

    def joined(which):
        mine = jnp.concatenate([s1[which], after(s2[which], input_grad)], axis=1)
        other = flip_bit(mine, "dp", 0)
        low, high = jnp.where(core == 0, mine, other), jnp.where(core == 0, other, mine)
        return jnp.concatenate([low, high], axis=1)[:, :units].astype(F32)

    project_grad = joined(2)
    expand_grad = joined(3)

    start = lax.axis_index("fsdp") * share
    totals = totals.reshape(2, -1)
    per_channel = lambda v: v.reshape(-1)[:channels]
    return (
        block_out.transpose(1, 0, 2)[None],
        input_grad.transpose(1, 0, 2)[None],
        local[:TAPS].T,
        lax.dynamic_slice_in_dim(totals[1], start, share),
        lax.dynamic_slice_in_dim(totals[0], start, share),
        expand_grad,
        local[TAPS + 1 :].reshape(-1),
        project_grad,
        local[TAPS],
        per_channel(stat[0:8]),
        per_channel(stat[16:24]),
    )


def solution(mesh):
    rows = P("fsdp", None, "dp", None)
    return jax.shard_map(
        per_device,
        mesh=mesh,
        in_specs=(
            rows,
            rows,
            P("dp", None),
            P(),
            P("fsdp", None),
            P("fsdp"),
            P("fsdp"),
            P("fsdp", None),
            P("fsdp"),
            P("fsdp", None),
            P("fsdp"),
        ),
        out_specs=(
            rows,
            rows,
            P("fsdp", None),
            P("fsdp"),
            P("fsdp"),
            P("fsdp", None),
            P("fsdp"),
            P("fsdp", None),
            P("fsdp"),
            P(),
            P(),
        ),
        check_vma=False,
    )
```

```python
import functools

import jax
import jax.numpy as jnp
from jax import lax
from jax.experimental import pallas as pl
from jax.experimental.pallas import tpu as pltpu
from jax.sharding import PartitionSpec as P

KS = 7
REACH = KS // 2
TAPS = KS * KS
ROLLOUT = 8
EPS = 1e-05
F32, BF16 = jnp.float32, jnp.bfloat16
GRP = 16
TILE = 256
MIB = 2**20
GELU_A = 0.7978845608028654
GELU_B = 0.044715
NT = (((1,), (1,)), ((), ()))
TN = (((0,), (0,)), ((), ()))


def params(limit=60):
    return pltpu.CompilerParams(vmem_limit_bytes=limit * MIB)


def cost(us):
    return pl.CostEstimate(flops=int(us * 1.15e9), bytes_accessed=10**5, transcendentals=0)


def whole(shape):
    zeros = (0,) * len(shape)
    return pl.BlockSpec(shape, lambda *g: zeros, pipeline_mode=pl.Buffered(1))


def roll_lanes(v, shift):
    shift %= v.shape[-1]
    return v if shift == 0 else pltpu.roll(v, shift, v.ndim - 1)


def columns_of(*rows):
    pieces = []
    for k in range(rows[0].shape[0]):
        used = [v[k : k + 1, :] for v in rows]
        block = jnp.concatenate(used + [jnp.zeros((128 - len(rows), 128), F32)], axis=0)
        pieces.append(block.T)
    return jnp.concatenate(pieces, axis=0)


def wide(column):
    return jnp.broadcast_to(column, (column.shape[0], 128))


def copies_of(cols, out_ref):
    copies = out_ref.shape[0]
    for k in range(cols.shape[0] // 128):
        block = cols[k * 128 : (k + 1) * 128, :].T
        for q in range(2):
            row = jnp.broadcast_to(block[q : q + 1, :][None], (copies, 1, 128))
            out_ref[:, 8 * q + k : 8 * q + k + 1, :] = row


def spread_taps(cols, pick_ref, e_ref):
    count = cols.shape[0]
    lane = lax.broadcasted_iota(jnp.int32, (count, 128), 1)
    own = lax.broadcasted_iota(jnp.int32, (count, 128), 0) % GRP == lane % GRP
    high = cols.astype(BF16)
    low = (cols - high.astype(F32)).astype(BF16)
    for h, part in enumerate((high, low)):
        for j in range(KS):
            picked = jnp.dot(part, pick_ref[j], preferred_element_type=F32)
            e_ref[h, j] = jnp.where(own, picked, 0.0).astype(BF16)


def tap_picker():
    tap = lax.broadcasted_iota(jnp.int32, (128, 128), 0)
    lane = lax.broadcasted_iota(jnp.int32, (128, 128), 1)
    inside = lane < KS * GRP
    first = KS * (lane // GRP)
    return [jnp.where((tap == first + j) & inside, 1.0, 0.0).astype(BF16) for j in range(KS)]


def conv_rows(field_ref, taps_ref, s, rows, flip):
    x = field_ref[:, s, :].reshape((rows + 2 * REACH) * GRP, field_ref.shape[-1])
    parts = [taps_ref[h, :, s, :].reshape(KS * GRP, 128)[:, : KS * GRP] for h in range(2)]
    taps = jnp.concatenate(parts, axis=1)
    out = []
    for r in range(rows):
        src = rows - 1 - r if flip else r
        window = x[src * GRP : (src + KS) * GRP]
        sums = jnp.dot(taps, jnp.concatenate([window, window], axis=0), preferred_element_type=F32)
        acc = None
        for j in range(KS):
            moved = roll_lanes(sums[j * GRP : (j + 1) * GRP], j - REACH if flip else REACH - j)
            acc = moved if acc is None else acc + moved
        out.append(acc)
    return out


def conv_kernel(
    x_ref, up_ref, dn_ref, small_ref, m_ref, out_ref, st_ref, par_ref,
    field_ref, cols_ref, e_ref, pick_ref, count_ref, *, share
):
    rows, block = x_ref.shape[0], x_ref.shape[1]
    step = pl.program_id(0)

    @pl.when(step == 0)
    def _():
        for j, pick in enumerate(tap_picker()):
            pick_ref[j] = pick
        count = jnp.sum(jnp.sum(m_ref[...], axis=0), axis=1, keepdims=True)[0:8]
        count_ref[...] = jnp.broadcast_to(count, (8, 128))
        cols_ref[...] = jnp.zeros(cols_ref.shape, F32)
        given, wide = small_ref.shape[1], pl.cdiv(share, 128) * 128
        for f in range(small_ref.shape[0]):
            v = small_ref[f]
            v = jnp.concatenate([v, jnp.zeros((given, wide - share), F32)], axis=1)
            v = jnp.concatenate([v, jnp.zeros((128 - given, wide), F32)], axis=0)
            par_ref[f * share : (f + 1) * share, :] = v.T[:share]

    field_ref[0:REACH] = up_ref[...]
    field_ref[REACH : REACH + rows] = x_ref[...]
    field_ref[REACH + rows :] = dn_ref[...]
    here = pl.multiple_of(step * block, GRP)
    spread_taps(par_ref[pl.ds(here, block), :], pick_ref, e_ref)
    lane = lax.broadcasted_iota(jnp.int32, (GRP, 128), 1)
    inv_n = 1.0 / jnp.maximum(count_ref[0:1, 0:1], 1.0)
    for g in range(block // GRP):
        s = pl.ds(g * GRP, GRP)
        acc = conv_rows(field_ref, e_ref, s, rows, False)
        total = None
        for r in range(rows):
            out_ref[r, s, :] = acc[r]
            v = acc[r] * m_ref[r]
            total = v if total is None else total + v
        mean = jnp.sum(total, axis=-1, keepdims=True) * inv_n
        total = None
        for r in range(rows):
            d = acc[r] - mean
            v = d * d * m_ref[r]
            total = v if total is None else total + v
        dev = jnp.sum(total, axis=-1, keepdims=True)
        at = pl.multiple_of(step * block + g * GRP, GRP)
        cols_ref[pl.ds(at, GRP), :] = jnp.where(lane == 0, mean, dev)

    @pl.when(step == pl.num_programs(0) - 1)
    def _():
        st_ref[...] = jnp.broadcast_to(count_ref[0:1, :][None], st_ref.shape)
        copies_of(cols_ref[...], st_ref)


def conv_forward(x, up, dn, small, m16, copies, block):
    rows, channels, width = x.shape
    n_fs, given, share = small.shape
    padded = pl.cdiv(channels, 128) * 128
    return pl.pallas_call(
        functools.partial(conv_kernel, share=share),
        grid=(channels // block,),
        in_specs=[
            pl.BlockSpec((rows, block, width), lambda g: (0, g, 0)),
            pl.BlockSpec((REACH, block, width), lambda g: (0, g, 0)),
            pl.BlockSpec((REACH, block, width), lambda g: (0, g, 0)),
            whole((n_fs, given, share)),
            whole((rows, GRP, width)),
        ],
        out_specs=[
            pl.BlockSpec((rows, block, width), lambda g: (0, g, 0)),
            pl.BlockSpec((copies, 16, 128), lambda g: (0, 0, 0)),
            pl.BlockSpec((channels, 128), lambda g: (0, 0)),
        ],
        out_shape=[
            jax.ShapeDtypeStruct((rows, channels, width), F32),
            jax.ShapeDtypeStruct((copies, 16, 128), F32),
            jax.ShapeDtypeStruct((channels, 128), F32),
        ],
        scratch_shapes=[
            pltpu.VMEM((rows + 2 * REACH, block, width), BF16),
            pltpu.VMEM((padded, 128), F32),
            pltpu.VMEM((2, KS, block, 128), BF16),
            pltpu.VMEM((KS, 128, 128), BF16),
            pltpu.VMEM((8, 128), F32),
        ],
        compiler_params=params(),
        cost_estimate=cost(0.4),
        name="conv_forward",
    )(x, up, dn, small, m16)


def input_grad_kernel(
    g_ref, up_ref, dn_ref, par_ref, og_ref, m_ref, out_ref, field_ref, e_ref, pick_ref
):
    @pl.when(pl.program_id(0) == 0)
    def _():
        for j, pick in enumerate(tap_picker()):
            pick_ref[j] = pick

    rows, block = g_ref.shape[0], g_ref.shape[1]
    last = rows + 2 * REACH - 1
    for q in range(REACH):
        field_ref[last - q] = up_ref[q]
        field_ref[REACH - 1 - q] = dn_ref[q]
    for q in range(rows):
        field_ref[last - REACH - q] = g_ref[q]
    spread_taps(par_ref[...], pick_ref, e_ref)
    for g in range(block // GRP):
        s = pl.ds(g * GRP, GRP)
        acc = conv_rows(field_ref, e_ref, s, rows, True)
        for r in range(rows):
            out_ref[r, s, :] = og_ref[r, s, :].astype(F32) * m_ref[r] + acc[r]


def input_gradient(grad, up, dn, par, og, m16, block):
    rows, channels, width = grad.shape
    return pl.pallas_call(
        input_grad_kernel,
        grid=(channels // block,),
        in_specs=[
            pl.BlockSpec((rows, block, width), lambda g: (0, g, 0)),
            pl.BlockSpec((REACH, block, width), lambda g: (0, g, 0)),
            pl.BlockSpec((REACH, block, width), lambda g: (0, g, 0)),
            pl.BlockSpec((block, 128), lambda g: (g, 0)),
            pl.BlockSpec((rows, block, width), lambda g: (0, g, 0)),
            whole((rows, GRP, width)),
        ],
        out_specs=pl.BlockSpec((rows, block, width), lambda g: (0, g, 0)),
        out_shape=jax.ShapeDtypeStruct((rows, channels, width), F32),
        scratch_shapes=[
            pltpu.VMEM((rows + 2 * REACH, block, width), BF16),
            pltpu.VMEM((2, KS, block, 128), BF16),
            pltpu.VMEM((KS, 128, 128), BF16),
        ],
        compiler_params=params(),
        cost_estimate=cost(0.32),
        name="input_gradient",
    )(grad, up, dn, par, og, m16)


def tap_grad_kernel(x_ref, up_ref, dn_ref, g_ref, out_ref, field_ref, cols_ref, *, share):
    rows, block, width = x_ref.shape
    field_ref[0:REACH] = up_ref[...]
    field_ref[REACH : REACH + rows] = x_ref[...]
    field_ref[REACH + rows :] = dn_ref[...]
    lane = lax.broadcasted_iota(jnp.int32, (GRP, 128), 1)
    own = lax.broadcasted_iota(jnp.int32, (GRP, 128), 0) == lane % GRP
    for g in range(block // GRP):
        s = pl.ds(g * GRP, GRP)
        x = field_ref[:, s, :].reshape((rows + 2 * REACH) * GRP, width)
        fields = jnp.concatenate([x[r * GRP : (r + KS) * GRP] for r in range(rows)], axis=1)
        grads = []
        for j in range(KS):
            moved = [roll_lanes(g_ref[r, s, :], j - REACH) for r in range(rows)]
            grads.append(jnp.concatenate(moved, axis=1))
        grads = jnp.concatenate(grads, axis=0)
        sums = lax.dot_general(grads, fields, NT, preferred_element_type=F32)
        sums = jnp.concatenate([sums, jnp.zeros((KS * GRP, 128 - KS * GRP), F32)], axis=1)
        out = None
        for j in range(KS):
            acc = jnp.where(own, sums[j * GRP : (j + 1) * GRP], 0.0)
            for k in (8, 4, 2, 1):
                acc = acc + pltpu.roll(acc, 128 - k, 1)
            acc = roll_lanes(acc, j)
            out = acc if out is None else jnp.where(lane % GRP == j, acc, out)
        at = pl.multiple_of(pl.program_id(0) * block + g * GRP, GRP)
        cols_ref[pl.ds(at, GRP), :] = out

    @pl.when(pl.program_id(0) == pl.num_programs(0) - 1)
    def _():
        blocks = [cols_ref[k : k + 128, :].T for k in range(0, cols_ref.shape[0], 128)]
        wide = jnp.concatenate(blocks, axis=1)
        taps = jnp.concatenate([wide[GRP * i : GRP * i + KS] for i in range(KS)], axis=0)
        for f in range(out_ref.shape[0]):
            out_ref[f] = taps[:, f * share : (f + 1) * share]


def tap_gradient(x, up, dn, grad, block, share):
    rows, channels, width = x.shape
    padded = pl.cdiv(channels, 128) * 128
    return pl.pallas_call(
        functools.partial(tap_grad_kernel, share=share),
        grid=(channels // block,),
        in_specs=[
            pl.BlockSpec((rows, block, width), lambda g: (0, g, 0)),
            pl.BlockSpec((REACH, block, width), lambda g: (0, g, 0)),
            pl.BlockSpec((REACH, block, width), lambda g: (0, g, 0)),
            pl.BlockSpec((rows, block, width), lambda g: (0, g, 0)),
        ],
        out_specs=pl.BlockSpec((channels // share, TAPS, share), lambda g: (0, 0, 0)),
        out_shape=jax.ShapeDtypeStruct((channels // share, TAPS, share), F32),
        scratch_shapes=[
            pltpu.VMEM((rows + 2 * REACH, block, width), BF16),
            pltpu.VMEM((padded, 128), F32),
        ],
        compiler_params=params(),
        cost_estimate=cost(0.35),
        name="tap_gradient",
    )(x, up, dn, grad)


def mask_grad_kernel(og_ref, m_ref, out_ref, sum_ref, cols_ref):
    row = pl.program_id(0)
    channels = og_ref.shape[1]
    v = og_ref[0].astype(F32) * m_ref[0, 0:1]
    out_ref[...] = v.astype(BF16)
    part = v[:, 0:128]
    for k in range(128, v.shape[1], 128):
        part = part + v[:, k : k + 128]

    @pl.when(row == 0)
    def _():
        cols_ref[...] = jnp.zeros(cols_ref.shape, F32)

    cols_ref[0:channels, :] += part

    @pl.when(row == pl.num_programs(0) - 1)
    def _():
        sums = jnp.broadcast_to(jnp.sum(cols_ref[...], axis=1, keepdims=True), cols_ref.shape)
        copies_of(sums, sum_ref)


def mask_gradient(og, m16):
    rows, channels, width = og.shape
    padded = pl.cdiv(channels, 128) * 128
    pixels = rows * width
    return pl.pallas_call(
        mask_grad_kernel,
        grid=(rows,),
        in_specs=[
            pl.BlockSpec((1, channels, width), lambda r: (r, 0, 0)),
            pl.BlockSpec((1, GRP, width), lambda r: (r, 0, 0)),
        ],
        out_specs=[
            pl.BlockSpec((channels, width), lambda r: (0, r)),
            pl.BlockSpec((1, 16, 128), lambda r: (0, 0, 0)),
        ],
        out_shape=[
            jax.ShapeDtypeStruct((channels, pixels), BF16),
            jax.ShapeDtypeStruct((1, 16, 128), F32),
        ],
        scratch_shapes=[pltpu.VMEM((padded, 128), F32)],
        compiler_params=params(),
        cost_estimate=cost(0.11),
        name="mask_gradient",
    )(og, m16)


def activate_kernel(conv_ref, all_ref, par_ref, out_ref, stat_ref, cols_ref):
    channels = conv_ref.shape[1]

    @pl.when(pl.program_id(0) == 0)
    def _():
        means, squares = all_ref[:, 0:8, :], all_ref[:, 8:16, :]
        counts = all_ref[:, 7:8, :]
        count = jnp.sum(counts, axis=0)
        mean = jnp.sum(counts * means, axis=0) / count
        apart = means - mean[None]
        variance = jnp.sum(squares + counts * apart * apart, axis=0) / count
        inv_std = lax.rsqrt(variance + EPS)
        stat_ref[0:8] = mean
        stat_ref[8:16] = inv_std
        stat_ref[16:24] = jnp.sqrt(variance + EPS)
        stat_ref[24:32] = jnp.broadcast_to(count, (8, 128))
        c, p = columns_of(mean[0:7], inv_std[0:7])[:channels], par_ref[...]
        cols_ref[0] = wide(c[:, 0:1])
        cols_ref[1] = wide(c[:, 1:2] * p[:, TAPS : TAPS + 1])
        cols_ref[2] = wide(p[:, TAPS + 1 : TAPS + 2])

    for k in range(0, out_ref.shape[1], 128):
        v = (conv_ref[0, :, k : k + 128] - cols_ref[0]) * cols_ref[1] + cols_ref[2]
        out_ref[:, k : k + 128] = v.astype(BF16)


def activate(conv, stats, par):
    rows, channels, width = conv.shape
    pixels = rows * width
    return pl.pallas_call(
        activate_kernel,
        grid=(rows,),
        in_specs=[
            pl.BlockSpec((1, channels, width), lambda r: (r, 0, 0)),
            whole(stats.shape),
            whole(par.shape),
        ],
        out_specs=[
            pl.BlockSpec((channels, width), lambda r: (0, r)),
            pl.BlockSpec((32, 128), lambda r: (0, 0)),
        ],
        out_shape=[
            jax.ShapeDtypeStruct((channels, pixels), BF16),
            jax.ShapeDtypeStruct((32, 128), F32),
        ],
        scratch_shapes=[pltpu.VMEM((3, channels, 128), F32)],
        compiler_params=params(),
        cost_estimate=cost(0.13),
        name="activate",
    )(conv, stats, par)


def gelu_parts(v):
    v2 = v * v
    t = jnp.tanh(v * (GELU_A + (GELU_A * GELU_B) * v2))
    s = 0.5 * t + 0.5
    h = v * s
    return h, s + h * (1.0 - s) * (2 * GELU_A + (6 * GELU_A * GELU_B) * v2)


def halves(v, mine, piece):
    keep, send = [], []
    for o in range(0, v.shape[0], 2 * piece):
        first, second = v[o : o + piece], v[o + piece : o + 2 * piece]
        keep.append(jnp.where(mine == 0, first, second))
        send.append(jnp.where(mine == 0, second, first))
    return jnp.concatenate(keep, axis=0), jnp.concatenate(send, axis=0)


def hidden_kernel(bits_ref, act_ref, bg_ref, we_ref, wp_ref, eb_ref, *refs, step, pieces):
    if pieces is None:
        h_ref, g_ref, dwp_ref, dwe_ref, ebg_ref = refs
    else:
        other_p, other_e, h_ref, g_ref, keep_p, send_p, keep_e, send_e, ebg_ref = refs
    we, wp, bias = we_ref[...], wp_ref[...], eb_ref[...]
    total = None
    for p in range(0, act_ref.shape[1], step):
        pre = lax.dot_general(act_ref[:, p : p + step], we, TN, preferred_element_type=F32) + bias
        pull = lax.dot_general(bg_ref[:, p : p + step], wp, TN, preferred_element_type=F32)
        h, slope = gelu_parts(pre)
        grad = (pull * slope).astype(BF16)
        h_ref[p : p + step, :] = h.astype(BF16)
        g_ref[p : p + step, :] = grad
        part = jnp.sum(grad.astype(F32), axis=0, keepdims=True)
        total = part if total is None else total + part
    ebg_ref[...] = total
    dwp = jnp.dot(bg_ref[...], h_ref[...], preferred_element_type=F32)
    dwe = jnp.dot(act_ref[...], g_ref[...], preferred_element_type=F32)
    if pieces is None:
        dwp_ref[...] = dwp.astype(BF16)
        dwe_ref[...] = dwe.astype(BF16)
    else:
        keep, send = halves(dwp + other_p[...].astype(F32), bits_ref[0], pieces[0])
        keep_p[...] = keep
        send_p[...] = send.astype(BF16)
        keep, send = halves(dwe + other_e[...].astype(F32), bits_ref[1], pieces[1])
        keep_e[...] = keep
        send_e[...] = send.astype(BF16)


def hidden_layer(act, bg, we, wp, eb, first, units, bits, others=None, pieces=None):
    channels, pixels = act.shape
    off = first // TILE
    column = lambda rows: pl.BlockSpec((rows, TILE), lambda g: (0, g))
    weight = pl.BlockSpec((channels, TILE), lambda g: (0, g + off))
    shape = lambda rows, dtype: jax.ShapeDtypeStruct((rows, units), dtype)
    in_specs = [pl.BlockSpec(memory_space=pltpu.SMEM), whole(act.shape), whole(bg.shape), weight, weight]
    in_specs.append(pl.BlockSpec((1, TILE), lambda g: (0, g + off)))
    operands = [bits, act, bg, we, wp, eb]
    out_specs = [column(pixels), column(pixels)]
    out_shape = [shape(pixels, BF16), shape(pixels, BF16)]
    if others is None:
        out_specs += [column(channels), column(channels)]
        out_shape += [shape(channels, BF16), shape(channels, BF16)]
    else:
        in_specs += [column(channels), column(channels)]
        operands += list(others)
        out_specs += [column(channels // 2)] * 4
        out_shape += [shape(channels // 2, F32), shape(channels // 2, BF16)] * 2
    out_specs.append(column(1))
    out_shape.append(shape(1, F32))
    return pl.pallas_call(
        functools.partial(hidden_kernel, step=128, pieces=pieces),
        grid=(pl.cdiv(units, TILE),),
        in_specs=in_specs,
        out_specs=out_specs,
        out_shape=out_shape,
        compiler_params=params(),
        cost_estimate=cost(0.3),
        name="hidden_layer",
    )(*operands)


def contract(weights, hiddens):
    total = None
    for (w_ref, first, units), h_ref in zip(weights, hiddens, strict=True):
        part = lax.dot_general(
            w_ref[:, first : first + units], h_ref[...], NT, preferred_element_type=F32
        )
        total = part if total is None else total + part
    return total


def act_grad_kernel(*refs, cuts):
    n = len(cuts)
    w_refs, h_refs = refs[0:2], refs[2 : 2 + n]
    conv_ref, stat_ref, out_ref, sum_ref, cols_ref, acc_ref = refs[2 + n :]
    channels = conv_ref.shape[1]
    row = pl.program_id(0)

    @pl.when(row == 0)
    def _():
        cols_ref[...] = columns_of(stat_ref[0:7], stat_ref[8:15])[: cols_ref.shape[0]]
        acc_ref[...] = jnp.zeros(acc_ref.shape, F32)

    grad = contract([(w_refs[w], first, units) for w, first, units in cuts], h_refs)
    out_ref[0] = grad
    c = cols_ref[0:channels, :]
    scaled = grad * ((conv_ref[0] - c[:, 0:1]) * c[:, 1:2])
    plain, weighted = grad[:, 0:128], scaled[:, 0:128]
    for k in range(128, grad.shape[1], 128):
        plain = plain + grad[:, k : k + 128]
        weighted = weighted + scaled[:, k : k + 128]
    acc_ref[0, 0:channels, :] += plain
    acc_ref[1, 0:channels, :] += weighted

    @pl.when(row == pl.num_programs(0) - 1)
    def _():
        lane = lax.broadcasted_iota(jnp.int32, cols_ref.shape, 1)
        plain = jnp.sum(acc_ref[0], axis=1, keepdims=True)
        weighted = jnp.sum(acc_ref[1], axis=1, keepdims=True)
        sum_ref[...] = jnp.zeros(sum_ref.shape, F32)
        copies_of(jnp.where(lane == 0, plain, weighted), sum_ref)


def activation_gradient(weights, hiddens, cuts, conv, stat, copies):
    rows, channels, width = conv.shape
    padded = pl.cdiv(channels, 128) * 128
    return pl.pallas_call(
        functools.partial(act_grad_kernel, cuts=cuts),
        grid=(rows,),
        in_specs=[whole(w.shape) for w in weights]
        + [pl.BlockSpec((width, h.shape[1]), lambda r: (r, 0)) for h in hiddens]
        + [pl.BlockSpec((1, channels, width), lambda r: (r, 0, 0)), whole(stat.shape)],
        out_specs=[
            pl.BlockSpec((1, channels, width), lambda r: (r, 0, 0)),
            pl.BlockSpec((copies, 16, 128), lambda r: (0, 0, 0)),
        ],
        out_shape=[
            jax.ShapeDtypeStruct((rows, channels, width), F32),
            jax.ShapeDtypeStruct((copies, 16, 128), F32),
        ],
        scratch_shapes=[pltpu.VMEM((padded, 128), F32), pltpu.VMEM((2, padded, 128), F32)],
        compiler_params=params(),
        cost_estimate=cost(0.32),
        name="activation_gradient",
    )(*weights, *hiddens, conv, stat)


def block_out_kernel(*refs, cuts):
    n = len(cuts)
    w_refs, h_refs = refs[0:2], refs[2 : 2 + n]
    x_ref, m_ref, par_ref = refs[2 + n : 5 + n]
    out_ref = refs[-1]
    branch = contract([(w_refs[w], first, units) for w, first, units in cuts], h_refs)
    branch = branch + par_ref[:, TAPS + 2 : TAPS + 3]
    out_ref[0] = ((x_ref[0].astype(F32) + branch) * m_ref[0, 0:1]).astype(BF16)


def block_output(weights, hiddens, cuts, x, m16, par):
    rows, channels, width = x.shape
    return pl.pallas_call(
        functools.partial(block_out_kernel, cuts=cuts),
        grid=(rows,),
        in_specs=[whole(w.shape) for w in weights]
        + [pl.BlockSpec((width, h.shape[1]), lambda r: (r, 0)) for h in hiddens]
        + [
            pl.BlockSpec((1, channels, width), lambda r: (r, 0, 0)),
            pl.BlockSpec((1, GRP, width), lambda r: (r, 0, 0)),
            whole(par.shape),
        ],
        out_specs=pl.BlockSpec((1, channels, width), lambda r: (r, 0, 0)),
        out_shape=jax.ShapeDtypeStruct((rows, channels, width), BF16),
        compiler_params=params(),
        cost_estimate=cost(0.29),
        name="block_output",
    )(*weights, *hiddens, x, m16, par)


def conv_grad_kernel(
    da_ref, conv_ref, m_ref, all_ref, stat_ref, par_ref, out_ref, top_ref, end_ref, sum_ref, cols_ref
):
    row = pl.program_id(0)
    channels = conv_ref.shape[1]

    @pl.when(pl.program_id(0) == 0)
    def _():
        sums = jnp.sum(all_ref[...], axis=0)
        sum_ref[...] = sums
        count = stat_ref[24:32]
        c = columns_of(
            stat_ref[0:7], stat_ref[8:15], (sums[0:8] / count)[0:7], (sums[8:16] / count)[0:7]
        )[:channels]
        factor = c[:, 1:2] * par_ref[:, TAPS : TAPS + 1]
        cols_ref[0] = wide(c[:, 0:1])
        cols_ref[1] = wide(factor)
        cols_ref[2] = wide(factor * c[:, 2:3])
        cols_ref[3] = wide(factor * c[:, 1:2] * c[:, 3:4])

    for k in range(0, out_ref.shape[2], 128):
        s = slice(k, k + 128)
        apart = conv_ref[0, :, s] - cols_ref[0]
        correction = m_ref[0, 0:1, s] * (cols_ref[2] + apart * cols_ref[3])
        out_ref[0, :, s] = (cols_ref[1] * da_ref[0, :, s] - correction).astype(BF16)
    grad = out_ref[0]

    @pl.when(row < REACH)
    def _():
        top_ref[0] = grad

    @pl.when(row >= pl.num_programs(0) - REACH)
    def _():
        end_ref[0] = grad


def conv_gradient(da, conv, m16, sums, stat, par):
    rows, channels, width = conv.shape
    return pl.pallas_call(
        conv_grad_kernel,
        grid=(rows,),
        in_specs=[
            pl.BlockSpec((1, channels, width), lambda r: (r, 0, 0)),
            pl.BlockSpec((1, channels, width), lambda r: (r, 0, 0)),
            pl.BlockSpec((1, GRP, width), lambda r: (r, 0, 0)),
            whole(sums.shape),
            whole(stat.shape),
            whole(par.shape),
        ],
        out_specs=[
            pl.BlockSpec((1, channels, width), lambda r: (r, 0, 0)),
            pl.BlockSpec((1, channels, width), lambda r: (jnp.minimum(r, REACH - 1), 0, 0)),
            pl.BlockSpec((1, channels, width), lambda r: (jnp.maximum(r - rows + REACH, 0), 0, 0)),
            pl.BlockSpec((16, 128), lambda r: (0, 0)),
        ],
        out_shape=[
            jax.ShapeDtypeStruct((rows, channels, width), BF16),
            jax.ShapeDtypeStruct((REACH, channels, width), BF16),
            jax.ShapeDtypeStruct((REACH, channels, width), BF16),
            jax.ShapeDtypeStruct((16, 128), F32),
        ],
        scratch_shapes=[pltpu.VMEM((4, channels, 128), F32)],
        compiler_params=params(),
        cost_estimate=cost(0.19),
        name="conv_gradient",
    )(da, conv, m16, sums, stat, par)


def join_kernel(index_ref, *refs, names, share):
    n = len(names)
    for index in names:

        @pl.when(index_ref[0] == index)
        def _(index=index):
            for w in range(2):
                for k, name in enumerate(names):
                    row = (index ^ name) * share
                    refs[2 * n + w][row : row + share, :] = refs[w * n + k][...]


def join_pieces(index, first, second):
    names = sorted(first)
    share, cols = first[0].shape
    channels = share * len(names)
    if share % 8:
        out = []
        for pieces in (first, second):
            whole_array = jnp.zeros((channels, cols), BF16)
            for name in names:
                start = (index ^ name) * share
                whole_array = lax.dynamic_update_slice_in_dim(whole_array, pieces[name], start, axis=0)
            out.append(whole_array)
        return out
    tile = 2 * TILE
    column = lambda height: pl.BlockSpec((height, tile), lambda g: (0, g))
    return pl.pallas_call(
        functools.partial(join_kernel, names=names, share=share),
        grid=(pl.cdiv(cols, tile),),
        in_specs=[pl.BlockSpec(memory_space=pltpu.SMEM)] + [column(share)] * (2 * len(names)),
        out_specs=[column(channels)] * 2,
        out_shape=[jax.ShapeDtypeStruct((channels, cols), BF16)] * 2,
        compiler_params=params(),
        cost_estimate=cost(0.08),
        name="join_pieces",
    )(index[None], *[first[k] for k in names], *[second[k] for k in names])


def place_kernel(core_ref, *refs, starts):
    n = len(starts)
    for w in range(2):
        out_ref = refs[4 * n + w]
        for k, (low, high) in enumerate(starts):
            mine, other = refs[2 * (w * n + k)][...], refs[2 * (w * n + k) + 1][...]
            mine, other = mine.astype(F32), other.astype(F32)
            for at, v in (
                (low, jnp.where(core_ref[0] == 0, mine, other)),
                (high, jnp.where(core_ref[0] == 0, other, mine)),
            ):
                wide = min(v.shape[1], out_ref.shape[1] - at)
                out_ref[:, at : at + wide] = v[:, :wide]


def place_columns(core, pairs, starts, units):
    share = pairs[0][0][0].shape[0]
    tile = share
    operands = [v for parts in pairs for pair in parts for v in pair]
    return pl.pallas_call(
        functools.partial(place_kernel, starts=starts),
        grid=(share // tile,),
        in_specs=[pl.BlockSpec(memory_space=pltpu.SMEM)]
        + [pl.BlockSpec((tile, v.shape[1]), lambda g: (g, 0)) for v in operands],
        out_specs=[pl.BlockSpec((tile, units), lambda g: (g, 0))] * 2,
        out_shape=[jax.ShapeDtypeStruct((share, units), F32)] * 2,
        compiler_params=params(),
        cost_estimate=cost(0.08),
        name="place_columns",
    )(core[None], *operands)


def halo(first, last):
    size = lax.axis_size("dp")
    up = [(i, i + 1) for i in range(size - 1)]
    down = [(j, i) for i, j in up]
    return (
        lax.ppermute(last, "dp", up),
        lax.ppermute(first, "dp", down),
    )


def after(value, *others):
    return lax.optimization_barrier((value,) + others)[0]


def from_all(values, axis):
    copies = jnp.broadcast_to(values[None], (lax.axis_size(axis),) + values.shape)
    return lax.all_to_all(copies, axis, 0, 0)


def flip_bit(values, axis, bit):
    size = lax.axis_size(axis)
    return lax.ppermute(values, axis, [(i, i ^ (1 << bit)) for i in range(size)])


def bit_of(axis, bit):
    return (lax.axis_index(axis) >> bit) & 1


def gather_pieces(own, order):
    return {0: own} | {1 << bit: flip_bit(own, "fsdp", bit) for bit in order}


def gather_others(have, order, *others):
    reached = {0: have[0]}
    for bit in order:
        for name, v in list(reached.items()):
            far = have.get(name | 1 << bit)
            reached[name | 1 << bit] = far if far is not None else flip_bit(after(v, *others), "fsdp", bit)
    return reached


def per_device(
    inputs,
    out_grad,
    ocean_mask,
    rollout_lengths,
    conv_weight,
    norm_gain,
    norm_bias,
    expand_weight,
    expand_bias,
    project_weight,
    project_bias,
):
    channels, rows, width = inputs.shape[1:]
    n_fs, n_dp = lax.axis_size("fsdp"), lax.axis_size("dp")
    devices = ("dp", "fsdp")
    share = conv_weight.shape[0]
    units = expand_weight.shape[1]
    half = pl.cdiv(units // 128, 2) * 128
    bits = list(range(n_fs.bit_length() - 1))
    core = bit_of("dp", 0)
    x = inputs[0].transpose(1, 0, 2)
    og = out_grad[0].transpose(1, 0, 2)
    block = 5 * GRP

    ratio = expand_bias.shape[0] // share
    small = jnp.concatenate(
        [
            conv_weight.T,
            norm_gain[None],
            norm_bias[None],
            project_bias.astype(F32)[None],
            expand_bias.astype(F32).reshape(ratio, share),
        ],
        axis=0,
    )
    every = from_all(small, "fsdp")
    e_bias = jnp.pad(every[:, TAPS + 3 :].reshape(1, units), ((0, 0), (0, 2 * half - units)))
    x_up, x_dn = halo(x[:REACH], x[-REACH:])

    def columns(weight):
        wide = jnp.pad(weight, ((0, 0), (0, 2 * half - units)))
        return lax.dynamic_slice_in_dim(after(wide, every), (1 - core) * half, half, axis=1)

    eb_own = lax.dynamic_slice_in_dim(e_bias, core * half, half, axis=1)
    eb_peer = lax.dynamic_slice_in_dim(e_bias, (1 - core) * half, half, axis=1)

    sample = lax.axis_index("fsdp")
    length = lax.dynamic_index_in_dim(rollout_lengths, sample, keepdims=False)
    live = jnp.where(sample % ROLLOUT < length, 1.0, 0.0).astype(F32)
    weight = live * ocean_mask.astype(F32)
    m16 = jnp.broadcast_to(weight[:, None, :], (rows, GRP, width))

    we_pieces = gather_pieces(columns(expand_weight), bits)
    wp_pieces = gather_pieces(columns(project_weight), bits[::-1])
    bg, bg_sum = mask_gradient(og, after(m16, small))
    early = [p[1 << b] for p, b in ((we_pieces, bits[0]), (wp_pieces, bits[-1]))]
    we_pieces = gather_others(we_pieces, bits, bg)
    wp_pieces = gather_others(wp_pieces, bits[::-1], bg)

    copies = n_fs * n_dp
    ready = after(m16, bg, *early)
    conv, stats, par = conv_forward(x, x_up, x_dn, every, ready, copies, block)
    index = lax.axis_index("fsdp")
    far = n_fs - 1
    we_pieces[far], wp_pieces[far], index, _ = lax.optimization_barrier(
        (we_pieces[far], wp_pieces[far], index, conv)
    )
    we_peer, wp_peer = join_pieces(index, we_pieces, wp_pieces)
    we_own = flip_bit(we_peer, "dp", 0)
    wp_own = flip_bit(wp_peer, "dp", 0)
    stats = lax.all_to_all(stats, devices, 0, 0)
    act, stat = activate(conv, stats, par)

    groups = [[i for i in range(n_dp) if i % 2 == c] for c in range(2)]
    orders = (bits[::-1], bits)
    flags = jnp.stack([bit_of("fsdp", bit) for bit in bits]).astype(jnp.int32)
    first = half // (2 * TILE) * TILE
    second = half - first

    def piece(order, n):
        return share << len([b for b in order[n + 1 :] if b < order[n]])

    def other_core(grads):
        return [flip_bit(v, "dp", 0) for v in grads]

    def exchanged(pairs, n):
        return [(keep, flip_bit(send, "fsdp", o[n])) for (keep, send), o in zip(pairs, orders, strict=True)]

    def arrived(pairs, *cover):
        came = lax.optimization_barrier((*[came for _, came in pairs], *cover))
        return [(keep, v) for (keep, _), v in zip(pairs, came)]

    def split(pairs, n):
        out = []
        for (kept, came), order in zip(pairs, orders, strict=True):
            total = kept + came.astype(F32)
            keep, send = halves(total, flags[order[n]], piece(order, n))
            out.append((keep, send.astype(BF16)))
        return out

    def sends(pairs):
        return [send for _, send in pairs]

    def rounded(pairs):
        return [(keep + came.astype(F32)).astype(BF16) for keep, came in pairs]

    def over_bands(sums, groups):
        return [lax.psum(v, "dp", axis_index_groups=groups) for v in sums]

    lead = jnp.stack([flags[o[0]] for o in orders])
    pieces = tuple(piece(o, 0) for o in orders)
    q1 = hidden_layer(act, bg, we_peer, wp_peer, eb_peer, 0, first, lead)
    c1 = other_core(q1[2:4])
    q2 = hidden_layer(act, bg, we_peer, wp_peer, after(eb_peer, q1[0]), first, second, lead)
    c2 = other_core(q2[2:4])
    o1 = hidden_layer(act, bg, we_own, wp_own, after(eb_own, q2[0]), 0, first, lead, c1, pieces)
    s1 = exchanged([(o1[2], o1[3]), (o1[4], o1[5])], 0)
    o2 = hidden_layer(act, bg, we_own, wp_own, after(eb_own, o1[0]), first, second, lead, c2, pieces)
    for n in range(1, len(bits)):
        s1 = split(arrived(s1, o2[0]), n)
        last = sends(s1)
        s1 = exchanged(s1, n)
    s2 = exchanged([(o2[2], after(o2[3], *last)), (o2[4], after(o2[5], *last))], 0)

    cuts = ((1, 0, first), (0, 0, first), (1, first, second), (0, first, second))
    parts = (q1, o1, q2, o2)
    hidden = [p[0] for p in parts]
    block_out = block_output((wp_own, wp_peer), hidden, cuts, x, m16, after(par, *last))
    s1 = rounded(arrived(s1, block_out))
    b1 = over_bands(s1, groups)
    for n in range(1, len(bits)):
        s2 = split(arrived(s2, block_out, *s1), n)
        last = sends(s2)
        s2 = exchanged(s2, n)
    ready = after(stat, *s1, *last)
    da, sums = activation_gradient((we_own, we_peer), [p[1] for p in parts], cuts, conv, ready, copies)
    sums = lax.all_to_all(sums, devices, 0, 0)
    s2 = rounded(arrived(s2, da))
    conv_grad, g_first, g_last, totals = conv_gradient(da, conv, m16, sums, stat, after(par, *s2))
    g_up, g_dn = halo(g_first, g_last)
    b2 = over_bands(s2, groups[::-1])
    tap_local = tap_gradient(x, x_up, x_dn, conv_grad, block, share)

    eb_o = jnp.concatenate([o1[-1], o2[-1]], axis=1)
    eb_q = jnp.concatenate([q1[-1], q2[-1]], axis=1)
    eb_all = jnp.concatenate(
        [jnp.where(core == 0, eb_o, eb_q), jnp.where(core == 0, eb_q, eb_o)], axis=1
    )[0, :units]
    local = jnp.concatenate(
        [
            tap_local,
            bg_sum[0, :8].reshape(-1)[:channels].reshape(n_fs, 1, share),
            eb_all.reshape(n_fs, ratio, share),
        ],
        axis=1,
    )
    local = lax.all_to_all(local, "fsdp", 0, 0)
    local = from_all(jnp.sum(local, axis=0), "dp")
    g_up, g_dn, ready, _ = lax.optimization_barrier((g_up, g_dn, par, tap_local))
    input_grad = input_gradient(conv_grad, g_up, g_dn, ready, og, m16, block)
    local = jnp.sum(after(local, input_grad), axis=0)

    pairs = []
    for one, two in zip(b1, b2, strict=True):
        two = after(two, input_grad)
        pairs.append([(one, flip_bit(one, "dp", 0)), (two, flip_bit(two, "dp", 0))])
    starts = ((0, half), (first, half + first))
    project_grad, expand_grad = place_columns(core, pairs, starts, units)

    start = lax.axis_index("fsdp") * share
    totals = totals.reshape(2, -1)
    per_channel = lambda v: v.reshape(-1)[:channels]
    return (
        block_out.transpose(1, 0, 2)[None],
        input_grad.transpose(1, 0, 2)[None],
        local[:TAPS].T,
        lax.dynamic_slice_in_dim(totals[1], start, share),
        lax.dynamic_slice_in_dim(totals[0], start, share),
        expand_grad,
        local[TAPS + 1 :].reshape(-1),
        project_grad,
        local[TAPS],
        per_channel(stat[0:8]),
        per_channel(stat[16:24]),
    )


def solution(mesh):
    rows = P("fsdp", None, "dp", None)
    return jax.shard_map(
        per_device,
        mesh=mesh,
        in_specs=(
            rows,
            rows,
            P("dp", None),
            P(),
            P("fsdp", None),
            P("fsdp"),
            P("fsdp"),
            P("fsdp", None),
            P("fsdp"),
            P("fsdp", None),
            P("fsdp"),
        ),
        out_specs=(
            rows,
            rows,
            P("fsdp", None),
            P("fsdp"),
            P("fsdp"),
            P("fsdp", None),
            P("fsdp"),
            P("fsdp", None),
            P("fsdp"),
            P(),
            P(),
        ),
        check_vma=False,
    )
```

```python
import functools

import jax
import jax.numpy as jnp
from jax import lax
from jax.experimental import pallas as pl
from jax.experimental.pallas import tpu as pltpu
from jax.sharding import PartitionSpec as P

KS = 7
REACH = KS // 2
TAPS = KS * KS
ROLLOUT = 8
EPS = 1e-05
F32, BF16 = jnp.float32, jnp.bfloat16
GRP = 16
TILE = 256
MIB = 2**20
GELU_A = 0.7978845608028654
GELU_B = 0.044715
NT = (((1,), (1,)), ((), ()))
TN = (((0,), (0,)), ((), ()))


def params(limit=60):
    return pltpu.CompilerParams(vmem_limit_bytes=limit * MIB)


def cost(us):
    return pl.CostEstimate(flops=int(us * 1.15e9), bytes_accessed=10**5, transcendentals=0)


def whole(shape):
    zeros = (0,) * len(shape)
    return pl.BlockSpec(shape, lambda *g: zeros, pipeline_mode=pl.Buffered(1))


def roll_lanes(v, shift):
    shift %= v.shape[-1]
    return v if shift == 0 else pltpu.roll(v, shift, v.ndim - 1)


def columns_of(*rows):
    pieces = []
    for k in range(rows[0].shape[0]):
        used = [v[k : k + 1, :] for v in rows]
        block = jnp.concatenate(used + [jnp.zeros((128 - len(rows), 128), F32)], axis=0)
        pieces.append(block.T)
    return jnp.concatenate(pieces, axis=0)


def wide(column):
    return jnp.broadcast_to(column, (column.shape[0], 128))


def copies_of(cols, out_ref):
    copies = out_ref.shape[0]
    for k in range(cols.shape[0] // 128):
        block = cols[k * 128 : (k + 1) * 128, :].T
        for q in range(2):
            row = jnp.broadcast_to(block[q : q + 1, :][None], (copies, 1, 128))
            out_ref[:, 8 * q + k : 8 * q + k + 1, :] = row


def spread_taps(cols, pick_ref, e_ref):
    count = cols.shape[0]
    lane = lax.broadcasted_iota(jnp.int32, (count, 128), 1)
    own = lax.broadcasted_iota(jnp.int32, (count, 128), 0) % GRP == lane % GRP
    high = cols.astype(BF16)
    low = (cols - high.astype(F32)).astype(BF16)
    for h, part in enumerate((high, low)):
        for j in range(KS):
            picked = jnp.dot(part, pick_ref[j], preferred_element_type=F32)
            e_ref[h, j] = jnp.where(own, picked, 0.0).astype(BF16)


def tap_picker():
    tap = lax.broadcasted_iota(jnp.int32, (128, 128), 0)
    lane = lax.broadcasted_iota(jnp.int32, (128, 128), 1)
    inside = lane < KS * GRP
    first = KS * (lane // GRP)
    return [jnp.where((tap == first + j) & inside, 1.0, 0.0).astype(BF16) for j in range(KS)]


def conv_rows(field_ref, taps_ref, s, rows, flip):
    x = field_ref[:, s, :].reshape((rows + 2 * REACH) * GRP, field_ref.shape[-1])
    parts = [taps_ref[h, :, s, :].reshape(KS * GRP, 128)[:, : KS * GRP] for h in range(2)]
    taps = jnp.concatenate(parts, axis=1)
    out = []
    for r in range(rows):
        src = rows - 1 - r if flip else r
        window = x[src * GRP : (src + KS) * GRP]
        sums = jnp.dot(taps, jnp.concatenate([window, window], axis=0), preferred_element_type=F32)
        acc = None
        for j in range(KS):
            moved = roll_lanes(sums[j * GRP : (j + 1) * GRP], j - REACH if flip else REACH - j)
            acc = moved if acc is None else acc + moved
        out.append(acc)
    return out


def conv_kernel(
    x_ref, up_ref, dn_ref, small_ref, m_ref, out_ref, st_ref, par_ref,
    field_ref, cols_ref, e_ref, pick_ref, count_ref, *, share
):
    rows, block = x_ref.shape[0], x_ref.shape[1]
    step = pl.program_id(0)

    @pl.when(step == 0)
    def _():
        for j, pick in enumerate(tap_picker()):
            pick_ref[j] = pick
        count = jnp.sum(jnp.sum(m_ref[...], axis=0), axis=1, keepdims=True)[0:8]
        count_ref[...] = jnp.broadcast_to(count, (8, 128))
        cols_ref[...] = jnp.zeros(cols_ref.shape, F32)
        given, wide = small_ref.shape[1], pl.cdiv(share, 128) * 128
        for f in range(small_ref.shape[0]):
            v = small_ref[f]
            v = jnp.concatenate([v, jnp.zeros((given, wide - share), F32)], axis=1)
            v = jnp.concatenate([v, jnp.zeros((128 - given, wide), F32)], axis=0)
            par_ref[f * share : (f + 1) * share, :] = v.T[:share]

    field_ref[0:REACH] = up_ref[...]
    field_ref[REACH : REACH + rows] = x_ref[...]
    field_ref[REACH + rows :] = dn_ref[...]
    here = pl.multiple_of(step * block, GRP)
    spread_taps(par_ref[pl.ds(here, block), :], pick_ref, e_ref)
    lane = lax.broadcasted_iota(jnp.int32, (GRP, 128), 1)
    inv_n = 1.0 / jnp.maximum(count_ref[0:1, 0:1], 1.0)
    for g in range(block // GRP):
        s = pl.ds(g * GRP, GRP)
        acc = conv_rows(field_ref, e_ref, s, rows, False)
        total = None
        for r in range(rows):
            out_ref[r, s, :] = acc[r]
            v = acc[r] * m_ref[r]
            total = v if total is None else total + v
        mean = jnp.sum(total, axis=-1, keepdims=True) * inv_n
        total = None
        for r in range(rows):
            d = acc[r] - mean
            v = d * d * m_ref[r]
            total = v if total is None else total + v
        dev = jnp.sum(total, axis=-1, keepdims=True)
        at = pl.multiple_of(step * block + g * GRP, GRP)
        cols_ref[pl.ds(at, GRP), :] = jnp.where(lane == 0, mean, dev)

    @pl.when(step == pl.num_programs(0) - 1)
    def _():
        st_ref[...] = jnp.broadcast_to(count_ref[0:1, :][None], st_ref.shape)
        copies_of(cols_ref[...], st_ref)


def conv_forward(x, up, dn, small, m16, copies, block):
    rows, channels, width = x.shape
    n_fs, given, share = small.shape
    padded = pl.cdiv(channels, 128) * 128
    return pl.pallas_call(
        functools.partial(conv_kernel, share=share),
        grid=(channels // block,),
        in_specs=[
            pl.BlockSpec((rows, block, width), lambda g: (0, g, 0)),
            pl.BlockSpec((REACH, block, width), lambda g: (0, g, 0)),
            pl.BlockSpec((REACH, block, width), lambda g: (0, g, 0)),
            whole((n_fs, given, share)),
            whole((rows, GRP, width)),
        ],
        out_specs=[
            pl.BlockSpec((rows, block, width), lambda g: (0, g, 0)),
            pl.BlockSpec((copies, 16, 128), lambda g: (0, 0, 0)),
            pl.BlockSpec((channels, 128), lambda g: (0, 0)),
        ],
        out_shape=[
            jax.ShapeDtypeStruct((rows, channels, width), F32),
            jax.ShapeDtypeStruct((copies, 16, 128), F32),
            jax.ShapeDtypeStruct((channels, 128), F32),
        ],
        scratch_shapes=[
            pltpu.VMEM((rows + 2 * REACH, block, width), BF16),
            pltpu.VMEM((padded, 128), F32),
            pltpu.VMEM((2, KS, block, 128), BF16),
            pltpu.VMEM((KS, 128, 128), BF16),
            pltpu.VMEM((8, 128), F32),
        ],
        compiler_params=params(),
        cost_estimate=cost(0.4),
        name="conv_forward",
    )(x, up, dn, small, m16)


def input_grad_kernel(
    g_ref, up_ref, dn_ref, par_ref, og_ref, m_ref, out_ref, field_ref, e_ref, pick_ref
):
    @pl.when(pl.program_id(0) == 0)
    def _():
        for j, pick in enumerate(tap_picker()):
            pick_ref[j] = pick

    rows, block = g_ref.shape[0], g_ref.shape[1]
    last = rows + 2 * REACH - 1
    for q in range(REACH):
        field_ref[last - q] = up_ref[q]
        field_ref[REACH - 1 - q] = dn_ref[q]
    for q in range(rows):
        field_ref[last - REACH - q] = g_ref[q]
    spread_taps(par_ref[...], pick_ref, e_ref)
    for g in range(block // GRP):
        s = pl.ds(g * GRP, GRP)
        acc = conv_rows(field_ref, e_ref, s, rows, True)
        for r in range(rows):
            out_ref[r, s, :] = og_ref[r, s, :].astype(F32) * m_ref[r] + acc[r]


def input_gradient(grad, up, dn, par, og, m16, block):
    rows, channels, width = grad.shape
    return pl.pallas_call(
        input_grad_kernel,
        grid=(channels // block,),
        in_specs=[
            pl.BlockSpec((rows, block, width), lambda g: (0, g, 0)),
            pl.BlockSpec((REACH, block, width), lambda g: (0, g, 0)),
            pl.BlockSpec((REACH, block, width), lambda g: (0, g, 0)),
            pl.BlockSpec((block, 128), lambda g: (g, 0)),
            pl.BlockSpec((rows, block, width), lambda g: (0, g, 0)),
            whole((rows, GRP, width)),
        ],
        out_specs=pl.BlockSpec((rows, block, width), lambda g: (0, g, 0)),
        out_shape=jax.ShapeDtypeStruct((rows, channels, width), F32),
        scratch_shapes=[
            pltpu.VMEM((rows + 2 * REACH, block, width), BF16),
            pltpu.VMEM((2, KS, block, 128), BF16),
            pltpu.VMEM((KS, 128, 128), BF16),
        ],
        compiler_params=params(),
        cost_estimate=cost(0.32),
        name="input_gradient",
    )(grad, up, dn, par, og, m16)


def tap_grad_kernel(x_ref, up_ref, dn_ref, g_ref, out_ref, field_ref, cols_ref, *, share):
    rows, block, width = x_ref.shape
    field_ref[0:REACH] = up_ref[...]
    field_ref[REACH : REACH + rows] = x_ref[...]
    field_ref[REACH + rows :] = dn_ref[...]
    lane = lax.broadcasted_iota(jnp.int32, (GRP, 128), 1)
    own = lax.broadcasted_iota(jnp.int32, (GRP, 128), 0) == lane % GRP
    for g in range(block // GRP):
        s = pl.ds(g * GRP, GRP)
        x = field_ref[:, s, :].reshape((rows + 2 * REACH) * GRP, width)
        fields = jnp.concatenate([x[r * GRP : (r + KS) * GRP] for r in range(rows)], axis=1)
        grads = []
        for j in range(KS):
            moved = [roll_lanes(g_ref[r, s, :], j - REACH) for r in range(rows)]
            grads.append(jnp.concatenate(moved, axis=1))
        grads = jnp.concatenate(grads, axis=0)
        sums = lax.dot_general(grads, fields, NT, preferred_element_type=F32)
        sums = jnp.concatenate([sums, jnp.zeros((KS * GRP, 128 - KS * GRP), F32)], axis=1)
        out = None
        for j in range(KS):
            acc = jnp.where(own, sums[j * GRP : (j + 1) * GRP], 0.0)
            for k in (8, 4, 2, 1):
                acc = acc + pltpu.roll(acc, 128 - k, 1)
            acc = roll_lanes(acc, j)
            out = acc if out is None else jnp.where(lane % GRP == j, acc, out)
        at = pl.multiple_of(pl.program_id(0) * block + g * GRP, GRP)
        cols_ref[pl.ds(at, GRP), :] = out

    @pl.when(pl.program_id(0) == pl.num_programs(0) - 1)
    def _():
        blocks = [cols_ref[k : k + 128, :].T for k in range(0, cols_ref.shape[0], 128)]
        wide = jnp.concatenate(blocks, axis=1)
        taps = jnp.concatenate([wide[GRP * i : GRP * i + KS] for i in range(KS)], axis=0)
        for f in range(out_ref.shape[0]):
            out_ref[f] = taps[:, f * share : (f + 1) * share]


def tap_gradient(x, up, dn, grad, block, share):
    rows, channels, width = x.shape
    padded = pl.cdiv(channels, 128) * 128
    return pl.pallas_call(
        functools.partial(tap_grad_kernel, share=share),
        grid=(channels // block,),
        in_specs=[
            pl.BlockSpec((rows, block, width), lambda g: (0, g, 0)),
            pl.BlockSpec((REACH, block, width), lambda g: (0, g, 0)),
            pl.BlockSpec((REACH, block, width), lambda g: (0, g, 0)),
            pl.BlockSpec((rows, block, width), lambda g: (0, g, 0)),
        ],
        out_specs=pl.BlockSpec((channels // share, TAPS, share), lambda g: (0, 0, 0)),
        out_shape=jax.ShapeDtypeStruct((channels // share, TAPS, share), F32),
        scratch_shapes=[
            pltpu.VMEM((rows + 2 * REACH, block, width), BF16),
            pltpu.VMEM((padded, 128), F32),
        ],
        compiler_params=params(),
        cost_estimate=cost(6),
        name="tap_gradient",
    )(x, up, dn, grad)


def mask_grad_kernel(og_ref, m_ref, out_ref, sum_ref, cols_ref):
    row = pl.program_id(0)
    channels = og_ref.shape[1]
    v = og_ref[0].astype(F32) * m_ref[0, 0:1]
    out_ref[...] = v.astype(BF16)
    part = v[:, 0:128]
    for k in range(128, v.shape[1], 128):
        part = part + v[:, k : k + 128]

    @pl.when(row == 0)
    def _():
        cols_ref[...] = jnp.zeros(cols_ref.shape, F32)

    cols_ref[0:channels, :] += part

    @pl.when(row == pl.num_programs(0) - 1)
    def _():
        sums = jnp.broadcast_to(jnp.sum(cols_ref[...], axis=1, keepdims=True), cols_ref.shape)
        copies_of(sums, sum_ref)


def mask_gradient(og, m16):
    rows, channels, width = og.shape
    padded = pl.cdiv(channels, 128) * 128
    pixels = rows * width
    return pl.pallas_call(
        mask_grad_kernel,
        grid=(rows,),
        in_specs=[
            pl.BlockSpec((1, channels, width), lambda r: (r, 0, 0)),
            pl.BlockSpec((1, GRP, width), lambda r: (r, 0, 0)),
        ],
        out_specs=[
            pl.BlockSpec((channels, width), lambda r: (0, r)),
            pl.BlockSpec((1, 16, 128), lambda r: (0, 0, 0)),
        ],
        out_shape=[
            jax.ShapeDtypeStruct((channels, pixels), BF16),
            jax.ShapeDtypeStruct((1, 16, 128), F32),
        ],
        scratch_shapes=[pltpu.VMEM((padded, 128), F32)],
        compiler_params=params(),
        cost_estimate=cost(0.11),
        name="mask_gradient",
    )(og, m16)


def activate_kernel(conv_ref, all_ref, par_ref, out_ref, stat_ref, cols_ref):
    channels = conv_ref.shape[1]

    @pl.when(pl.program_id(0) == 0)
    def _():
        means, squares = all_ref[:, 0:8, :], all_ref[:, 8:16, :]
        counts = all_ref[:, 7:8, :]
        count = jnp.sum(counts, axis=0)
        mean = jnp.sum(counts * means, axis=0) / count
        apart = means - mean[None]
        variance = jnp.sum(squares + counts * apart * apart, axis=0) / count
        inv_std = lax.rsqrt(variance + EPS)
        stat_ref[0:8] = mean
        stat_ref[8:16] = inv_std
        stat_ref[16:24] = jnp.sqrt(variance + EPS)
        stat_ref[24:32] = jnp.broadcast_to(count, (8, 128))
        c, p = columns_of(mean[0:7], inv_std[0:7])[:channels], par_ref[...]
        cols_ref[0] = wide(c[:, 0:1])
        cols_ref[1] = wide(c[:, 1:2] * p[:, TAPS : TAPS + 1])
        cols_ref[2] = wide(p[:, TAPS + 1 : TAPS + 2])

    for k in range(0, out_ref.shape[1], 128):
        v = (conv_ref[0, :, k : k + 128] - cols_ref[0]) * cols_ref[1] + cols_ref[2]
        out_ref[:, k : k + 128] = v.astype(BF16)


def activate(conv, stats, par):
    rows, channels, width = conv.shape
    pixels = rows * width
    return pl.pallas_call(
        activate_kernel,
        grid=(rows,),
        in_specs=[
            pl.BlockSpec((1, channels, width), lambda r: (r, 0, 0)),
            whole(stats.shape),
            whole(par.shape),
        ],
        out_specs=[
            pl.BlockSpec((channels, width), lambda r: (0, r)),
            pl.BlockSpec((32, 128), lambda r: (0, 0)),
        ],
        out_shape=[
            jax.ShapeDtypeStruct((channels, pixels), BF16),
            jax.ShapeDtypeStruct((32, 128), F32),
        ],
        scratch_shapes=[pltpu.VMEM((3, channels, 128), F32)],
        compiler_params=params(),
        cost_estimate=cost(0.13),
        name="activate",
    )(conv, stats, par)


def gelu_parts(v):
    v2 = v * v
    t = jnp.tanh(v * (GELU_A + (GELU_A * GELU_B) * v2))
    s = 0.5 * t + 0.5
    h = v * s
    return h, s + h * (1.0 - s) * (2 * GELU_A + (6 * GELU_A * GELU_B) * v2)


def halves(v, mine, piece):
    keep, send = [], []
    for o in range(0, v.shape[0], 2 * piece):
        first, second = v[o : o + piece], v[o + piece : o + 2 * piece]
        keep.append(jnp.where(mine == 0, first, second))
        send.append(jnp.where(mine == 0, second, first))
    return jnp.concatenate(keep, axis=0), jnp.concatenate(send, axis=0)


def hidden_kernel(bits_ref, act_ref, bg_ref, we_ref, wp_ref, eb_ref, *refs, step, pieces):
    if pieces is None:
        h_ref, g_ref, dwp_ref, dwe_ref, ebg_ref = refs
    else:
        other_p, other_e, h_ref, g_ref, keep_p, send_p, keep_e, send_e, ebg_ref = refs
    we, wp, bias = we_ref[...], wp_ref[...], eb_ref[...]
    total = None
    for p in range(0, act_ref.shape[1], step):
        pre = lax.dot_general(act_ref[:, p : p + step], we, TN, preferred_element_type=F32) + bias
        pull = lax.dot_general(bg_ref[:, p : p + step], wp, TN, preferred_element_type=F32)
        h, slope = gelu_parts(pre)
        grad = (pull * slope).astype(BF16)
        h_ref[p : p + step, :] = h.astype(BF16)
        g_ref[p : p + step, :] = grad
        part = jnp.sum(grad.astype(F32), axis=0, keepdims=True)
        total = part if total is None else total + part
    ebg_ref[...] = total
    dwp = jnp.dot(bg_ref[...], h_ref[...], preferred_element_type=F32)
    dwe = jnp.dot(act_ref[...], g_ref[...], preferred_element_type=F32)
    if pieces is None:
        dwp_ref[...] = dwp.astype(BF16)
        dwe_ref[...] = dwe.astype(BF16)
    else:
        keep, send = halves(dwp + other_p[...].astype(F32), bits_ref[0], pieces[0])
        keep_p[...] = keep
        send_p[...] = send.astype(BF16)
        keep, send = halves(dwe + other_e[...].astype(F32), bits_ref[1], pieces[1])
        keep_e[...] = keep
        send_e[...] = send.astype(BF16)


def hidden_layer(act, bg, we, wp, eb, first, units, bits, others=None, pieces=None):
    channels, pixels = act.shape
    off = first // TILE
    column = lambda rows: pl.BlockSpec((rows, TILE), lambda g: (0, g))
    weight = pl.BlockSpec((channels, TILE), lambda g: (0, g + off))
    shape = lambda rows, dtype: jax.ShapeDtypeStruct((rows, units), dtype)
    in_specs = [pl.BlockSpec(memory_space=pltpu.SMEM), whole(act.shape), whole(bg.shape), weight, weight]
    in_specs.append(pl.BlockSpec((1, TILE), lambda g: (0, g + off)))
    operands = [bits, act, bg, we, wp, eb]
    out_specs = [column(pixels), column(pixels)]
    out_shape = [shape(pixels, BF16), shape(pixels, BF16)]
    if others is None:
        out_specs += [column(channels), column(channels)]
        out_shape += [shape(channels, BF16), shape(channels, BF16)]
    else:
        in_specs += [column(channels), column(channels)]
        operands += list(others)
        out_specs += [column(channels // 2)] * 4
        out_shape += [shape(channels // 2, F32), shape(channels // 2, BF16)] * 2
    out_specs.append(column(1))
    out_shape.append(shape(1, F32))
    return pl.pallas_call(
        functools.partial(hidden_kernel, step=128, pieces=pieces),
        grid=(pl.cdiv(units, TILE),),
        in_specs=in_specs,
        out_specs=out_specs,
        out_shape=out_shape,
        compiler_params=params(),
        cost_estimate=cost(0.3),
        name="hidden_layer",
    )(*operands)


def split_kernel(bits_ref, *refs, pieces):
    n = len(pieces)
    for k, piece in enumerate(pieces):
        total = refs[2 * k][...] + refs[2 * k + 1][...].astype(F32)
        keep, send = halves(total, bits_ref[k], piece)
        refs[2 * n + 2 * k][...] = keep
        refs[2 * n + 2 * k + 1][...] = send.astype(BF16)


def split_sums(bits, pairs, pieces):
    rows, cols = pairs[0][0].shape
    shape = lambda dtype: jax.ShapeDtypeStruct((rows // 2, cols), dtype)
    spec = lambda height: pl.BlockSpec((height, cols), lambda: (0, 0))
    out = pl.pallas_call(
        functools.partial(split_kernel, pieces=pieces),
        in_specs=[pl.BlockSpec(memory_space=pltpu.SMEM)] + [spec(rows)] * (2 * len(pairs)),
        out_specs=[spec(rows // 2)] * (2 * len(pairs)),
        out_shape=[shape(F32), shape(BF16)] * len(pairs),
        compiler_params=params(),
        cost_estimate=cost(3),
        name="split_sums",
    )(bits, *[v for pair in pairs for v in pair])
    return [(out[2 * k], out[2 * k + 1]) for k in range(len(pairs))]


def round_kernel(*refs):
    n = len(refs) // 3
    for k in range(n):
        refs[2 * n + k][...] = (refs[2 * k][...] + refs[2 * k + 1][...].astype(F32)).astype(BF16)


def round_sums(pairs):
    spec = pl.BlockSpec(pairs[0][0].shape, lambda: (0, 0))
    return pl.pallas_call(
        round_kernel,
        in_specs=[spec] * (2 * len(pairs)),
        out_specs=[spec] * len(pairs),
        out_shape=[jax.ShapeDtypeStruct(pairs[0][0].shape, BF16)] * len(pairs),
        compiler_params=params(),
        cost_estimate=cost(3),
        name="round_sums",
    )(*[v for pair in pairs for v in pair])


def contract(weights, hiddens):
    total = None
    for (w_ref, first, units), h_ref in zip(weights, hiddens, strict=True):
        part = lax.dot_general(
            w_ref[:, first : first + units], h_ref[...], NT, preferred_element_type=F32
        )
        total = part if total is None else total + part
    return total


def act_grad_kernel(*refs, cuts):
    n = len(cuts)
    w_refs, h_refs = refs[0:2], refs[2 : 2 + n]
    conv_ref, stat_ref, out_ref, sum_ref, cols_ref, acc_ref = refs[2 + n :]
    channels = conv_ref.shape[1]
    row = pl.program_id(0)

    @pl.when(row == 0)
    def _():
        cols_ref[...] = columns_of(stat_ref[0:7], stat_ref[8:15])[: cols_ref.shape[0]]
        acc_ref[...] = jnp.zeros(acc_ref.shape, F32)

    grad = contract([(w_refs[w], first, units) for w, first, units in cuts], h_refs)
    out_ref[0] = grad
    c = cols_ref[0:channels, :]
    scaled = grad * ((conv_ref[0] - c[:, 0:1]) * c[:, 1:2])
    plain, weighted = grad[:, 0:128], scaled[:, 0:128]
    for k in range(128, grad.shape[1], 128):
        plain = plain + grad[:, k : k + 128]
        weighted = weighted + scaled[:, k : k + 128]
    acc_ref[0, 0:channels, :] += plain
    acc_ref[1, 0:channels, :] += weighted

    @pl.when(row == pl.num_programs(0) - 1)
    def _():
        lane = lax.broadcasted_iota(jnp.int32, cols_ref.shape, 1)
        plain = jnp.sum(acc_ref[0], axis=1, keepdims=True)
        weighted = jnp.sum(acc_ref[1], axis=1, keepdims=True)
        sum_ref[...] = jnp.zeros(sum_ref.shape, F32)
        copies_of(jnp.where(lane == 0, plain, weighted), sum_ref)


def activation_gradient(weights, hiddens, cuts, conv, stat, copies):
    rows, channels, width = conv.shape
    padded = pl.cdiv(channels, 128) * 128
    return pl.pallas_call(
        functools.partial(act_grad_kernel, cuts=cuts),
        grid=(rows,),
        in_specs=[whole(w.shape) for w in weights]
        + [pl.BlockSpec((width, h.shape[1]), lambda r: (r, 0)) for h in hiddens]
        + [pl.BlockSpec((1, channels, width), lambda r: (r, 0, 0)), whole(stat.shape)],
        out_specs=[
            pl.BlockSpec((1, channels, width), lambda r: (r, 0, 0)),
            pl.BlockSpec((copies, 16, 128), lambda r: (0, 0, 0)),
        ],
        out_shape=[
            jax.ShapeDtypeStruct((rows, channels, width), F32),
            jax.ShapeDtypeStruct((copies, 16, 128), F32),
        ],
        scratch_shapes=[pltpu.VMEM((padded, 128), F32), pltpu.VMEM((2, padded, 128), F32)],
        compiler_params=params(),
        cost_estimate=cost(0.32),
        name="activation_gradient",
    )(*weights, *hiddens, conv, stat)


def block_out_kernel(*refs, cuts):
    n = len(cuts)
    w_refs, h_refs = refs[0:2], refs[2 : 2 + n]
    x_ref, m_ref, par_ref = refs[2 + n : 5 + n]
    out_ref = refs[-1]
    branch = contract([(w_refs[w], first, units) for w, first, units in cuts], h_refs)
    branch = branch + par_ref[:, TAPS + 2 : TAPS + 3]
    out_ref[0] = ((x_ref[0].astype(F32) + branch) * m_ref[0, 0:1]).astype(BF16)


def block_output(weights, hiddens, cuts, x, m16, par):
    rows, channels, width = x.shape
    return pl.pallas_call(
        functools.partial(block_out_kernel, cuts=cuts),
        grid=(rows,),
        in_specs=[whole(w.shape) for w in weights]
        + [pl.BlockSpec((width, h.shape[1]), lambda r: (r, 0)) for h in hiddens]
        + [
            pl.BlockSpec((1, channels, width), lambda r: (r, 0, 0)),
            pl.BlockSpec((1, GRP, width), lambda r: (r, 0, 0)),
            whole(par.shape),
        ],
        out_specs=pl.BlockSpec((1, channels, width), lambda r: (r, 0, 0)),
        out_shape=jax.ShapeDtypeStruct((rows, channels, width), BF16),
        compiler_params=params(),
        cost_estimate=cost(0.29),
        name="block_output",
    )(*weights, *hiddens, x, m16, par)


def conv_grad_kernel(
    da_ref, conv_ref, m_ref, all_ref, stat_ref, par_ref, out_ref, top_ref, end_ref, sum_ref, cols_ref
):
    row = pl.program_id(0)
    channels = conv_ref.shape[1]

    @pl.when(pl.program_id(0) == 0)
    def _():
        sums = jnp.sum(all_ref[...], axis=0)
        sum_ref[...] = sums
        count = stat_ref[24:32]
        c = columns_of(
            stat_ref[0:7], stat_ref[8:15], (sums[0:8] / count)[0:7], (sums[8:16] / count)[0:7]
        )[:channels]
        factor = c[:, 1:2] * par_ref[:, TAPS : TAPS + 1]
        cols_ref[0] = wide(c[:, 0:1])
        cols_ref[1] = wide(factor)
        cols_ref[2] = wide(factor * c[:, 2:3])
        cols_ref[3] = wide(factor * c[:, 1:2] * c[:, 3:4])

    for k in range(0, out_ref.shape[2], 128):
        s = slice(k, k + 128)
        apart = conv_ref[0, :, s] - cols_ref[0]
        correction = m_ref[0, 0:1, s] * (cols_ref[2] + apart * cols_ref[3])
        out_ref[0, :, s] = (cols_ref[1] * da_ref[0, :, s] - correction).astype(BF16)
    grad = out_ref[0]

    @pl.when(row < REACH)
    def _():
        top_ref[0] = grad

    @pl.when(row >= pl.num_programs(0) - REACH)
    def _():
        end_ref[0] = grad


def conv_gradient(da, conv, m16, sums, stat, par):
    rows, channels, width = conv.shape
    return pl.pallas_call(
        conv_grad_kernel,
        grid=(rows,),
        in_specs=[
            pl.BlockSpec((1, channels, width), lambda r: (r, 0, 0)),
            pl.BlockSpec((1, channels, width), lambda r: (r, 0, 0)),
            pl.BlockSpec((1, GRP, width), lambda r: (r, 0, 0)),
            whole(sums.shape),
            whole(stat.shape),
            whole(par.shape),
        ],
        out_specs=[
            pl.BlockSpec((1, channels, width), lambda r: (r, 0, 0)),
            pl.BlockSpec((1, channels, width), lambda r: (jnp.minimum(r, REACH - 1), 0, 0)),
            pl.BlockSpec((1, channels, width), lambda r: (jnp.maximum(r - rows + REACH, 0), 0, 0)),
            pl.BlockSpec((16, 128), lambda r: (0, 0)),
        ],
        out_shape=[
            jax.ShapeDtypeStruct((rows, channels, width), BF16),
            jax.ShapeDtypeStruct((REACH, channels, width), BF16),
            jax.ShapeDtypeStruct((REACH, channels, width), BF16),
            jax.ShapeDtypeStruct((16, 128), F32),
        ],
        scratch_shapes=[pltpu.VMEM((4, channels, 128), F32)],
        compiler_params=params(),
        cost_estimate=cost(0.2),
        name="conv_gradient",
    )(da, conv, m16, sums, stat, par)


def join_kernel(index_ref, *refs, names, share):
    n = len(names)
    for index in names:

        @pl.when(index_ref[0] == index)
        def _(index=index):
            for w in range(2):
                for k, name in enumerate(names):
                    row = (index ^ name) * share
                    refs[2 * n + w][row : row + share, :] = refs[w * n + k][...]


def join_pieces(index, first, second):
    names = sorted(first)
    share, cols = first[0].shape
    channels = share * len(names)
    if share % 8:
        out = []
        for pieces in (first, second):
            whole_array = jnp.zeros((channels, cols), BF16)
            for name in names:
                start = (index ^ name) * share
                whole_array = lax.dynamic_update_slice_in_dim(whole_array, pieces[name], start, axis=0)
            out.append(whole_array)
        return out
    tile = 2 * TILE
    column = lambda height: pl.BlockSpec((height, tile), lambda g: (0, g))
    return pl.pallas_call(
        functools.partial(join_kernel, names=names, share=share),
        grid=(pl.cdiv(cols, tile),),
        in_specs=[pl.BlockSpec(memory_space=pltpu.SMEM)] + [column(share)] * (2 * len(names)),
        out_specs=[column(channels)] * 2,
        out_shape=[jax.ShapeDtypeStruct((channels, cols), BF16)] * 2,
        compiler_params=params(),
        cost_estimate=cost(0.08),
        name="join_pieces",
    )(index[None], *[first[k] for k in names], *[second[k] for k in names])


def place_kernel(core_ref, *refs, starts):
    n = len(starts)
    for w in range(2):
        out_ref = refs[4 * n + w]
        for k, (low, high) in enumerate(starts):
            mine, other = refs[2 * (w * n + k)][...], refs[2 * (w * n + k) + 1][...]
            mine, other = mine.astype(F32), other.astype(F32)
            for at, v in (
                (low, jnp.where(core_ref[0] == 0, mine, other)),
                (high, jnp.where(core_ref[0] == 0, other, mine)),
            ):
                wide = min(v.shape[1], out_ref.shape[1] - at)
                out_ref[:, at : at + wide] = v[:, :wide]


def place_columns(core, pairs, starts, units):
    share = pairs[0][0][0].shape[0]
    tile = share
    operands = [v for parts in pairs for pair in parts for v in pair]
    return pl.pallas_call(
        functools.partial(place_kernel, starts=starts),
        grid=(share // tile,),
        in_specs=[pl.BlockSpec(memory_space=pltpu.SMEM)]
        + [pl.BlockSpec((tile, v.shape[1]), lambda g: (g, 0)) for v in operands],
        out_specs=[pl.BlockSpec((tile, units), lambda g: (g, 0))] * 2,
        out_shape=[jax.ShapeDtypeStruct((share, units), F32)] * 2,
        compiler_params=params(),
        cost_estimate=cost(0.08),
        name="place_columns",
    )(core[None], *operands)


def halo(first, last):
    size = lax.axis_size("dp")
    up = [(i, i + 1) for i in range(size - 1)]
    down = [(j, i) for i, j in up]
    return (
        lax.ppermute(last, "dp", up),
        lax.ppermute(first, "dp", down),
    )


def after(value, *others):
    return lax.optimization_barrier((value,) + others)[0]


def from_all(values, axis):
    copies = jnp.broadcast_to(values[None], (lax.axis_size(axis),) + values.shape)
    return lax.all_to_all(copies, axis, 0, 0)


def flip_bit(values, axis, bit):
    size = lax.axis_size(axis)
    return lax.ppermute(values, axis, [(i, i ^ (1 << bit)) for i in range(size)])


def bit_of(axis, bit):
    return (lax.axis_index(axis) >> bit) & 1


def gather_pieces(own, order):
    return {0: own} | {1 << bit: flip_bit(own, "fsdp", bit) for bit in order}


def gather_others(have, order, *others):
    reached = {0: have[0]}
    for bit in order:
        for name, v in list(reached.items()):
            far = have.get(name | 1 << bit)
            reached[name | 1 << bit] = far if far is not None else flip_bit(after(v, *others), "fsdp", bit)
    return reached


def per_device(
    inputs,
    out_grad,
    ocean_mask,
    rollout_lengths,
    conv_weight,
    norm_gain,
    norm_bias,
    expand_weight,
    expand_bias,
    project_weight,
    project_bias,
):
    channels, rows, width = inputs.shape[1:]
    n_fs, n_dp = lax.axis_size("fsdp"), lax.axis_size("dp")
    devices = ("dp", "fsdp")
    share = conv_weight.shape[0]
    units = expand_weight.shape[1]
    half = pl.cdiv(units // 128, 2) * 128
    bits = list(range(n_fs.bit_length() - 1))
    core = bit_of("dp", 0)
    x = inputs[0].transpose(1, 0, 2)
    og = out_grad[0].transpose(1, 0, 2)
    block = 5 * GRP

    ratio = expand_bias.shape[0] // share
    x_first, x_last = x[:REACH], x[-REACH:]
    small = jnp.concatenate(
        [
            after(conv_weight, x_first, x_last).T,
            norm_gain[None],
            norm_bias[None],
            project_bias.astype(F32)[None],
            expand_bias.astype(F32).reshape(ratio, share),
        ],
        axis=0,
    )
    every = from_all(small, "fsdp")
    e_bias = jnp.pad(every[:, TAPS + 3 :].reshape(1, units), ((0, 0), (0, 2 * half - units)))
    x_up, x_dn = halo(x_first, x_last)

    def columns(weight):
        weight = after(weight, every)
        high = jnp.pad(weight[:, half:], ((0, 0), (0, 2 * half - units)))
        return jnp.where(core == 0, high, weight[:, :half])

    eb_own = lax.dynamic_slice_in_dim(e_bias, core * half, half, axis=1)
    eb_peer = lax.dynamic_slice_in_dim(e_bias, (1 - core) * half, half, axis=1)

    sample = lax.axis_index("fsdp")
    length = lax.dynamic_index_in_dim(rollout_lengths, sample, keepdims=False)
    live = jnp.where(sample % ROLLOUT < length, 1.0, 0.0).astype(F32)
    weight = live * ocean_mask.astype(F32)
    m16 = jnp.broadcast_to(weight[:, None, :], (rows, GRP, width))

    we_pieces = gather_pieces(columns(expand_weight), bits)
    wp_pieces = gather_pieces(columns(project_weight), bits[::-1])

    copies = n_fs * n_dp
    orders = (bits[::-1], bits)
    flags = jnp.stack([bit_of("fsdp", bit) for bit in bits]).astype(jnp.int32)
    lead = jnp.stack([flags[o[0]] for o in orders])
    bg, bg_sum = mask_gradient(og, after(m16, we_pieces[0], wp_pieces[0]))
    early = [p[1 << b] for p, b in ((we_pieces, bits[0]), (wp_pieces, bits[-1]))]
    we_pieces = gather_others(we_pieces, bits, bg)
    wp_pieces = gather_others(wp_pieces, bits[::-1], bg)
    ready, eb_own, eb_peer, lead, *_ = lax.optimization_barrier(
        (m16, eb_own, eb_peer, lead, bg, *early)
    )
    conv, stats, par = conv_forward(x, x_up, x_dn, every, ready, copies, block)
    stats = lax.all_to_all(stats, devices, 0, 0)
    index = lax.axis_index("fsdp")
    far = n_fs - 1
    we_pieces[far], wp_pieces[far], index, _ = lax.optimization_barrier(
        (we_pieces[far], wp_pieces[far], index, conv)
    )
    we_peer, wp_peer = join_pieces(index, we_pieces, wp_pieces)
    act, stat = activate(conv, after(stats, we_peer, wp_peer), par)
    we_own = flip_bit(after(we_peer, act), "dp", 0)
    wp_own = flip_bit(after(wp_peer, act), "dp", 0)

    groups = [[i for i in range(n_dp) if i % 2 == c] for c in range(2)]
    first = half // (2 * TILE) * TILE
    second = half - first

    def piece(order, n):
        return share << len([b for b in order[n + 1 :] if b < order[n]])

    def other_core(grads):
        return [flip_bit(v, "dp", 0) for v in grads]

    def exchanged(pairs, n):
        return [(keep, flip_bit(send, "fsdp", o[n])) for (keep, send), o in zip(pairs, orders, strict=True)]

    def arrived(pairs, *cover):
        came = lax.optimization_barrier((*[came for _, came in pairs], *cover))
        return [(keep, v) for (keep, _), v in zip(pairs, came)]

    def split(pairs, n):
        taken = [flags[order[n]] for order in orders]
        return split_sums(jnp.stack(taken), pairs, tuple(piece(order, n) for order in orders))

    def sends(pairs):
        return [send for _, send in pairs]

    def over_bands(sums, groups):
        return [lax.psum(v, "dp", axis_index_groups=groups) for v in sums]

    pieces = tuple(piece(o, 0) for o in orders)
    q1 = hidden_layer(act, bg, we_peer, wp_peer, eb_peer, 0, first, lead)
    c1 = other_core(q1[2:4])
    q2 = hidden_layer(act, bg, we_peer, wp_peer, after(eb_peer, q1[0]), first, second, lead)
    c2 = other_core(q2[2:4])
    o1 = hidden_layer(act, bg, we_own, wp_own, after(eb_own, q2[0]), 0, first, lead, c1, pieces)
    s1 = exchanged([(o1[2], o1[3]), (o1[4], o1[5])], 0)
    o2 = hidden_layer(act, bg, we_own, wp_own, after(eb_own, o1[0]), first, second, lead, c2, pieces)
    for n in range(1, len(bits)):
        s1 = split(arrived(s1, o2[0]), n)
        last = sends(s1)
        s1 = exchanged(s1, n)

    s2 = exchanged([(o2[2], after(o2[3], *last)), (o2[4], after(o2[5], *last))], 0)
    cuts = ((1, 0, first), (0, 0, first), (1, first, second), (0, first, second))
    parts = (q1, o1, q2, o2)
    hidden = [p[0] for p in parts]
    da, sums = activation_gradient(
        (we_own, we_peer), [p[1] for p in parts], cuts, conv, after(stat, *last), copies
    )
    sums = lax.all_to_all(sums, devices, 0, 0)
    s1 = round_sums(arrived(s1, da))
    b1 = over_bands(s1, groups)
    for n in range(1, len(bits)):
        s2 = split(arrived(s2, da, *s1), n)
        last = sends(s2)
        s2 = exchanged(s2, n)
    ready = after(sums, *last)
    conv_grad, g_first, g_last, totals = conv_gradient(da, conv, m16, ready, stat, par)
    g_up, g_dn = halo(g_first, g_last)
    s2 = round_sums(arrived(s2, conv_grad))
    tap_local = tap_gradient(x, x_up, x_dn, after(conv_grad, *s2), block, share)
    s2 = list(lax.optimization_barrier((*s2, *b1, tap_local))[:2])
    b2 = over_bands(s2, groups)

    eb_o = jnp.concatenate([o1[-1], o2[-1]], axis=1)
    eb_q = jnp.concatenate([q1[-1], q2[-1]], axis=1)
    eb_all = jnp.concatenate(
        [jnp.where(core == 0, eb_o, eb_q), jnp.where(core == 0, eb_q, eb_o)], axis=1
    )[0, :units]
    local = jnp.concatenate(
        [
            tap_local,
            bg_sum[0, :8].reshape(-1)[:channels].reshape(n_fs, 1, share),
            eb_all.reshape(n_fs, ratio, share),
        ],
        axis=1,
    )
    local = lax.all_to_all(local, "fsdp", 0, 0)
    g_up, g_dn, ready, _ = lax.optimization_barrier((g_up, g_dn, par, tap_local))
    input_grad = input_gradient(conv_grad, g_up, g_dn, ready, og, m16, block)
    local = jnp.sum(after(local, input_grad), axis=0)
    block_out = block_output((wp_own, wp_peer), hidden, cuts, x, m16, after(par, input_grad, local))
    local = jnp.sum(after(from_all(local, "dp"), block_out), axis=0)

    pairs = []
    for one, two in zip(b1, b2, strict=True):
        one, two = after(one, block_out), after(two, block_out)
        pairs.append([(one, flip_bit(one, "dp", 0)), (two, flip_bit(two, "dp", 0))])
    starts = ((0, half), (first, half + first))
    project_grad, expand_grad = place_columns(core, pairs, starts, units)

    start = lax.axis_index("fsdp") * share
    totals = totals.reshape(2, -1)
    per_channel = lambda v: v.reshape(-1)[:channels]
    return (
        block_out.transpose(1, 0, 2)[None],
        input_grad.transpose(1, 0, 2)[None],
        local[:TAPS].T,
        lax.dynamic_slice_in_dim(totals[1], start, share),
        lax.dynamic_slice_in_dim(totals[0], start, share),
        expand_grad,
        local[TAPS + 1 :].reshape(-1),
        project_grad,
        local[TAPS],
        per_channel(stat[0:8]),
        per_channel(stat[16:24]),
    )


def solution(mesh):
    rows = P("fsdp", None, "dp", None)
    return jax.shard_map(
        per_device,
        mesh=mesh,
        in_specs=(
            rows,
            rows,
            P("dp", None),
            P(),
            P("fsdp", None),
            P("fsdp"),
            P("fsdp"),
            P("fsdp", None),
            P("fsdp"),
            P("fsdp", None),
            P("fsdp"),
        ),
        out_specs=(
            rows,
            rows,
            P("fsdp", None),
            P("fsdp"),
            P("fsdp"),
            P("fsdp", None),
            P("fsdp"),
            P("fsdp", None),
            P("fsdp"),
            P(),
            P(),
        ),
        check_vma=False,
    )
```

```python
import functools

import jax
import jax.numpy as jnp
from jax import lax
from jax.experimental import pallas as pl
from jax.experimental.pallas import tpu as pltpu
from jax.sharding import PartitionSpec as P

KS = 7
REACH = KS // 2
TAPS = KS * KS
ROLLOUT = 8
EPS = 1e-05
F32, BF16 = jnp.float32, jnp.bfloat16
GRP = 16
TILE = 256
VMEM = 639 * 2**20 // 10
GELU_A = 0.7978845608028654
GELU_B = 0.044715
NT = (((1,), (1,)), ((), ()))
TN = (((0,), (0,)), ((), ()))


def params():
    return pltpu.CompilerParams(vmem_limit_bytes=VMEM)


def cost(us):
    return pl.CostEstimate(flops=int(us * 1.15e9), bytes_accessed=10**5, transcendentals=0)


def whole(shape):
    zeros = (0,) * len(shape)
    return pl.BlockSpec(shape, lambda *g: zeros, pipeline_mode=pl.Buffered(1))


def roll_lanes(v, shift):
    shift %= v.shape[-1]
    return v if shift == 0 else pltpu.roll(v, shift, v.ndim - 1)


def columns_of(*rows):
    pieces = []
    for k in range(rows[0].shape[0]):
        used = [v[k : k + 1, :] for v in rows]
        block = jnp.concatenate(used + [jnp.zeros((128 - len(rows), 128), F32)], axis=0)
        pieces.append(block.T)
    return jnp.concatenate(pieces, axis=0)


def wide(column):
    return jnp.broadcast_to(column, (column.shape[0], 128))


def copies_of(cols, out_ref):
    copies = out_ref.shape[0]
    for k in range(cols.shape[0] // 128):
        block = cols[k * 128 : (k + 1) * 128, :].T
        for q in range(2):
            row = jnp.broadcast_to(block[q : q + 1, :][None], (copies, 1, 128))
            out_ref[:, 8 * q + k : 8 * q + k + 1, :] = row


def spread_taps(cols, pick_ref, e_ref):
    count = cols.shape[0]
    lane = lax.broadcasted_iota(jnp.int32, (count, 128), 1)
    own = lax.broadcasted_iota(jnp.int32, (count, 128), 0) % GRP == lane % GRP
    high = cols.astype(BF16)
    low = (cols - high.astype(F32)).astype(BF16)
    for h, part in enumerate((high, low)):
        for j in range(KS):
            picked = jnp.dot(part, pick_ref[j], preferred_element_type=F32)
            e_ref[h, j] = jnp.where(own, picked, 0.0).astype(BF16)


def tap_picker():
    tap = lax.broadcasted_iota(jnp.int32, (128, 128), 0)
    lane = lax.broadcasted_iota(jnp.int32, (128, 128), 1)
    inside = lane < KS * GRP
    first = KS * (lane // GRP)
    return [jnp.where((tap == first + j) & inside, 1.0, 0.0).astype(BF16) for j in range(KS)]


def conv_rows(field_ref, taps_ref, s, rows, flip):
    x = field_ref[:, s, :].reshape((rows + 2 * REACH) * GRP, field_ref.shape[-1])
    parts = [taps_ref[h, :, s, :].reshape(KS * GRP, 128)[:, : KS * GRP] for h in range(2)]
    taps = jnp.concatenate(parts, axis=1)
    out = []
    for r in range(rows):
        src = rows - 1 - r if flip else r
        window = x[src * GRP : (src + KS) * GRP]
        sums = jnp.dot(taps, jnp.concatenate([window, window], axis=0), preferred_element_type=F32)
        acc = None
        for j in range(KS):
            moved = roll_lanes(sums[j * GRP : (j + 1) * GRP], j - REACH if flip else REACH - j)
            acc = moved if acc is None else acc + moved
        out.append(acc)
    return out


def conv_kernel(
    x_ref, up_ref, dn_ref, small_ref, m_ref, out_ref, st_ref, par_ref,
    field_ref, cols_ref, e_ref, pick_ref, count_ref, *, share
):
    rows, block = x_ref.shape[0], x_ref.shape[1]
    step = pl.program_id(0)

    @pl.when(step == 0)
    def _():
        for j, pick in enumerate(tap_picker()):
            pick_ref[j] = pick
        count = jnp.sum(jnp.sum(m_ref[...], axis=0), axis=1, keepdims=True)[0:8]
        count_ref[...] = jnp.broadcast_to(count, (8, 128))
        cols_ref[...] = jnp.zeros(cols_ref.shape, F32)
        given, wide = small_ref.shape[1], pl.cdiv(share, 128) * 128
        for f in range(small_ref.shape[0]):
            v = small_ref[f]
            v = jnp.concatenate([v, jnp.zeros((given, wide - share), F32)], axis=1)
            v = jnp.concatenate([v, jnp.zeros((128 - given, wide), F32)], axis=0)
            par_ref[f * share : (f + 1) * share, :] = v.T[:share]

    field_ref[0:REACH] = up_ref[...]
    field_ref[REACH : REACH + rows] = x_ref[...]
    field_ref[REACH + rows :] = dn_ref[...]
    here = pl.multiple_of(step * block, GRP)
    spread_taps(par_ref[pl.ds(here, block), :], pick_ref, e_ref)
    lane = lax.broadcasted_iota(jnp.int32, (GRP, 128), 1)
    inv_n = 1.0 / jnp.maximum(count_ref[0:1, 0:1], 1.0)
    for g in range(block // GRP):
        s = pl.ds(g * GRP, GRP)
        acc = conv_rows(field_ref, e_ref, s, rows, False)
        total = None
        for r in range(rows):
            out_ref[r, s, :] = acc[r]
            v = acc[r] * m_ref[r]
            total = v if total is None else total + v
        mean = jnp.sum(total, axis=-1, keepdims=True) * inv_n
        total = None
        for r in range(rows):
            d = acc[r] - mean
            v = d * d * m_ref[r]
            total = v if total is None else total + v
        dev = jnp.sum(total, axis=-1, keepdims=True)
        at = pl.multiple_of(step * block + g * GRP, GRP)
        cols_ref[pl.ds(at, GRP), :] = jnp.where(lane == 0, mean, dev)

    @pl.when(step == pl.num_programs(0) - 1)
    def _():
        st_ref[...] = jnp.broadcast_to(count_ref[0:1, :][None], st_ref.shape)
        copies_of(cols_ref[...], st_ref)


def conv_forward(x, up, dn, small, m16, copies, block):
    rows, channels, width = x.shape
    n_fs, given, share = small.shape
    padded = pl.cdiv(channels, 128) * 128
    return pl.pallas_call(
        functools.partial(conv_kernel, share=share),
        grid=(channels // block,),
        in_specs=[
            pl.BlockSpec((rows, block, width), lambda g: (0, g, 0)),
            pl.BlockSpec((REACH, block, width), lambda g: (0, g, 0)),
            pl.BlockSpec((REACH, block, width), lambda g: (0, g, 0)),
            whole((n_fs, given, share)),
            whole((rows, GRP, width)),
        ],
        out_specs=[
            pl.BlockSpec((rows, block, width), lambda g: (0, g, 0)),
            pl.BlockSpec((copies, 16, 128), lambda g: (0, 0, 0)),
            pl.BlockSpec((channels, 128), lambda g: (0, 0)),
        ],
        out_shape=[
            jax.ShapeDtypeStruct((rows, channels, width), F32),
            jax.ShapeDtypeStruct((copies, 16, 128), F32),
            jax.ShapeDtypeStruct((channels, 128), F32),
        ],
        scratch_shapes=[
            pltpu.VMEM((rows + 2 * REACH, block, width), BF16),
            pltpu.VMEM((padded, 128), F32),
            pltpu.VMEM((2, KS, block, 128), BF16),
            pltpu.VMEM((KS, 128, 128), BF16),
            pltpu.VMEM((8, 128), F32),
        ],
        compiler_params=params(),
        cost_estimate=cost(0.4),
        name="conv_forward",
    )(x, up, dn, small, m16)


def input_grad_kernel(
    g_ref, up_ref, dn_ref, par_ref, og_ref, m_ref, out_ref, field_ref, e_ref, pick_ref
):
    @pl.when(pl.program_id(0) == 0)
    def _():
        for j, pick in enumerate(tap_picker()):
            pick_ref[j] = pick

    rows, block = g_ref.shape[0], g_ref.shape[1]
    last = rows + 2 * REACH - 1
    for q in range(REACH):
        field_ref[last - q] = up_ref[q]
        field_ref[REACH - 1 - q] = dn_ref[q]
    for q in range(rows):
        field_ref[last - REACH - q] = g_ref[q]
    spread_taps(par_ref[...], pick_ref, e_ref)
    for g in range(block // GRP):
        s = pl.ds(g * GRP, GRP)
        acc = conv_rows(field_ref, e_ref, s, rows, True)
        for r in range(rows):
            out_ref[r, s, :] = og_ref[r, s, :].astype(F32) * m_ref[r] + acc[r]


def input_gradient(grad, up, dn, par, og, m16, block):
    rows, channels, width = grad.shape
    return pl.pallas_call(
        input_grad_kernel,
        grid=(channels // block,),
        in_specs=[
            pl.BlockSpec((rows, block, width), lambda g: (0, g, 0)),
            pl.BlockSpec((REACH, block, width), lambda g: (0, g, 0)),
            pl.BlockSpec((REACH, block, width), lambda g: (0, g, 0)),
            pl.BlockSpec((block, 128), lambda g: (g, 0)),
            pl.BlockSpec((rows, block, width), lambda g: (0, g, 0)),
            whole((rows, GRP, width)),
        ],
        out_specs=pl.BlockSpec((rows, block, width), lambda g: (0, g, 0)),
        out_shape=jax.ShapeDtypeStruct((rows, channels, width), F32),
        scratch_shapes=[
            pltpu.VMEM((rows + 2 * REACH, block, width), BF16),
            pltpu.VMEM((2, KS, block, 128), BF16),
            pltpu.VMEM((KS, 128, 128), BF16),
        ],
        compiler_params=params(),
        cost_estimate=cost(5),
        name="input_gradient",
    )(grad, up, dn, par, og, m16)


def tap_grad_kernel(
    x_ref, up_ref, dn_ref, g_ref, bg_ref, eb_ref, out_ref, field_ref, cols_ref, *, share
):
    rows, block, width = x_ref.shape
    field_ref[0:REACH] = up_ref[...]
    field_ref[REACH : REACH + rows] = x_ref[...]
    field_ref[REACH + rows :] = dn_ref[...]
    lane = lax.broadcasted_iota(jnp.int32, (GRP, 128), 1)
    own = lax.broadcasted_iota(jnp.int32, (GRP, 128), 0) == lane % GRP
    for g in range(block // GRP):
        s = pl.ds(g * GRP, GRP)
        x = field_ref[:, s, :].reshape((rows + 2 * REACH) * GRP, width)
        fields = jnp.concatenate([x[r * GRP : (r + KS) * GRP] for r in range(rows)], axis=1)
        grads = []
        for j in range(KS):
            moved = [roll_lanes(g_ref[r, s, :], j - REACH) for r in range(rows)]
            grads.append(jnp.concatenate(moved, axis=1))
        grads = jnp.concatenate(grads, axis=0)
        sums = lax.dot_general(grads, fields, NT, preferred_element_type=F32)
        sums = jnp.concatenate([sums, jnp.zeros((KS * GRP, 128 - KS * GRP), F32)], axis=1)
        out = None
        for j in range(KS):
            acc = jnp.where(own, sums[j * GRP : (j + 1) * GRP], 0.0)
            for k in (8, 4, 2, 1):
                acc = acc + pltpu.roll(acc, 128 - k, 1)
            acc = roll_lanes(acc, j)
            out = acc if out is None else jnp.where(lane % GRP == j, acc, out)
        at = pl.multiple_of(pl.program_id(0) * block + g * GRP, GRP)
        cols_ref[pl.ds(at, GRP), :] = out

    @pl.when(pl.program_id(0) == pl.num_programs(0) - 1)
    def _():
        blocks = [cols_ref[k : k + 128, :].T for k in range(0, cols_ref.shape[0], 128)]
        wide = jnp.concatenate(blocks, axis=1)
        taps = jnp.concatenate([wide[GRP * i : GRP * i + KS] for i in range(KS)], axis=0)
        band = jnp.concatenate([bg_ref[0, k : k + 1, :] for k in range(wide.shape[1] // 128)], axis=1)
        units = eb_ref[...]
        ratio = out_ref.shape[1] - TAPS - 1
        for f in range(out_ref.shape[0]):
            out_ref[f, 0:TAPS, :] = taps[:, f * share : (f + 1) * share]
            out_ref[f, TAPS : TAPS + 1, :] = band[:, f * share : (f + 1) * share]
            for q in range(ratio):
                at = (f * ratio + q) * share
                out_ref[f, TAPS + 1 + q : TAPS + 2 + q, :] = units[:, at : at + share]


def tap_gradient(x, up, dn, grad, bg_sum, eb_sum, block, share):
    rows, channels, width = x.shape
    padded = pl.cdiv(channels, 128) * 128
    height = TAPS + 1 + eb_sum.shape[1] // channels
    return pl.pallas_call(
        functools.partial(tap_grad_kernel, share=share),
        grid=(channels // block,),
        in_specs=[
            pl.BlockSpec((rows, block, width), lambda g: (0, g, 0)),
            pl.BlockSpec((REACH, block, width), lambda g: (0, g, 0)),
            pl.BlockSpec((REACH, block, width), lambda g: (0, g, 0)),
            pl.BlockSpec((rows, block, width), lambda g: (0, g, 0)),
            whole(bg_sum.shape),
            whole(eb_sum.shape),
        ],
        out_specs=pl.BlockSpec((channels // share, height, share), lambda g: (0, 0, 0)),
        out_shape=jax.ShapeDtypeStruct((channels // share, height, share), F32),
        scratch_shapes=[
            pltpu.VMEM((rows + 2 * REACH, block, width), BF16),
            pltpu.VMEM((padded, 128), F32),
        ],
        compiler_params=params(),
        cost_estimate=cost(15),
        name="tap_gradient",
    )(x, up, dn, grad, bg_sum, eb_sum)


def mask_grad_kernel(og_ref, m_ref, out_ref, sum_ref, cols_ref):
    row = pl.program_id(0)
    channels = og_ref.shape[1]
    v = og_ref[0].astype(F32) * m_ref[0, 0:1]
    out_ref[...] = v.astype(BF16)
    part = v[:, 0:128]
    for k in range(128, v.shape[1], 128):
        part = part + v[:, k : k + 128]

    @pl.when(row == 0)
    def _():
        cols_ref[...] = jnp.zeros(cols_ref.shape, F32)

    cols_ref[0:channels, :] += part

    @pl.when(row == pl.num_programs(0) - 1)
    def _():
        sums = jnp.broadcast_to(jnp.sum(cols_ref[...], axis=1, keepdims=True), cols_ref.shape)
        copies_of(sums, sum_ref)


def mask_gradient(og, m16):
    rows, channels, width = og.shape
    padded = pl.cdiv(channels, 128) * 128
    pixels = rows * width
    return pl.pallas_call(
        mask_grad_kernel,
        grid=(rows,),
        in_specs=[
            pl.BlockSpec((1, channels, width), lambda r: (r, 0, 0)),
            pl.BlockSpec((1, GRP, width), lambda r: (r, 0, 0)),
        ],
        out_specs=[
            pl.BlockSpec((channels, width), lambda r: (0, r)),
            pl.BlockSpec((1, 16, 128), lambda r: (0, 0, 0)),
        ],
        out_shape=[
            jax.ShapeDtypeStruct((channels, pixels), BF16),
            jax.ShapeDtypeStruct((1, 16, 128), F32),
        ],
        scratch_shapes=[pltpu.VMEM((padded, 128), F32)],
        compiler_params=params(),
        cost_estimate=cost(0.1),
        name="mask_gradient",
    )(og, m16)


def activate(conv_ref, all_ref, par_ref, act_ref, stat_ref):
    rows, channels, width = conv_ref.shape
    means, squares = all_ref[:, 0:8, :], all_ref[:, 8:16, :]
    counts = all_ref[:, 7:8, :]
    count = jnp.sum(counts, axis=0)
    mean = jnp.sum(counts * means, axis=0) / count
    apart = means - mean[None]
    variance = jnp.sum(squares + counts * apart * apart, axis=0) / count
    inv_std = lax.rsqrt(variance + EPS)
    stat_ref[0:8] = mean
    stat_ref[8:16] = inv_std
    stat_ref[16:24] = jnp.sqrt(variance + EPS)
    stat_ref[24:32] = jnp.broadcast_to(count, (8, 128))
    c, p = columns_of(mean[0:7], inv_std[0:7])[:channels], par_ref[...]
    centre = wide(c[:, 0:1])
    scale = wide(c[:, 1:2] * p[:, TAPS : TAPS + 1])
    shift = wide(p[:, TAPS + 1 : TAPS + 2])
    for r in range(rows):
        for k in range(0, width, 128):
            v = (conv_ref[r, :, k : k + 128] - centre) * scale + shift
            act_ref[:, r * width + k : r * width + k + 128] = v.astype(BF16)


def gelu_parts(v):
    v2 = v * v
    t = jnp.tanh(v * (GELU_A + (GELU_A * GELU_B) * v2))
    s = 0.5 * t + 0.5
    h = v * s
    return h, s + h * (1.0 - s) * (2 * GELU_A + (6 * GELU_A * GELU_B) * v2)


def halves(v, mine, piece):
    keep, send = [], []
    for o in range(0, v.shape[0], 2 * piece):
        first, second = v[o : o + piece], v[o + piece : o + 2 * piece]
        keep.append(jnp.where(mine == 0, first, second))
        send.append(jnp.where(mine == 0, second, first))
    return jnp.concatenate(keep, axis=0), jnp.concatenate(send, axis=0)


def hidden_kernel(bits_ref, bg_ref, we_ref, wp_ref, eb_ref, *refs, step, pieces, leads):
    if leads:
        conv_ref, all_ref, par_ref, h_ref, g_ref, dwp_ref, dwe_ref, ebg_ref, act_ref, stat_ref = refs

        @pl.when(pl.program_id(0) == 0)
        def _():
            activate(conv_ref, all_ref, par_ref, act_ref, stat_ref)

    else:
        act_ref, refs = refs[0], refs[1:]
    if leads:
        pass
    elif pieces is None:
        h_ref, g_ref, dwp_ref, dwe_ref, ebg_ref = refs
    else:
        other_p, other_e, h_ref, g_ref, keep_p, send_p, keep_e, send_e, ebg_ref = refs
    we, wp, bias = we_ref[...], wp_ref[...], eb_ref[...]
    total = None
    for p in range(0, act_ref.shape[1], step):
        pre = lax.dot_general(act_ref[:, p : p + step], we, TN, preferred_element_type=F32) + bias
        pull = lax.dot_general(bg_ref[:, p : p + step], wp, TN, preferred_element_type=F32)
        h, slope = gelu_parts(pre)
        grad = (pull * slope).astype(BF16)
        h_ref[p : p + step, :] = h.astype(BF16)
        g_ref[p : p + step, :] = grad
        part = jnp.sum(grad.astype(F32), axis=0, keepdims=True)
        total = part if total is None else total + part
    ebg_ref[...] = total
    dwp = jnp.dot(bg_ref[...], h_ref[...], preferred_element_type=F32)
    dwe = jnp.dot(act_ref[...], g_ref[...], preferred_element_type=F32)
    if pieces is None:
        dwp_ref[...] = dwp.astype(BF16)
        dwe_ref[...] = dwe.astype(BF16)
    else:
        keep, send = halves(dwp + other_p[...].astype(F32), bits_ref[0], pieces[0])
        keep_p[...] = keep
        send_p[...] = send.astype(BF16)
        keep, send = halves(dwe + other_e[...].astype(F32), bits_ref[1], pieces[1])
        keep_e[...] = keep
        send_e[...] = send.astype(BF16)


def hidden_layer(act, bg, we, wp, eb, first, units, bits, others=None, pieces=None, front=None):
    channels, pixels = bg.shape
    off = first // TILE
    column = lambda rows: pl.BlockSpec((rows, TILE), lambda g: (0, g))
    weight = pl.BlockSpec((channels, TILE), lambda g: (0, g + off))
    shape = lambda rows, dtype: jax.ShapeDtypeStruct((rows, units), dtype)
    in_specs = [pl.BlockSpec(memory_space=pltpu.SMEM), whole(bg.shape), weight, weight]
    in_specs.append(pl.BlockSpec((1, TILE), lambda g: (0, g + off)))
    made = [act] if front is None else list(front)
    operands = [bits, bg, we, wp, eb] + made
    in_specs += [whole(v.shape) for v in made]
    out_specs = [column(pixels), column(pixels)]
    out_shape = [shape(pixels, BF16), shape(pixels, BF16)]
    if others is None:
        out_specs += [column(channels), column(channels)]
        out_shape += [shape(channels, BF16), shape(channels, BF16)]
    else:
        in_specs += [column(channels), column(channels)]
        operands += list(others)
        out_specs += [column(channels // 2)] * 4
        out_shape += [shape(channels // 2, F32), shape(channels // 2, BF16)] * 2
    out_specs.append(column(1))
    out_shape.append(shape(1, F32))
    if front is not None:
        out_specs += [pl.BlockSpec((channels, pixels), lambda g: (0, 0)), pl.BlockSpec((32, 128), lambda g: (0, 0))]
        out_shape += [jax.ShapeDtypeStruct((channels, pixels), BF16), jax.ShapeDtypeStruct((32, 128), F32)]
    return pl.pallas_call(
        functools.partial(hidden_kernel, step=128, pieces=pieces, leads=front is not None),
        grid=(pl.cdiv(units, TILE),),
        in_specs=in_specs,
        out_specs=out_specs,
        out_shape=out_shape,
        compiler_params=params(),
        cost_estimate=cost(0.3),
        name="hidden_layer",
    )(*operands)


def split_kernel(bits_ref, *refs, pieces):
    n = len(pieces)
    for k, piece in enumerate(pieces):
        total = refs[2 * k][...] + refs[2 * k + 1][...].astype(F32)
        keep, send = halves(total, bits_ref[k], piece)
        refs[2 * n + 2 * k][...] = keep
        refs[2 * n + 2 * k + 1][...] = send.astype(BF16)


def split_sums(bits, pairs, pieces):
    rows, cols = pairs[0][0].shape
    shape = lambda dtype: jax.ShapeDtypeStruct((rows // 2, cols), dtype)
    spec = lambda height: pl.BlockSpec((height, cols), lambda: (0, 0))
    out = pl.pallas_call(
        functools.partial(split_kernel, pieces=pieces),
        in_specs=[pl.BlockSpec(memory_space=pltpu.SMEM)] + [spec(rows)] * (2 * len(pairs)),
        out_specs=[spec(rows // 2)] * (2 * len(pairs)),
        out_shape=[shape(F32), shape(BF16)] * len(pairs),
        compiler_params=params(),
        cost_estimate=cost(3),
        name="split_sums",
    )(bits, *[v for pair in pairs for v in pair])
    return [(out[2 * k], out[2 * k + 1]) for k in range(len(pairs))]


def band_split_kernel(bit_ref, *refs):
    keep_ref, send_ref = refs[-2:]
    rows = keep_ref.shape[1]
    for k in range(keep_ref.shape[0]):
        total = refs[2 * k][...] + refs[2 * k + 1][...].astype(F32)
        low, high = total[:rows], total[total.shape[0] - rows :]
        keep_ref[k] = jnp.where(bit_ref[0] == 0, low, high)
        send_ref[k] = jnp.where(bit_ref[0] == 0, high, low).astype(BF16)


def band_split(bit, pairs):
    share, cols = pairs[0][0].shape
    rows = pl.cdiv(pl.cdiv(share, 2), 8) * 8
    spec = pl.BlockSpec((share, cols), lambda: (0, 0))
    out = pl.BlockSpec((len(pairs), rows, cols), lambda: (0, 0, 0))
    shape = lambda dtype: jax.ShapeDtypeStruct((len(pairs), rows, cols), dtype)
    return pl.pallas_call(
        band_split_kernel,
        in_specs=[pl.BlockSpec(memory_space=pltpu.SMEM)] + [spec] * (2 * len(pairs)),
        out_specs=[out, out],
        out_shape=[shape(F32), shape(BF16)],
        compiler_params=params(),
        cost_estimate=cost(3),
        name="band_split",
    )(bit[None], *[v for pair in pairs for v in pair])


def round_kernel(*refs):
    n = len(refs) // 3
    for k in range(n):
        refs[2 * n + k][...] = (refs[2 * k][...] + refs[2 * k + 1][...].astype(F32)).astype(BF16)


def round_sums(pairs):
    spec = pl.BlockSpec(pairs[0][0].shape, lambda: (0, 0))
    return pl.pallas_call(
        round_kernel,
        in_specs=[spec] * (2 * len(pairs)),
        out_specs=[spec] * len(pairs),
        out_shape=[jax.ShapeDtypeStruct(pairs[0][0].shape, BF16)] * len(pairs),
        compiler_params=params(),
        cost_estimate=cost(3),
        name="round_sums",
    )(*[v for pair in pairs for v in pair])


def contract(weights, hiddens):
    total = None
    for (w_ref, first, units), h_ref in zip(weights, hiddens, strict=True):
        part = lax.dot_general(
            w_ref[:, first : first + units], h_ref[...], NT, preferred_element_type=F32
        )
        total = part if total is None else total + part
    return total


def act_grad_kernel(*refs, cuts):
    n = len(cuts)
    w_refs, h_refs = refs[0:2], refs[2 : 2 + n]
    conv_ref, stat_ref, out_ref, sum_ref, cols_ref, acc_ref = refs[2 + n :]
    channels = conv_ref.shape[1]
    row = pl.program_id(0)

    @pl.when(row == 0)
    def _():
        cols_ref[...] = columns_of(stat_ref[0:7], stat_ref[8:15])[: cols_ref.shape[0]]
        acc_ref[...] = jnp.zeros(acc_ref.shape, F32)

    grad = contract([(w_refs[w], first, units) for w, first, units in cuts], h_refs)
    out_ref[0] = grad
    c = cols_ref[0:channels, :]
    scaled = grad * ((conv_ref[0] - c[:, 0:1]) * c[:, 1:2])
    plain, weighted = grad[:, 0:128], scaled[:, 0:128]
    for k in range(128, grad.shape[1], 128):
        plain = plain + grad[:, k : k + 128]
        weighted = weighted + scaled[:, k : k + 128]
    acc_ref[0, 0:channels, :] += plain
    acc_ref[1, 0:channels, :] += weighted

    @pl.when(row == pl.num_programs(0) - 1)
    def _():
        lane = lax.broadcasted_iota(jnp.int32, cols_ref.shape, 1)
        plain = jnp.sum(acc_ref[0], axis=1, keepdims=True)
        weighted = jnp.sum(acc_ref[1], axis=1, keepdims=True)
        sum_ref[...] = jnp.zeros(sum_ref.shape, F32)
        copies_of(jnp.where(lane == 0, plain, weighted), sum_ref)


def activation_gradient(weights, hiddens, cuts, conv, stat, copies):
    rows, channels, width = conv.shape
    padded = pl.cdiv(channels, 128) * 128
    return pl.pallas_call(
        functools.partial(act_grad_kernel, cuts=cuts),
        grid=(rows,),
        in_specs=[whole(w.shape) for w in weights]
        + [pl.BlockSpec((width, h.shape[1]), lambda r: (r, 0)) for h in hiddens]
        + [pl.BlockSpec((1, channels, width), lambda r: (r, 0, 0)), whole(stat.shape)],
        out_specs=[
            pl.BlockSpec((1, channels, width), lambda r: (r, 0, 0)),
            pl.BlockSpec((copies, 16, 128), lambda r: (0, 0, 0)),
        ],
        out_shape=[
            jax.ShapeDtypeStruct((rows, channels, width), F32),
            jax.ShapeDtypeStruct((copies, 16, 128), F32),
        ],
        scratch_shapes=[pltpu.VMEM((padded, 128), F32), pltpu.VMEM((2, padded, 128), F32)],
        compiler_params=params(),
        cost_estimate=cost(0.3),
        name="activation_gradient",
    )(*weights, *hiddens, conv, stat)


def block_out_kernel(*refs, cuts):
    n = len(cuts)
    w_refs, h_refs = refs[0:2], refs[2 : 2 + n]
    x_ref, m_ref, par_ref = refs[2 + n : 5 + n]
    out_ref = refs[-1]
    branch = contract([(w_refs[w], first, units) for w, first, units in cuts], h_refs)
    branch = branch + par_ref[:, TAPS + 2 : TAPS + 3]
    out_ref[0] = ((x_ref[0].astype(F32) + branch) * m_ref[0, 0:1]).astype(BF16)


def block_output(weights, hiddens, cuts, x, m16, par):
    rows, channels, width = x.shape
    return pl.pallas_call(
        functools.partial(block_out_kernel, cuts=cuts),
        grid=(rows,),
        in_specs=[whole(w.shape) for w in weights]
        + [pl.BlockSpec((width, h.shape[1]), lambda r: (r, 0)) for h in hiddens]
        + [
            pl.BlockSpec((1, channels, width), lambda r: (r, 0, 0)),
            pl.BlockSpec((1, GRP, width), lambda r: (r, 0, 0)),
            whole(par.shape),
        ],
        out_specs=pl.BlockSpec((1, channels, width), lambda r: (r, 0, 0)),
        out_shape=jax.ShapeDtypeStruct((rows, channels, width), BF16),
        compiler_params=params(),
        cost_estimate=cost(5),
        name="block_output",
    )(*weights, *hiddens, x, m16, par)


def conv_grad_kernel(
    da_ref, conv_ref, m_ref, all_ref, stat_ref, par_ref, out_ref, top_ref, end_ref, sum_ref, cols_ref
):
    row = pl.program_id(0)
    channels = conv_ref.shape[1]

    @pl.when(pl.program_id(0) == 0)
    def _():
        sums = jnp.sum(all_ref[...], axis=0)
        sum_ref[...] = sums
        count = stat_ref[24:32]
        c = columns_of(
            stat_ref[0:7], stat_ref[8:15], (sums[0:8] / count)[0:7], (sums[8:16] / count)[0:7]
        )[:channels]
        factor = c[:, 1:2] * par_ref[:, TAPS : TAPS + 1]
        cols_ref[0] = wide(c[:, 0:1])
        cols_ref[1] = wide(factor)
        cols_ref[2] = wide(factor * c[:, 2:3])
        cols_ref[3] = wide(factor * c[:, 1:2] * c[:, 3:4])

    for k in range(0, out_ref.shape[2], 128):
        s = slice(k, k + 128)
        apart = conv_ref[0, :, s] - cols_ref[0]
        correction = m_ref[0, 0:1, s] * (cols_ref[2] + apart * cols_ref[3])
        out_ref[0, :, s] = (cols_ref[1] * da_ref[0, :, s] - correction).astype(BF16)
    grad = out_ref[0]

    @pl.when(row < REACH)
    def _():
        top_ref[0] = grad

    @pl.when(row >= pl.num_programs(0) - REACH)
    def _():
        end_ref[0] = grad


def conv_gradient(da, conv, m16, sums, stat, par):
    rows, channels, width = conv.shape
    return pl.pallas_call(
        conv_grad_kernel,
        grid=(rows,),
        in_specs=[
            pl.BlockSpec((1, channels, width), lambda r: (r, 0, 0)),
            pl.BlockSpec((1, channels, width), lambda r: (r, 0, 0)),
            pl.BlockSpec((1, GRP, width), lambda r: (r, 0, 0)),
            whole(sums.shape),
            whole(stat.shape),
            whole(par.shape),
        ],
        out_specs=[
            pl.BlockSpec((1, channels, width), lambda r: (r, 0, 0)),
            pl.BlockSpec((1, channels, width), lambda r: (jnp.minimum(r, REACH - 1), 0, 0)),
            pl.BlockSpec((1, channels, width), lambda r: (jnp.maximum(r - rows + REACH, 0), 0, 0)),
            pl.BlockSpec((16, 128), lambda r: (0, 0)),
        ],
        out_shape=[
            jax.ShapeDtypeStruct((rows, channels, width), BF16),
            jax.ShapeDtypeStruct((REACH, channels, width), BF16),
            jax.ShapeDtypeStruct((REACH, channels, width), BF16),
            jax.ShapeDtypeStruct((16, 128), F32),
        ],
        scratch_shapes=[pltpu.VMEM((4, channels, 128), F32)],
        compiler_params=params(),
        cost_estimate=cost(0.2),
        name="conv_gradient",
    )(da, conv, m16, sums, stat, par)


def join_kernel(index_ref, *refs, names, share):
    n = len(names)
    for index in names:

        @pl.when(index_ref[0] == index)
        def _(index=index):
            for w in range(2):
                for k, name in enumerate(names):
                    row = (index ^ name) * share
                    refs[2 * n + w][row : row + share, :] = refs[w * n + k][...]


def join_pieces(index, first, second):
    names = sorted(first)
    share, cols = first[0].shape
    channels = share * len(names)
    if share % 8:
        out = []
        for pieces in (first, second):
            whole_array = jnp.zeros((channels, cols), BF16)
            for name in names:
                start = (index ^ name) * share
                whole_array = lax.dynamic_update_slice_in_dim(whole_array, pieces[name], start, axis=0)
            out.append(whole_array)
        return out
    tile = 2 * TILE
    column = lambda height: pl.BlockSpec((height, tile), lambda g: (0, g))
    return pl.pallas_call(
        functools.partial(join_kernel, names=names, share=share),
        grid=(pl.cdiv(cols, tile),),
        in_specs=[pl.BlockSpec(memory_space=pltpu.SMEM)] + [column(share)] * (2 * len(names)),
        out_specs=[column(channels)] * 2,
        out_shape=[jax.ShapeDtypeStruct((channels, cols), BF16)] * 2,
        compiler_params=params(),
        cost_estimate=cost(0.1),
        name="join_pieces",
    )(index[None], *[first[k] for k in names], *[second[k] for k in names])


def place_kernel(flags_ref, *refs, starts):
    outs = refs[-2:]
    core, band = flags_ref[0], flags_ref[1]
    (low, high), (low_half, high_half) = starts

    def put(out_ref, rows, at, v):
        wide = min(v.shape[1], out_ref.shape[1] - at)
        out_ref[rows, at : at + wide] = v[:, :wide]

    for w, out_ref in enumerate(outs):
        share = out_ref.shape[0]
        mine, other = refs[2 * w][...].astype(F32), refs[2 * w + 1][...].astype(F32)
        put(out_ref, slice(0, share), low, jnp.where(core == 0, mine, other))
        put(out_ref, slice(0, share), high, jnp.where(core == 0, other, mine))
        own, far, own_other, far_other = (ref[w].astype(F32) for ref in refs[4:8])
        rows = own.shape[0]
        both = []
        for near, away in ((own, far), (own_other, far_other)):
            first = jnp.where(band == 0, near, away)
            last = jnp.where(band == 0, away, near)[2 * rows - share :]
            both.append((first, last))
        for part, at in ((slice(0, rows), 0), (slice(rows, share), 1)):
            put(out_ref, part, low_half, jnp.where(core == 0, both[0][at], both[1][at]))
            put(out_ref, part, high_half, jnp.where(core == 0, both[1][at], both[0][at]))


def place_columns(flags, whole_parts, half_parts, starts, share, units):
    operands = [v for pair in whole_parts for v in pair] + list(half_parts)
    return pl.pallas_call(
        functools.partial(place_kernel, starts=starts),
        in_specs=[pl.BlockSpec(memory_space=pltpu.SMEM)]
        + [pl.BlockSpec(v.shape, lambda n=v.ndim: (0,) * n) for v in operands],
        out_specs=[pl.BlockSpec((share, units), lambda: (0, 0))] * 2,
        out_shape=[jax.ShapeDtypeStruct((share, units), F32)] * 2,
        compiler_params=params(),
        cost_estimate=cost(0.1),
        name="place_columns",
    )(flags, *operands)


def halo(first, last):
    size = lax.axis_size("dp")
    up = [(i, i + 1) for i in range(size - 1)]
    down = [(j, i) for i, j in up]
    return (
        lax.ppermute(last, "dp", up),
        lax.ppermute(first, "dp", down),
    )


def after(value, *others):
    return lax.optimization_barrier((value,) + others)[0]


def from_all(values, axis):
    copies = jnp.broadcast_to(values[None], (lax.axis_size(axis),) + values.shape)
    return lax.all_to_all(copies, axis, 0, 0)


def flip_bit(values, axis, bit):
    size = lax.axis_size(axis)
    return lax.ppermute(values, axis, [(i, i ^ (1 << bit)) for i in range(size)])


def bit_of(axis, bit):
    return (lax.axis_index(axis) >> bit) & 1


def gather_pieces(own, order):
    return {0: own} | {1 << bit: flip_bit(own, "fsdp", bit) for bit in order}


def gather_others(have, order, *others):
    reached = {0: have[0]}
    for bit in order:
        for name, v in list(reached.items()):
            far = have.get(name | 1 << bit)
            reached[name | 1 << bit] = far if far is not None else flip_bit(after(v, *others), "fsdp", bit)
    return reached


def per_device(
    inputs,
    out_grad,
    ocean_mask,
    rollout_lengths,
    conv_weight,
    norm_gain,
    norm_bias,
    expand_weight,
    expand_bias,
    project_weight,
    project_bias,
):
    channels, rows, width = inputs.shape[1:]
    n_fs, n_dp = lax.axis_size("fsdp"), lax.axis_size("dp")
    devices = ("dp", "fsdp")
    share = conv_weight.shape[0]
    units = expand_weight.shape[1]
    half = pl.cdiv(units // 128, 2) * 128
    bits = list(range(n_fs.bit_length() - 1))
    core = bit_of("dp", 0)
    x = inputs[0].transpose(1, 0, 2)
    og = out_grad[0].transpose(1, 0, 2)
    block = 5 * GRP

    ratio = expand_bias.shape[0] // share
    x_first, x_last = x[:REACH], x[-REACH:]
    small = jnp.concatenate(
        [
            after(conv_weight, x_first, x_last).T,
            norm_gain[None],
            norm_bias[None],
            project_bias.astype(F32)[None],
            expand_bias.astype(F32).reshape(ratio, share),
        ],
        axis=0,
    )
    every = from_all(small, "fsdp")
    e_bias = jnp.pad(every[:, TAPS + 3 :].reshape(1, units), ((0, 0), (0, 2 * half - units)))
    x_up, x_dn = halo(x_first, x_last)

    def columns(weight):
        weight = after(weight, every)
        high = jnp.pad(weight[:, half:], ((0, 0), (0, 2 * half - units)))
        return jnp.where(core == 0, high, weight[:, :half])

    eb_own = lax.dynamic_slice_in_dim(e_bias, core * half, half, axis=1)
    eb_peer = lax.dynamic_slice_in_dim(e_bias, (1 - core) * half, half, axis=1)

    sample = lax.axis_index("fsdp")
    length = lax.dynamic_index_in_dim(rollout_lengths, sample, keepdims=False)
    live = jnp.where(sample % ROLLOUT < length, 1.0, 0.0).astype(F32)
    weight = live * ocean_mask.astype(F32)
    m16 = jnp.broadcast_to(weight[:, None, :], (rows, GRP, width))

    we_pieces = gather_pieces(columns(expand_weight), bits)
    wp_pieces = gather_pieces(columns(project_weight), bits[::-1])

    copies = n_fs * n_dp
    orders = (bits[::-1], bits)
    flags = jnp.stack([bit_of("fsdp", bit) for bit in bits]).astype(jnp.int32)
    lead = jnp.stack([flags[o[0]] for o in orders])
    bg, bg_sum = mask_gradient(og, after(m16, we_pieces[0], wp_pieces[0]))
    early = [p[1 << b] for p, b in ((we_pieces, bits[0]), (wp_pieces, bits[-1]))]
    we_pieces = gather_others(we_pieces, bits, bg)
    wp_pieces = gather_others(wp_pieces, bits[::-1], bg)
    ready, eb_own, eb_peer, lead, *_ = lax.optimization_barrier(
        (m16, eb_own, eb_peer, lead, bg, *early)
    )
    conv, stats, par = conv_forward(x, x_up, x_dn, every, ready, copies, block)
    stats = lax.all_to_all(stats, devices, 0, 0)
    index = lax.axis_index("fsdp")
    far = n_fs - 1
    we_pieces[far], wp_pieces[far], index, _ = lax.optimization_barrier(
        (we_pieces[far], wp_pieces[far], index, conv)
    )
    we_peer, wp_peer = join_pieces(index, we_pieces, wp_pieces)
    groups = [[i for i in range(n_dp) if i % 2 == c] for c in range(2)]
    first = half // (2 * TILE) * TILE
    second = half - first

    def piece(order, n):
        return share << len([b for b in order[n + 1 :] if b < order[n]])

    def other_core(grads):
        return [flip_bit(v, "dp", 0) for v in grads]

    def exchanged(pairs, n):
        return [(keep, flip_bit(send, "fsdp", o[n])) for (keep, send), o in zip(pairs, orders, strict=True)]

    def arrived(pairs, *cover):
        came = lax.optimization_barrier((*[came for _, came in pairs], *cover))
        return [(keep, v) for (keep, _), v in zip(pairs, came)]

    def split(pairs, n):
        taken = [flags[order[n]] for order in orders]
        return split_sums(jnp.stack(taken), pairs, tuple(piece(order, n) for order in orders))

    def sends(pairs):
        return [send for _, send in pairs]

    def over_bands(sums, groups):
        return [lax.psum(v, "dp", axis_index_groups=groups) for v in sums]

    pieces = tuple(piece(o, 0) for o in orders)
    front = (conv, after(stats, we_peer, wp_peer), par)
    *q1, act, stat = hidden_layer(None, bg, we_peer, wp_peer, eb_peer, 0, first, lead, front=front)
    we_own = flip_bit(after(we_peer, act), "dp", 0)
    wp_own = flip_bit(after(wp_peer, act), "dp", 0)
    c1 = other_core(q1[2:4])
    q2 = hidden_layer(act, bg, we_peer, wp_peer, after(eb_peer, q1[0]), first, second, lead)
    c2 = other_core(q2[2:4])
    o1 = hidden_layer(act, bg, we_own, wp_own, after(eb_own, q2[0]), 0, first, lead, c1, pieces)
    s1 = exchanged([(o1[2], o1[3]), (o1[4], o1[5])], 0)
    o2 = hidden_layer(act, bg, we_own, wp_own, after(eb_own, o1[0]), first, second, lead, c2, pieces)
    for n in range(1, len(bits)):
        s1 = split(arrived(s1, o2[0]), n)
        last = sends(s1)
        s1 = exchanged(s1, n)

    s2 = exchanged([(o2[2], after(o2[3], *last)), (o2[4], after(o2[5], *last))], 0)
    eb_o = jnp.concatenate([o1[-1], o2[-1]], axis=1)
    eb_q = jnp.concatenate([q1[-1], q2[-1]], axis=1)
    eb_sum = jnp.concatenate(
        [jnp.where(core == 0, eb_o, eb_q), jnp.where(core == 0, eb_q, eb_o)], axis=1
    )[:, :units]
    cuts = ((1, 0, first), (0, 0, first), (1, first, second), (0, first, second))
    parts = (q1, o1, q2, o2)
    hidden = [p[0] for p in parts]
    da, sums = activation_gradient(
        (we_own, we_peer), [p[1] for p in parts], cuts, conv, after(stat, *last), copies
    )
    sums = lax.all_to_all(sums, devices, 0, 0)
    band = bit_of("dp", 1)
    z_keep, z_send = band_split(band, arrived(s1, da))
    z_came = flip_bit(z_send, "dp", 1)
    for n in range(1, len(bits)):
        s2 = split(arrived(s2, da, z_send), n)
        last = sends(s2)
        s2 = exchanged(s2, n)
    ready = after(sums, *last)
    conv_grad, g_first, g_last, totals = conv_gradient(da, conv, m16, ready, stat, par)
    g_up, g_dn = halo(g_first, g_last)
    z_came, *came = lax.optimization_barrier((z_came, *[v for _, v in s2], conv_grad))
    s2 = round_sums([(keep, v) for (keep, _), v in zip(s2, came)])
    b2 = over_bands(s2, groups)
    half_sum = (z_keep + z_came.astype(F32)).astype(BF16)
    ready = after(conv_grad, half_sum, *s2)
    tap_local = tap_gradient(x, x_up, x_dn, ready, bg_sum, eb_sum, block, share)
    g_up, g_dn, half_sum, _ = lax.optimization_barrier((g_up, g_dn, half_sum, tap_local))
    half_came = flip_bit(half_sum, "dp", 2)
    bands = n_dp.bit_length() - 1

    local = lax.all_to_all(tap_local, "fsdp", 0, 0)
    input_grad = input_gradient(conv_grad, g_up, g_dn, after(par, tap_local), og, m16, block)
    half_came, _ = lax.optimization_barrier((half_came, input_grad))
    half_sum = (half_sum.astype(F32) + half_came.astype(F32)).astype(BF16)
    for bit in range(3, bands):
        half_sum = (half_sum.astype(F32) + flip_bit(half_sum, "dp", bit).astype(F32)).astype(BF16)
    half_far = flip_bit(half_sum, "dp", 1)
    local = jnp.sum(after(local, input_grad), axis=0)
    block_out = block_output((wp_own, wp_peer), hidden, cuts, x, m16, after(par, input_grad, local, half_sum))
    local = jnp.sum(after(from_all(local, "dp"), block_out), axis=0)

    half_far, *b2 = lax.optimization_barrier((half_far, *b2, block_out))
    whole_parts = [(v, flip_bit(v, "dp", 0)) for v in b2[:2]]
    half_parts = (half_sum, half_far, flip_bit(half_sum, "dp", 0), flip_bit(half_far, "dp", 0))
    starts = ((first, half + first), (0, half))
    places = jnp.stack([core, band])
    project_grad, expand_grad = place_columns(places, whole_parts, half_parts, starts, share, units)

    start = lax.axis_index("fsdp") * share
    totals = totals.reshape(2, -1)
    per_channel = lambda v: v.reshape(-1)[:channels]
    return (
        block_out.transpose(1, 0, 2)[None],
        input_grad.transpose(1, 0, 2)[None],
        local[:TAPS].T,
        lax.dynamic_slice_in_dim(totals[1], start, share),
        lax.dynamic_slice_in_dim(totals[0], start, share),
        expand_grad,
        local[TAPS + 1 :].reshape(-1),
        project_grad,
        local[TAPS],
        per_channel(stat[0:8]),
        per_channel(stat[16:24]),
    )


def solution(mesh):
    rows = P("fsdp", None, "dp", None)
    return jax.shard_map(
        per_device,
        mesh=mesh,
        in_specs=(
            rows,
            rows,
            P("dp", None),
            P(),
            P("fsdp", None),
            P("fsdp"),
            P("fsdp"),
            P("fsdp", None),
            P("fsdp"),
            P("fsdp", None),
            P("fsdp"),
        ),
        out_specs=(
            rows,
            rows,
            P("fsdp", None),
            P("fsdp"),
            P("fsdp"),
            P("fsdp", None),
            P("fsdp"),
            P("fsdp", None),
            P("fsdp"),
            P(),
            P(),
        ),
        check_vma=False,
    )
```

```python
import functools

import jax
import jax.numpy as jnp
from jax import lax
from jax.experimental import pallas as pl
from jax.experimental.pallas import tpu as pltpu
from jax.sharding import PartitionSpec as P

KS = 7
REACH = KS // 2
TAPS = KS * KS
ROLLOUT = 8
EPS = 1e-05
F32, BF16 = jnp.float32, jnp.bfloat16
GRP = 16
TILE = 256
VMEM = 639 * 2**20 // 10
GELU_A = 0.7978845608028654
GELU_B = 0.044715
NT = (((1,), (1,)), ((), ()))
TN = (((0,), (0,)), ((), ()))


def params():
    return pltpu.CompilerParams(vmem_limit_bytes=VMEM)


def cost(us):
    return pl.CostEstimate(flops=int(us * 1.15e9), bytes_accessed=10**5, transcendentals=0)


def whole(shape):
    zeros = (0,) * len(shape)
    return pl.BlockSpec(shape, lambda *g: zeros, pipeline_mode=pl.Buffered(1))


def roll_lanes(v, shift):
    shift %= v.shape[-1]
    return v if shift == 0 else pltpu.roll(v, shift, v.ndim - 1)


def columns_of(*rows):
    pieces = []
    for k in range(rows[0].shape[0]):
        used = [v[k : k + 1, :] for v in rows]
        block = jnp.concatenate(used + [jnp.zeros((128 - len(rows), 128), F32)], axis=0)
        pieces.append(block.T)
    return jnp.concatenate(pieces, axis=0)


def wide(column):
    return jnp.broadcast_to(column, (column.shape[0], 128))


def copies_of(cols, out_ref):
    copies = out_ref.shape[0]
    for k in range(cols.shape[0] // 128):
        block = cols[k * 128 : (k + 1) * 128, :].T
        for q in range(2):
            row = jnp.broadcast_to(block[q : q + 1, :][None], (copies, 1, 128))
            out_ref[:, 8 * q + k : 8 * q + k + 1, :] = row


def spread_taps(cols, pick_ref, e_ref):
    count = cols.shape[0]
    lane = lax.broadcasted_iota(jnp.int32, (count, 128), 1)
    own = lax.broadcasted_iota(jnp.int32, (count, 128), 0) % GRP == lane % GRP
    high = cols.astype(BF16)
    low = (cols - high.astype(F32)).astype(BF16)
    for h, part in enumerate((high, low)):
        for j in range(KS):
            picked = jnp.dot(part, pick_ref[j], preferred_element_type=F32)
            e_ref[h, j] = jnp.where(own, picked, 0.0).astype(BF16)


def tap_picker():
    tap = lax.broadcasted_iota(jnp.int32, (128, 128), 0)
    lane = lax.broadcasted_iota(jnp.int32, (128, 128), 1)
    inside = lane < KS * GRP
    first = KS * (lane // GRP)
    return [jnp.where((tap == first + j) & inside, 1.0, 0.0).astype(BF16) for j in range(KS)]


def conv_rows(field_ref, taps_ref, s, rows, flip):
    x = field_ref[:, s, :].reshape((rows + 2 * REACH) * GRP, field_ref.shape[-1])
    parts = [taps_ref[h, :, s, :].reshape(KS * GRP, 128)[:, : KS * GRP] for h in range(2)]
    taps = jnp.concatenate(parts, axis=1)
    out = []
    for r in range(rows):
        src = rows - 1 - r if flip else r
        window = x[src * GRP : (src + KS) * GRP]
        sums = jnp.dot(taps, jnp.concatenate([window, window], axis=0), preferred_element_type=F32)
        acc = None
        for j in range(KS):
            moved = roll_lanes(sums[j * GRP : (j + 1) * GRP], j - REACH if flip else REACH - j)
            acc = moved if acc is None else acc + moved
        out.append(acc)
    return out


def conv_kernel(
    x_ref, up_ref, dn_ref, small_ref, m_ref, out_ref, st_ref, par_ref,
    field_ref, cols_ref, e_ref, pick_ref, count_ref, *, share
):
    rows, block = x_ref.shape[0], x_ref.shape[1]
    step = pl.program_id(0)

    @pl.when(step == 0)
    def _():
        for j, pick in enumerate(tap_picker()):
            pick_ref[j] = pick
        count = jnp.sum(jnp.sum(m_ref[...], axis=0), axis=1, keepdims=True)[0:8]
        count_ref[...] = jnp.broadcast_to(count, (8, 128))
        cols_ref[...] = jnp.zeros(cols_ref.shape, F32)
        given, wide = small_ref.shape[1], pl.cdiv(share, 128) * 128
        for f in range(small_ref.shape[0]):
            v = small_ref[f]
            v = jnp.concatenate([v, jnp.zeros((given, wide - share), F32)], axis=1)
            v = jnp.concatenate([v, jnp.zeros((128 - given, wide), F32)], axis=0)
            par_ref[f * share : (f + 1) * share, :] = v.T[:share]

    field_ref[0:REACH] = up_ref[...]
    field_ref[REACH : REACH + rows] = x_ref[...]
    field_ref[REACH + rows :] = dn_ref[...]
    here = pl.multiple_of(step * block, GRP)
    spread_taps(par_ref[pl.ds(here, block), :], pick_ref, e_ref)
    lane = lax.broadcasted_iota(jnp.int32, (GRP, 128), 1)
    inv_n = 1.0 / jnp.maximum(count_ref[0:1, 0:1], 1.0)
    for g in range(block // GRP):
        s = pl.ds(g * GRP, GRP)
        acc = conv_rows(field_ref, e_ref, s, rows, False)
        total = None
        for r in range(rows):
            out_ref[r, s, :] = acc[r]
            v = acc[r] * m_ref[r]
            total = v if total is None else total + v
        mean = jnp.sum(total, axis=-1, keepdims=True) * inv_n
        total = None
        for r in range(rows):
            d = acc[r] - mean
            v = d * d * m_ref[r]
            total = v if total is None else total + v
        dev = jnp.sum(total, axis=-1, keepdims=True)
        at = pl.multiple_of(step * block + g * GRP, GRP)
        cols_ref[pl.ds(at, GRP), :] = jnp.where(lane == 0, mean, dev)

    @pl.when(step == pl.num_programs(0) - 1)
    def _():
        st_ref[...] = jnp.broadcast_to(count_ref[0:1, :][None], st_ref.shape)
        copies_of(cols_ref[...], st_ref)


def conv_forward(x, up, dn, small, m16, copies, block):
    rows, channels, width = x.shape
    n_fs, given, share = small.shape
    padded = pl.cdiv(channels, 128) * 128
    return pl.pallas_call(
        functools.partial(conv_kernel, share=share),
        grid=(channels // block,),
        in_specs=[
            pl.BlockSpec((rows, block, width), lambda g: (0, g, 0)),
            pl.BlockSpec((REACH, block, width), lambda g: (0, g, 0)),
            pl.BlockSpec((REACH, block, width), lambda g: (0, g, 0)),
            whole((n_fs, given, share)),
            whole((rows, GRP, width)),
        ],
        out_specs=[
            pl.BlockSpec((rows, block, width), lambda g: (0, g, 0)),
            pl.BlockSpec((copies, 16, 128), lambda g: (0, 0, 0)),
            pl.BlockSpec((channels, 128), lambda g: (0, 0)),
        ],
        out_shape=[
            jax.ShapeDtypeStruct((rows, channels, width), F32),
            jax.ShapeDtypeStruct((copies, 16, 128), F32),
            jax.ShapeDtypeStruct((channels, 128), F32),
        ],
        scratch_shapes=[
            pltpu.VMEM((rows + 2 * REACH, block, width), BF16),
            pltpu.VMEM((padded, 128), F32),
            pltpu.VMEM((2, KS, block, 128), BF16),
            pltpu.VMEM((KS, 128, 128), BF16),
            pltpu.VMEM((8, 128), F32),
        ],
        compiler_params=params(),
        cost_estimate=cost(0.4),
        name="conv_forward",
    )(x, up, dn, small, m16)


def input_grad_kernel(
    g_ref, up_ref, dn_ref, par_ref, og_ref, m_ref, out_ref, field_ref, e_ref, pick_ref
):
    @pl.when(pl.program_id(0) == 0)
    def _():
        for j, pick in enumerate(tap_picker()):
            pick_ref[j] = pick

    rows, block = g_ref.shape[0], g_ref.shape[1]
    last = rows + 2 * REACH - 1
    for q in range(REACH):
        field_ref[last - q] = up_ref[q]
        field_ref[REACH - 1 - q] = dn_ref[q]
    for q in range(rows):
        field_ref[last - REACH - q] = g_ref[q]
    spread_taps(par_ref[...], pick_ref, e_ref)
    for g in range(block // GRP):
        s = pl.ds(g * GRP, GRP)
        acc = conv_rows(field_ref, e_ref, s, rows, True)
        for r in range(rows):
            out_ref[r, s, :] = og_ref[r, s, :].astype(F32) * m_ref[r] + acc[r]


def input_gradient(grad, up, dn, par, og, m16, block):
    rows, channels, width = grad.shape
    return pl.pallas_call(
        input_grad_kernel,
        grid=(channels // block,),
        in_specs=[
            pl.BlockSpec((rows, block, width), lambda g: (0, g, 0)),
            pl.BlockSpec((REACH, block, width), lambda g: (0, g, 0)),
            pl.BlockSpec((REACH, block, width), lambda g: (0, g, 0)),
            pl.BlockSpec((block, 128), lambda g: (g, 0)),
            pl.BlockSpec((rows, block, width), lambda g: (0, g, 0)),
            whole((rows, GRP, width)),
        ],
        out_specs=pl.BlockSpec((rows, block, width), lambda g: (0, g, 0)),
        out_shape=jax.ShapeDtypeStruct((rows, channels, width), F32),
        scratch_shapes=[
            pltpu.VMEM((rows + 2 * REACH, block, width), BF16),
            pltpu.VMEM((2, KS, block, 128), BF16),
            pltpu.VMEM((KS, 128, 128), BF16),
        ],
        compiler_params=params(),
        cost_estimate=cost(5),
        name="input_gradient",
    )(grad, up, dn, par, og, m16)


def tap_grad_kernel(
    bits_ref, x_ref, up_ref, dn_ref, g_ref, bg_ref, *refs, share
):
    out_ref, field_ref, cols_ref = refs[-3:]
    rows, block, width = x_ref.shape
    field_ref[0:REACH] = up_ref[...]
    field_ref[REACH : REACH + rows] = x_ref[...]
    field_ref[REACH + rows :] = dn_ref[...]
    lane = lax.broadcasted_iota(jnp.int32, (GRP, 128), 1)
    own = lax.broadcasted_iota(jnp.int32, (GRP, 128), 0) == lane % GRP
    for g in range(block // GRP):
        s = pl.ds(g * GRP, GRP)
        x = field_ref[:, s, :].reshape((rows + 2 * REACH) * GRP, width)
        fields = jnp.concatenate([x[r * GRP : (r + KS) * GRP] for r in range(rows)], axis=1)
        grads = []
        for j in range(KS):
            moved = [roll_lanes(g_ref[r, s, :], j - REACH) for r in range(rows)]
            grads.append(jnp.concatenate(moved, axis=1))
        grads = jnp.concatenate(grads, axis=0)
        sums = lax.dot_general(grads, fields, NT, preferred_element_type=F32)
        sums = jnp.concatenate([sums, jnp.zeros((KS * GRP, 128 - KS * GRP), F32)], axis=1)
        out = None
        for j in range(KS):
            acc = jnp.where(own, sums[j * GRP : (j + 1) * GRP], 0.0)
            for k in (8, 4, 2, 1):
                acc = acc + pltpu.roll(acc, 128 - k, 1)
            acc = roll_lanes(acc, j)
            out = acc if out is None else jnp.where(lane % GRP == j, acc, out)
        at = pl.multiple_of(pl.program_id(0) * block + g * GRP, GRP)
        cols_ref[pl.ds(at, GRP), :] = out

    @pl.when(pl.program_id(0) == pl.num_programs(0) - 1)
    def _():
        blocks = [cols_ref[k : k + 128, :].T for k in range(0, cols_ref.shape[0], 128)]
        wide = jnp.concatenate(blocks, axis=1)
        taps = jnp.concatenate([wide[GRP * i : GRP * i + KS] for i in range(KS)], axis=0)
        band = jnp.concatenate([bg_ref[0, k : k + 1, :] for k in range(wide.shape[1] // 128)], axis=1)
        own, peer = (jnp.concatenate([refs[q][...], refs[q + 1][...]], axis=1) for q in (0, 2))
        core = bits_ref[bits_ref.shape[0] - 2]
        units = jnp.concatenate(
            [jnp.where(core == 0, own, peer), jnp.where(core == 0, peer, own)], axis=1
        )
        ratio = out_ref.shape[1] - TAPS - 1
        for f in range(out_ref.shape[0]):
            out_ref[f, 0:TAPS, :] = taps[:, f * share : (f + 1) * share]
            out_ref[f, TAPS : TAPS + 1, :] = band[:, f * share : (f + 1) * share]
            for q in range(ratio):
                at = (f * ratio + q) * share
                out_ref[f, TAPS + 1 + q : TAPS + 2 + q, :] = units[:, at : at + share]


def tap_gradient(bits, x, up, dn, grad, bg_sum, eb_sums, units, block, share):
    rows, channels, width = x.shape
    padded = pl.cdiv(channels, 128) * 128
    height = TAPS + 1 + units // channels
    return pl.pallas_call(
        functools.partial(tap_grad_kernel, share=share),
        grid=(channels // block,),
        in_specs=[
            pl.BlockSpec(memory_space=pltpu.SMEM),
            pl.BlockSpec((rows, block, width), lambda g: (0, g, 0)),
            pl.BlockSpec((REACH, block, width), lambda g: (0, g, 0)),
            pl.BlockSpec((REACH, block, width), lambda g: (0, g, 0)),
            pl.BlockSpec((rows, block, width), lambda g: (0, g, 0)),
            whole(bg_sum.shape),
        ]
        + [whole(v.shape) for v in eb_sums],
        out_specs=pl.BlockSpec((channels // share, height, share), lambda g: (0, 0, 0)),
        out_shape=jax.ShapeDtypeStruct((channels // share, height, share), F32),
        scratch_shapes=[
            pltpu.VMEM((rows + 2 * REACH, block, width), BF16),
            pltpu.VMEM((padded, 128), F32),
        ],
        compiler_params=params(),
        cost_estimate=cost(15),
        name="tap_gradient",
    )(bits, x, up, dn, grad, bg_sum, *eb_sums)


def mask_grad_kernel(og_ref, m_ref, out_ref, sum_ref, cols_ref):
    row = pl.program_id(0)
    channels = og_ref.shape[1]
    v = og_ref[0].astype(F32) * m_ref[0, 0:1]
    out_ref[...] = v.astype(BF16)
    part = v[:, 0:128]
    for k in range(128, v.shape[1], 128):
        part = part + v[:, k : k + 128]

    @pl.when(row == 0)
    def _():
        cols_ref[...] = jnp.zeros(cols_ref.shape, F32)

    cols_ref[0:channels, :] += part

    @pl.when(row == pl.num_programs(0) - 1)
    def _():
        sums = jnp.broadcast_to(jnp.sum(cols_ref[...], axis=1, keepdims=True), cols_ref.shape)
        copies_of(sums, sum_ref)


def mask_gradient(og, m16):
    rows, channels, width = og.shape
    padded = pl.cdiv(channels, 128) * 128
    pixels = rows * width
    return pl.pallas_call(
        mask_grad_kernel,
        grid=(rows,),
        in_specs=[
            pl.BlockSpec((1, channels, width), lambda r: (r, 0, 0)),
            pl.BlockSpec((1, GRP, width), lambda r: (r, 0, 0)),
        ],
        out_specs=[
            pl.BlockSpec((channels, width), lambda r: (0, r)),
            pl.BlockSpec((1, 16, 128), lambda r: (0, 0, 0)),
        ],
        out_shape=[
            jax.ShapeDtypeStruct((channels, pixels), BF16),
            jax.ShapeDtypeStruct((1, 16, 128), F32),
        ],
        scratch_shapes=[pltpu.VMEM((padded, 128), F32)],
        compiler_params=params(),
        cost_estimate=cost(0.1),
        name="mask_gradient",
    )(og, m16)


def activate(conv_ref, all_ref, par_ref, act_ref, stat_ref):
    rows, channels, width = conv_ref.shape
    means, squares = all_ref[:, 0:8, :], all_ref[:, 8:16, :]
    counts = all_ref[:, 7:8, :]
    count = jnp.sum(counts, axis=0)
    mean = jnp.sum(counts * means, axis=0) / count
    apart = means - mean[None]
    variance = jnp.sum(squares + counts * apart * apart, axis=0) / count
    inv_std = lax.rsqrt(variance + EPS)
    stat_ref[0:8] = mean
    stat_ref[8:16] = inv_std
    stat_ref[16:24] = jnp.sqrt(variance + EPS)
    stat_ref[24:32] = jnp.broadcast_to(count, (8, 128))
    c, p = columns_of(mean[0:7], inv_std[0:7])[:channels], par_ref[...]
    centre = wide(c[:, 0:1])
    scale = wide(c[:, 1:2] * p[:, TAPS : TAPS + 1])
    shift = wide(p[:, TAPS + 1 : TAPS + 2])
    for r in range(rows):
        for k in range(0, width, 128):
            v = (conv_ref[r, :, k : k + 128] - centre) * scale + shift
            act_ref[:, r * width + k : r * width + k + 128] = v.astype(BF16)


def gelu_parts(v):
    v2 = v * v
    t = jnp.tanh(v * (GELU_A + (GELU_A * GELU_B) * v2))
    s = 0.5 * t + 0.5
    h = v * s
    return h, s + h * (1.0 - s) * (2 * GELU_A + (6 * GELU_A * GELU_B) * v2)


def halves(v, mine, piece):
    keep, send = [], []
    for o in range(0, v.shape[0], 2 * piece):
        first, second = v[o : o + piece], v[o + piece : o + 2 * piece]
        keep.append(jnp.where(mine == 0, first, second))
        send.append(jnp.where(mine == 0, second, first))
    return jnp.concatenate(keep, axis=0), jnp.concatenate(send, axis=0)


def hidden_kernel(bits_ref, bg_ref, we_ref, wp_ref, eb_ref, *refs, step, pieces, slots, leads):
    if leads:
        conv_ref, all_ref, par_ref, h_ref, g_ref, dwp_ref, dwe_ref, ebg_ref, act_ref, stat_ref = refs

        @pl.when(pl.program_id(0) == 0)
        def _():
            activate(conv_ref, all_ref, par_ref, act_ref, stat_ref)

    else:
        act_ref, refs = refs[0], refs[1:]
    if leads:
        pass
    elif pieces is None:
        h_ref, g_ref, dwp_ref, dwe_ref, ebg_ref = refs
    else:
        other_p, other_e, h_ref, g_ref, keep_p, send_p, keep_e, send_e, ebg_ref = refs
    we, wp, bias = we_ref[...], wp_ref[...], eb_ref[...]
    total = None
    for p in range(0, act_ref.shape[1], step):
        pre = lax.dot_general(act_ref[:, p : p + step], we, TN, preferred_element_type=F32) + bias
        pull = lax.dot_general(bg_ref[:, p : p + step], wp, TN, preferred_element_type=F32)
        h, slope = gelu_parts(pre)
        grad = (pull * slope).astype(BF16)
        h_ref[p : p + step, :] = h.astype(BF16)
        g_ref[p : p + step, :] = grad
        part = jnp.sum(grad.astype(F32), axis=0, keepdims=True)
        total = part if total is None else total + part
    ebg_ref[...] = total
    dwp = jnp.dot(bg_ref[...], h_ref[...], preferred_element_type=F32)
    dwe = jnp.dot(act_ref[...], g_ref[...], preferred_element_type=F32)
    if pieces is None:
        dwp_ref[...] = dwp.astype(BF16)
        dwe_ref[...] = dwe.astype(BF16)
    else:
        keep, send = halves(dwp + other_p[...].astype(F32), bits_ref[slots[0]], pieces[0])
        keep_p[...] = keep
        send_p[...] = send.astype(BF16)
        keep, send = halves(dwe + other_e[...].astype(F32), bits_ref[slots[1]], pieces[1])
        keep_e[...] = keep
        send_e[...] = send.astype(BF16)


def hidden_layer(act, bg, we, wp, eb, first, units, bits, others=None, pieces=None, slots=None, front=None):
    channels, pixels = bg.shape
    off = first // TILE
    column = lambda rows: pl.BlockSpec((rows, TILE), lambda g: (0, g))
    weight = pl.BlockSpec((channels, TILE), lambda g: (0, g + off))
    shape = lambda rows, dtype: jax.ShapeDtypeStruct((rows, units), dtype)
    in_specs = [pl.BlockSpec(memory_space=pltpu.SMEM), whole(bg.shape), weight, weight]
    in_specs.append(pl.BlockSpec((1, TILE), lambda g: (0, g + off)))
    made = [act] if front is None else list(front)
    operands = [bits, bg, we, wp, eb] + made
    in_specs += [whole(v.shape) for v in made]
    out_specs = [column(pixels), column(pixels)]
    out_shape = [shape(pixels, BF16), shape(pixels, BF16)]
    if others is None:
        out_specs += [column(channels), column(channels)]
        out_shape += [shape(channels, BF16), shape(channels, BF16)]
    else:
        in_specs += [column(channels), column(channels)]
        operands += list(others)
        out_specs += [column(channels // 2)] * 4
        out_shape += [shape(channels // 2, F32), shape(channels // 2, BF16)] * 2
    out_specs.append(column(1))
    out_shape.append(shape(1, F32))
    if front is not None:
        out_specs += [pl.BlockSpec((channels, pixels), lambda g: (0, 0)), pl.BlockSpec((32, 128), lambda g: (0, 0))]
        out_shape += [jax.ShapeDtypeStruct((channels, pixels), BF16), jax.ShapeDtypeStruct((32, 128), F32)]
    return pl.pallas_call(
        functools.partial(hidden_kernel, step=128, pieces=pieces, slots=slots, leads=front is not None),
        grid=(pl.cdiv(units, TILE),),
        in_specs=in_specs,
        out_specs=out_specs,
        out_shape=out_shape,
        compiler_params=params(),
        cost_estimate=cost(0.3),
        name="hidden_layer",
    )(*operands)


def split_kernel(bits_ref, *refs, pieces, slots):
    n = len(pieces)
    for k, (piece, slot) in enumerate(zip(pieces, slots, strict=True)):
        total = refs[2 * k][...] + refs[2 * k + 1][...].astype(F32)
        keep, send = halves(total, bits_ref[slot], piece)
        refs[2 * n + 2 * k][...] = keep
        refs[2 * n + 2 * k + 1][...] = send.astype(BF16)


def split_sums(bits, pairs, pieces, slots):
    rows, cols = pairs[0][0].shape
    shape = lambda dtype: jax.ShapeDtypeStruct((rows // 2, cols), dtype)
    spec = lambda height: pl.BlockSpec((height, cols), lambda: (0, 0))
    out = pl.pallas_call(
        functools.partial(split_kernel, pieces=pieces, slots=slots),
        in_specs=[pl.BlockSpec(memory_space=pltpu.SMEM)] + [spec(rows)] * (2 * len(pairs)),
        out_specs=[spec(rows // 2)] * (2 * len(pairs)),
        out_shape=[shape(F32), shape(BF16)] * len(pairs),
        compiler_params=params(),
        cost_estimate=cost(3),
        name="split_sums",
    )(bits, *[v for pair in pairs for v in pair])
    return [(out[2 * k], out[2 * k + 1]) for k in range(len(pairs))]


def band_split_kernel(bits_ref, *refs):
    keep_ref, send_ref = refs[-2:]
    rows = keep_ref.shape[1]
    band = bits_ref[bits_ref.shape[0] - 1]
    for k in range(keep_ref.shape[0]):
        total = refs[2 * k][...] + refs[2 * k + 1][...].astype(F32)
        low, high = total[:rows], total[total.shape[0] - rows :]
        keep_ref[k] = jnp.where(band == 0, low, high)
        send_ref[k] = jnp.where(band == 0, high, low).astype(BF16)


def band_split(bits, pairs):
    share, cols = pairs[0][0].shape
    rows = pl.cdiv(pl.cdiv(share, 2), 8) * 8
    spec = pl.BlockSpec((share, cols), lambda: (0, 0))
    out = pl.BlockSpec((len(pairs), rows, cols), lambda: (0, 0, 0))
    shape = lambda dtype: jax.ShapeDtypeStruct((len(pairs), rows, cols), dtype)
    return pl.pallas_call(
        band_split_kernel,
        in_specs=[pl.BlockSpec(memory_space=pltpu.SMEM)] + [spec] * (2 * len(pairs)),
        out_specs=[out, out],
        out_shape=[shape(F32), shape(BF16)],
        compiler_params=params(),
        cost_estimate=cost(3),
        name="band_split",
    )(bits, *[v for pair in pairs for v in pair])


def round_kernel(*refs):
    n = len(refs) // 3
    for k in range(n):
        total = refs[2 * k][...].astype(F32) + refs[2 * k + 1][...].astype(F32)
        refs[2 * n + k][...] = total.astype(BF16)


def round_sums(pairs):
    shape = pairs[0][0].shape
    spec = pl.BlockSpec(shape, lambda: (0,) * len(shape))
    return pl.pallas_call(
        round_kernel,
        in_specs=[spec] * (2 * len(pairs)),
        out_specs=[spec] * len(pairs),
        out_shape=[jax.ShapeDtypeStruct(pairs[0][0].shape, BF16)] * len(pairs),
        compiler_params=params(),
        cost_estimate=cost(3),
        name="round_sums",
    )(*[v for pair in pairs for v in pair])


def contract(weights, hiddens):
    total = None
    for (w_ref, first, units), h_ref in zip(weights, hiddens, strict=True):
        part = lax.dot_general(
            w_ref[:, first : first + units], h_ref[...], NT, preferred_element_type=F32
        )
        total = part if total is None else total + part
    return total


def act_grad_kernel(*refs, cuts):
    n = len(cuts)
    w_refs, h_refs = refs[0:2], refs[2 : 2 + n]
    conv_ref, stat_ref, out_ref, sum_ref, cols_ref, acc_ref = refs[2 + n :]
    channels = conv_ref.shape[1]
    row = pl.program_id(0)

    @pl.when(row == 0)
    def _():
        cols_ref[...] = columns_of(stat_ref[0:7], stat_ref[8:15])[: cols_ref.shape[0]]
        acc_ref[...] = jnp.zeros(acc_ref.shape, F32)

    grad = contract([(w_refs[w], first, units) for w, first, units in cuts], h_refs)
    out_ref[0] = grad
    c = cols_ref[0:channels, :]
    scaled = grad * ((conv_ref[0] - c[:, 0:1]) * c[:, 1:2])
    plain, weighted = grad[:, 0:128], scaled[:, 0:128]
    for k in range(128, grad.shape[1], 128):
        plain = plain + grad[:, k : k + 128]
        weighted = weighted + scaled[:, k : k + 128]
    acc_ref[0, 0:channels, :] += plain
    acc_ref[1, 0:channels, :] += weighted

    @pl.when(row == pl.num_programs(0) - 1)
    def _():
        lane = lax.broadcasted_iota(jnp.int32, cols_ref.shape, 1)
        plain = jnp.sum(acc_ref[0], axis=1, keepdims=True)
        weighted = jnp.sum(acc_ref[1], axis=1, keepdims=True)
        sum_ref[...] = jnp.zeros(sum_ref.shape, F32)
        copies_of(jnp.where(lane == 0, plain, weighted), sum_ref)


def activation_gradient(weights, hiddens, cuts, conv, stat, copies):
    rows, channels, width = conv.shape
    padded = pl.cdiv(channels, 128) * 128
    return pl.pallas_call(
        functools.partial(act_grad_kernel, cuts=cuts),
        grid=(rows,),
        in_specs=[whole(w.shape) for w in weights]
        + [pl.BlockSpec((width, h.shape[1]), lambda r: (r, 0)) for h in hiddens]
        + [pl.BlockSpec((1, channels, width), lambda r: (r, 0, 0)), whole(stat.shape)],
        out_specs=[
            pl.BlockSpec((1, channels, width), lambda r: (r, 0, 0)),
            pl.BlockSpec((copies, 16, 128), lambda r: (0, 0, 0)),
        ],
        out_shape=[
            jax.ShapeDtypeStruct((rows, channels, width), F32),
            jax.ShapeDtypeStruct((copies, 16, 128), F32),
        ],
        scratch_shapes=[pltpu.VMEM((padded, 128), F32), pltpu.VMEM((2, padded, 128), F32)],
        compiler_params=params(),
        cost_estimate=cost(0.3),
        name="activation_gradient",
    )(*weights, *hiddens, conv, stat)


def block_out_kernel(*refs, cuts):
    n = len(cuts)
    w_refs, h_refs = refs[0:2], refs[2 : 2 + n]
    x_ref, m_ref, par_ref = refs[2 + n : 5 + n]
    out_ref = refs[-1]
    branch = contract([(w_refs[w], first, units) for w, first, units in cuts], h_refs)
    branch = branch + par_ref[:, TAPS + 2 : TAPS + 3]
    out_ref[0] = ((x_ref[0].astype(F32) + branch) * m_ref[0, 0:1]).astype(BF16)


def block_output(weights, hiddens, cuts, x, m16, par):
    rows, channels, width = x.shape
    return pl.pallas_call(
        functools.partial(block_out_kernel, cuts=cuts),
        grid=(rows,),
        in_specs=[whole(w.shape) for w in weights]
        + [pl.BlockSpec((width, h.shape[1]), lambda r: (r, 0)) for h in hiddens]
        + [
            pl.BlockSpec((1, channels, width), lambda r: (r, 0, 0)),
            pl.BlockSpec((1, GRP, width), lambda r: (r, 0, 0)),
            whole(par.shape),
        ],
        out_specs=pl.BlockSpec((1, channels, width), lambda r: (r, 0, 0)),
        out_shape=jax.ShapeDtypeStruct((rows, channels, width), BF16),
        compiler_params=params(),
        cost_estimate=cost(5),
        name="block_output",
    )(*weights, *hiddens, x, m16, par)


def conv_grad_kernel(
    da_ref, conv_ref, m_ref, all_ref, stat_ref, par_ref, out_ref, top_ref, end_ref, sum_ref, cols_ref
):
    row = pl.program_id(0)
    channels = conv_ref.shape[1]

    @pl.when(pl.program_id(0) == 0)
    def _():
        sums = jnp.sum(all_ref[...], axis=0)
        sum_ref[...] = sums
        count = stat_ref[24:32]
        c = columns_of(
            stat_ref[0:7], stat_ref[8:15], (sums[0:8] / count)[0:7], (sums[8:16] / count)[0:7]
        )[:channels]
        factor = c[:, 1:2] * par_ref[:, TAPS : TAPS + 1]
        cols_ref[0] = wide(c[:, 0:1])
        cols_ref[1] = wide(factor)
        cols_ref[2] = wide(factor * c[:, 2:3])
        cols_ref[3] = wide(factor * c[:, 1:2] * c[:, 3:4])

    for k in range(0, out_ref.shape[2], 128):
        s = slice(k, k + 128)
        apart = conv_ref[0, :, s] - cols_ref[0]
        correction = m_ref[0, 0:1, s] * (cols_ref[2] + apart * cols_ref[3])
        out_ref[0, :, s] = (cols_ref[1] * da_ref[0, :, s] - correction).astype(BF16)
    grad = out_ref[0]

    @pl.when(row < REACH)
    def _():
        top_ref[0] = grad

    @pl.when(row >= pl.num_programs(0) - REACH)
    def _():
        end_ref[0] = grad


def conv_gradient(da, conv, m16, sums, stat, par):
    rows, channels, width = conv.shape
    return pl.pallas_call(
        conv_grad_kernel,
        grid=(rows,),
        in_specs=[
            pl.BlockSpec((1, channels, width), lambda r: (r, 0, 0)),
            pl.BlockSpec((1, channels, width), lambda r: (r, 0, 0)),
            pl.BlockSpec((1, GRP, width), lambda r: (r, 0, 0)),
            whole(sums.shape),
            whole(stat.shape),
            whole(par.shape),
        ],
        out_specs=[
            pl.BlockSpec((1, channels, width), lambda r: (r, 0, 0)),
            pl.BlockSpec((1, channels, width), lambda r: (jnp.minimum(r, REACH - 1), 0, 0)),
            pl.BlockSpec((1, channels, width), lambda r: (jnp.maximum(r - rows + REACH, 0), 0, 0)),
            pl.BlockSpec((16, 128), lambda r: (0, 0)),
        ],
        out_shape=[
            jax.ShapeDtypeStruct((rows, channels, width), BF16),
            jax.ShapeDtypeStruct((REACH, channels, width), BF16),
            jax.ShapeDtypeStruct((REACH, channels, width), BF16),
            jax.ShapeDtypeStruct((16, 128), F32),
        ],
        scratch_shapes=[pltpu.VMEM((4, channels, 128), F32)],
        compiler_params=params(),
        cost_estimate=cost(0.2),
        name="conv_gradient",
    )(da, conv, m16, sums, stat, par)


def join_kernel(index_ref, *refs, names, share):
    n = len(names)
    for index in names:

        @pl.when(index_ref[0] == index)
        def _(index=index):
            for w in range(2):
                for k, name in enumerate(names):
                    row = (index ^ name) * share
                    refs[2 * n + w][row : row + share, :] = refs[w * n + k][...]


def join_pieces(index, first, second):
    names = sorted(first)
    share, cols = first[0].shape
    channels = share * len(names)
    if share % 8:
        out = []
        for pieces in (first, second):
            whole_array = jnp.zeros((channels, cols), BF16)
            for name in names:
                start = (index ^ name) * share
                whole_array = lax.dynamic_update_slice_in_dim(whole_array, pieces[name], start, axis=0)
            out.append(whole_array)
        return out
    tile = 2 * TILE
    column = lambda height: pl.BlockSpec((height, tile), lambda g: (0, g))
    return pl.pallas_call(
        functools.partial(join_kernel, names=names, share=share),
        grid=(pl.cdiv(cols, tile),),
        in_specs=[pl.BlockSpec(memory_space=pltpu.SMEM)] + [column(share)] * (2 * len(names)),
        out_specs=[column(channels)] * 2,
        out_shape=[jax.ShapeDtypeStruct((channels, cols), BF16)] * 2,
        compiler_params=params(),
        cost_estimate=cost(0.1),
        name="join_pieces",
    )(index[None], *[first[k] for k in names], *[second[k] for k in names])


def place_kernel(flags_ref, *refs, starts):
    outs = refs[-2:]
    core, band = flags_ref[flags_ref.shape[0] - 2], flags_ref[flags_ref.shape[0] - 1]
    (low, high), (low_half, high_half) = starts

    def put(out_ref, rows, at, v):
        wide = min(v.shape[1], out_ref.shape[1] - at)
        out_ref[rows, at : at + wide] = v[:, :wide]

    for w, out_ref in enumerate(outs):
        share = out_ref.shape[0]
        mine, other = refs[2 * w][...].astype(F32), refs[2 * w + 1][...].astype(F32)
        put(out_ref, slice(0, share), low, jnp.where(core == 0, mine, other))
        put(out_ref, slice(0, share), high, jnp.where(core == 0, other, mine))
        own, far, own_other, far_other = (ref[w].astype(F32) for ref in refs[4:8])
        rows = own.shape[0]
        both = []
        for near, away in ((own, far), (own_other, far_other)):
            first = jnp.where(band == 0, near, away)
            last = jnp.where(band == 0, away, near)[2 * rows - share :]
            both.append((first, last))
        for part, at in ((slice(0, rows), 0), (slice(rows, share), 1)):
            put(out_ref, part, low_half, jnp.where(core == 0, both[0][at], both[1][at]))
            put(out_ref, part, high_half, jnp.where(core == 0, both[1][at], both[0][at]))


def place_columns(flags, whole_parts, half_parts, starts, share, units):
    operands = [v for pair in whole_parts for v in pair] + list(half_parts)
    return pl.pallas_call(
        functools.partial(place_kernel, starts=starts),
        in_specs=[pl.BlockSpec(memory_space=pltpu.SMEM)]
        + [pl.BlockSpec(v.shape, lambda n=v.ndim: (0,) * n) for v in operands],
        out_specs=[pl.BlockSpec((share, units), lambda: (0, 0))] * 2,
        out_shape=[jax.ShapeDtypeStruct((share, units), F32)] * 2,
        compiler_params=params(),
        cost_estimate=cost(0.1),
        name="place_columns",
    )(flags, *operands)


def halo(first, last):
    size = lax.axis_size("dp")
    up = [(i, i + 1) for i in range(size - 1)]
    down = [(j, i) for i, j in up]
    return (
        lax.ppermute(last, "dp", up),
        lax.ppermute(first, "dp", down),
    )


def after(value, *others):
    return lax.optimization_barrier((value,) + others)[0]


def from_all(values, axis):
    copies = jnp.broadcast_to(values[None], (lax.axis_size(axis),) + values.shape)
    return lax.all_to_all(copies, axis, 0, 0)


def flip_bit(values, axis, bit):
    size = lax.axis_size(axis)
    return lax.ppermute(values, axis, [(i, i ^ (1 << bit)) for i in range(size)])


def bit_of(axis, bit):
    return (lax.axis_index(axis) >> bit) & 1


def gather_pieces(own, order):
    return {0: own} | {1 << bit: flip_bit(own, "fsdp", bit) for bit in order}


def gather_others(have, order, *others):
    reached = {0: have[0]}
    for bit in order:
        for name, v in list(reached.items()):
            far = have.get(name | 1 << bit)
            reached[name | 1 << bit] = far if far is not None else flip_bit(after(v, *others), "fsdp", bit)
    return reached


def per_device(
    inputs,
    out_grad,
    ocean_mask,
    rollout_lengths,
    conv_weight,
    norm_gain,
    norm_bias,
    expand_weight,
    expand_bias,
    project_weight,
    project_bias,
):
    channels, rows, width = inputs.shape[1:]
    n_fs, n_dp = lax.axis_size("fsdp"), lax.axis_size("dp")
    devices = ("dp", "fsdp")
    share = conv_weight.shape[0]
    units = expand_weight.shape[1]
    half = pl.cdiv(units // 128, 2) * 128
    bits = list(range(n_fs.bit_length() - 1))
    core = bit_of("dp", 0)
    x = inputs[0].transpose(1, 0, 2)
    og = out_grad[0].transpose(1, 0, 2)
    block = 5 * GRP

    ratio = expand_bias.shape[0] // share
    x_first, x_last = x[:REACH], x[-REACH:]
    small = jnp.concatenate(
        [
            after(conv_weight, x_first, x_last).T,
            norm_gain[None],
            norm_bias[None],
            project_bias.astype(F32)[None],
            expand_bias.astype(F32).reshape(ratio, share),
        ],
        axis=0,
    )
    every = from_all(small, "fsdp")
    e_bias = jnp.pad(every[:, TAPS + 3 :].reshape(1, units), ((0, 0), (0, 2 * half - units)))
    x_up, x_dn = halo(x_first, x_last)

    def columns(weight):
        weight = after(weight, every)
        high = jnp.pad(weight[:, half:], ((0, 0), (0, 2 * half - units)))
        return jnp.where(core == 0, high, weight[:, :half])

    eb_own = lax.dynamic_slice_in_dim(e_bias, core * half, half, axis=1)
    eb_peer = lax.dynamic_slice_in_dim(e_bias, (1 - core) * half, half, axis=1)

    sample = lax.axis_index("fsdp")
    length = lax.dynamic_index_in_dim(rollout_lengths, sample, keepdims=False)
    live = jnp.where(sample % ROLLOUT < length, 1.0, 0.0).astype(F32)
    weight = live * ocean_mask.astype(F32)
    m16 = jnp.broadcast_to(weight[:, None, :], (rows, GRP, width))

    we_pieces = gather_pieces(columns(expand_weight), bits)
    wp_pieces = gather_pieces(columns(project_weight), bits[::-1])

    copies = n_fs * n_dp
    orders = (bits[::-1], bits)
    flags = jnp.stack([bit_of("fsdp", bit) for bit in bits] + [core, bit_of("dp", 1)]).astype(jnp.int32)
    bg, bg_sum = mask_gradient(og, after(m16, we_pieces[0], wp_pieces[0]))
    early = [p[1 << b] for p, b in ((we_pieces, bits[0]), (wp_pieces, bits[-1]))]
    we_pieces = gather_others(we_pieces, bits, bg)
    wp_pieces = gather_others(wp_pieces, bits[::-1], bg)
    ready, eb_own, eb_peer, flags, *_ = lax.optimization_barrier(
        (m16, eb_own, eb_peer, flags, bg, *early)
    )
    conv, stats, par = conv_forward(x, x_up, x_dn, every, ready, copies, block)
    stats = lax.all_to_all(stats, devices, 0, 0)
    index = lax.axis_index("fsdp")
    far = n_fs - 1
    we_pieces[far], wp_pieces[far], index, _ = lax.optimization_barrier(
        (we_pieces[far], wp_pieces[far], index, conv)
    )
    we_peer, wp_peer = join_pieces(index, we_pieces, wp_pieces)
    groups = [[i for i in range(n_dp) if i % 2 == c] for c in range(2)]
    first = half // (2 * TILE) * TILE
    second = half - first

    def piece(order, n):
        return share << len([b for b in order[n + 1 :] if b < order[n]])

    def other_core(grads):
        return [flip_bit(v, "dp", 0) for v in grads]

    def exchanged(pairs, n):
        return [(keep, flip_bit(send, "fsdp", o[n])) for (keep, send), o in zip(pairs, orders, strict=True)]

    def arrived(pairs, *cover):
        came = lax.optimization_barrier((*[came for _, came in pairs], *cover))
        return [(keep, v) for (keep, _), v in zip(pairs, came)]

    def split(pairs, n):
        slots = tuple(order[n] for order in orders)
        return split_sums(flags, pairs, tuple(piece(order, n) for order in orders), slots)

    def sends(pairs):
        return [send for _, send in pairs]

    def over_bands(sums, groups):
        return [lax.psum(v, "dp", axis_index_groups=groups) for v in sums]

    pieces = tuple(piece(o, 0) for o in orders)
    leads = tuple(o[0] for o in orders)
    front = (conv, after(stats, we_peer, wp_peer), par)
    *q1, act, stat = hidden_layer(None, bg, we_peer, wp_peer, eb_peer, 0, first, flags, front=front)
    we_own = flip_bit(after(we_peer, act), "dp", 0)
    wp_own = flip_bit(after(wp_peer, act), "dp", 0)
    c1 = other_core(q1[2:4])
    q2 = hidden_layer(act, bg, we_peer, wp_peer, after(eb_peer, q1[0]), first, second, flags)
    c2 = other_core(q2[2:4])
    o1 = hidden_layer(act, bg, we_own, wp_own, after(eb_own, q2[0]), 0, first, flags, c1, pieces, leads)
    s1 = exchanged([(o1[2], o1[3]), (o1[4], o1[5])], 0)
    o2 = hidden_layer(act, bg, we_own, wp_own, after(eb_own, o1[0]), first, second, flags, c2, pieces, leads)
    for n in range(1, len(bits)):
        s1 = split(arrived(s1, o2[0]), n)
        last = sends(s1)
        s1 = exchanged(s1, n)

    s2 = exchanged([(o2[2], after(o2[3], *last)), (o2[4], after(o2[5], *last))], 0)
    eb_sums = (o1[-1], o2[-1], q1[-1], q2[-1])
    cuts = ((1, 0, first), (0, 0, first), (1, first, second), (0, first, second))
    parts = (q1, o1, q2, o2)
    hidden = [p[0] for p in parts]
    da, sums = activation_gradient(
        (we_own, we_peer), [p[1] for p in parts], cuts, conv, after(stat, *last), copies
    )
    sums = lax.all_to_all(sums, devices, 0, 0)
    z_keep, z_send = band_split(flags, arrived(s1, da))
    z_came = flip_bit(z_send, "dp", 1)
    for n in range(1, len(bits)):
        s2 = split(arrived(s2, da, z_send), n)
        last = sends(s2)
        s2 = exchanged(s2, n)
    ready = after(sums, *last)
    conv_grad, g_first, g_last, totals = conv_gradient(da, conv, m16, ready, stat, par)
    g_up, g_dn = halo(g_first, g_last)
    z_came, *came = lax.optimization_barrier((z_came, *[v for _, v in s2], conv_grad))
    s2 = round_sums([(keep, v) for (keep, _), v in zip(s2, came)])
    b2 = over_bands(s2, groups)
    half_sum = round_sums([(z_keep, z_came)])[0]
    ready = after(conv_grad, half_sum, *s2)
    tap_local = tap_gradient(flags, x, x_up, x_dn, ready, bg_sum, eb_sums, units, block, share)
    g_up, g_dn, half_sum, _ = lax.optimization_barrier((g_up, g_dn, half_sum, tap_local))
    half_came = flip_bit(half_sum, "dp", 2)
    bands = n_dp.bit_length() - 1

    local = lax.all_to_all(tap_local, "fsdp", 0, 0)
    input_grad = input_gradient(conv_grad, g_up, g_dn, after(par, tap_local), og, m16, block)
    half_came, _ = lax.optimization_barrier((half_came, input_grad))
    half_sum = round_sums([(half_sum, half_came)])[0]
    for bit in range(3, bands):
        half_sum = (half_sum.astype(F32) + flip_bit(half_sum, "dp", bit).astype(F32)).astype(BF16)
    half_far = flip_bit(half_sum, "dp", 1)
    local = jnp.sum(after(local, input_grad), axis=0)
    block_out = block_output((wp_own, wp_peer), hidden, cuts, x, m16, after(par, input_grad, local, half_sum))
    local = jnp.sum(after(from_all(local, "dp"), block_out), axis=0)

    half_far, *b2 = lax.optimization_barrier((half_far, *b2, block_out))
    whole_parts = [(v, flip_bit(v, "dp", 0)) for v in b2[:2]]
    half_parts = (half_sum, half_far, flip_bit(half_sum, "dp", 0), flip_bit(half_far, "dp", 0))
    starts = ((first, half + first), (0, half))
    project_grad, expand_grad = place_columns(flags, whole_parts, half_parts, starts, share, units)

    start = lax.axis_index("fsdp") * share
    totals = totals.reshape(2, -1)
    per_channel = lambda v: v.reshape(-1)[:channels]
    return (
        block_out.transpose(1, 0, 2)[None],
        input_grad.transpose(1, 0, 2)[None],
        local[:TAPS].T,
        lax.dynamic_slice_in_dim(totals[1], start, share),
        lax.dynamic_slice_in_dim(totals[0], start, share),
        expand_grad,
        local[TAPS + 1 :].reshape(-1),
        project_grad,
        local[TAPS],
        per_channel(stat[0:8]),
        per_channel(stat[16:24]),
    )


def solution(mesh):
    rows = P("fsdp", None, "dp", None)
    return jax.shard_map(
        per_device,
        mesh=mesh,
        in_specs=(
            rows,
            rows,
            P("dp", None),
            P(),
            P("fsdp", None),
            P("fsdp"),
            P("fsdp"),
            P("fsdp", None),
            P("fsdp"),
            P("fsdp", None),
            P("fsdp"),
        ),
        out_specs=(
            rows,
            rows,
            P("fsdp", None),
            P("fsdp"),
            P("fsdp"),
            P("fsdp", None),
            P("fsdp"),
            P("fsdp", None),
            P("fsdp"),
            P(),
            P(),
        ),
        check_vma=False,
    )
```

```python
import functools

import jax
import jax.numpy as jnp
from jax import lax
from jax.experimental import pallas as pl
from jax.experimental.pallas import tpu as pltpu
from jax.sharding import PartitionSpec as P

KS = 7
REACH = KS // 2
TAPS = KS * KS
ROLLOUT = 8
EPS = 1e-05
F32, BF16 = jnp.float32, jnp.bfloat16
GRP = 16
TILE = 256
VMEM = 639 * 2**20 // 10
GELU_A = 0.7978845608028654
GELU_B = 0.044715
NT = (((1,), (1,)), ((), ()))
TN = (((0,), (0,)), ((), ()))


def params():
    return pltpu.CompilerParams(vmem_limit_bytes=VMEM)


def cost(us):
    return pl.CostEstimate(flops=int(us * 1.15e9), bytes_accessed=10**5, transcendentals=0)


def whole(shape):
    zeros = (0,) * len(shape)
    return pl.BlockSpec(shape, lambda *g: zeros, pipeline_mode=pl.Buffered(1))


def roll_lanes(v, shift):
    shift %= v.shape[-1]
    return v if shift == 0 else pltpu.roll(v, shift, v.ndim - 1)


def columns_of(*rows):
    pieces = []
    for k in range(rows[0].shape[0]):
        used = [v[k : k + 1, :] for v in rows]
        block = jnp.concatenate(used + [jnp.zeros((128 - len(rows), 128), F32)], axis=0)
        pieces.append(block.T)
    return jnp.concatenate(pieces, axis=0)


def wide(column):
    return jnp.broadcast_to(column, (column.shape[0], 128))


def copies_of(cols, out_ref):
    copies = out_ref.shape[0]
    for k in range(cols.shape[0] // 128):
        block = cols[k * 128 : (k + 1) * 128, :].T
        for q in range(2):
            row = jnp.broadcast_to(block[q : q + 1, :][None], (copies, 1, 128))
            out_ref[:, 8 * q + k : 8 * q + k + 1, :] = row


def spread_taps(cols, pick_ref, e_ref):
    count = cols.shape[0]
    lane = lax.broadcasted_iota(jnp.int32, (count, 128), 1)
    own = lax.broadcasted_iota(jnp.int32, (count, 128), 0) % GRP == lane % GRP
    high = cols.astype(BF16)
    low = (cols - high.astype(F32)).astype(BF16)
    for h, part in enumerate((high, low)):
        for j in range(KS):
            picked = jnp.dot(part, pick_ref[j], preferred_element_type=F32)
            e_ref[h, j] = jnp.where(own, picked, 0.0).astype(BF16)


def tap_picker():
    tap = lax.broadcasted_iota(jnp.int32, (128, 128), 0)
    lane = lax.broadcasted_iota(jnp.int32, (128, 128), 1)
    inside = lane < KS * GRP
    first = KS * (lane // GRP)
    return [jnp.where((tap == first + j) & inside, 1.0, 0.0).astype(BF16) for j in range(KS)]


def conv_rows(field_ref, taps_ref, s, rows, flip):
    x = field_ref[:, s, :].reshape((rows + 2 * REACH) * GRP, field_ref.shape[-1])
    parts = [taps_ref[h, :, s, :].reshape(KS * GRP, 128)[:, : KS * GRP] for h in range(2)]
    taps = jnp.concatenate(parts, axis=1)
    out = []
    for r in range(rows):
        src = rows - 1 - r if flip else r
        window = x[src * GRP : (src + KS) * GRP]
        sums = jnp.dot(taps, jnp.concatenate([window, window], axis=0), preferred_element_type=F32)
        acc = None
        for j in range(KS):
            moved = roll_lanes(sums[j * GRP : (j + 1) * GRP], j - REACH if flip else REACH - j)
            acc = moved if acc is None else acc + moved
        out.append(acc)
    return out


def conv_kernel(
    x_ref, up_ref, dn_ref, small_ref, m_ref, out_ref, st_ref, par_ref,
    field_ref, cols_ref, e_ref, pick_ref, count_ref, *, share
):
    rows, block = x_ref.shape[0], x_ref.shape[1]
    step = pl.program_id(0)

    @pl.when(step == 0)
    def _():
        for j, pick in enumerate(tap_picker()):
            pick_ref[j] = pick
        count = jnp.sum(jnp.sum(m_ref[...], axis=0), axis=1, keepdims=True)[0:8]
        count_ref[...] = jnp.broadcast_to(count, (8, 128))
        cols_ref[...] = jnp.zeros(cols_ref.shape, F32)
        given, wide = small_ref.shape[1], pl.cdiv(share, 128) * 128
        for f in range(small_ref.shape[0]):
            v = small_ref[f]
            v = jnp.concatenate([v, jnp.zeros((given, wide - share), F32)], axis=1)
            v = jnp.concatenate([v, jnp.zeros((128 - given, wide), F32)], axis=0)
            par_ref[f * share : (f + 1) * share, :] = v.T[:share]

    field_ref[0:REACH] = up_ref[...]
    field_ref[REACH : REACH + rows] = x_ref[...]
    field_ref[REACH + rows :] = dn_ref[...]
    here = pl.multiple_of(step * block, GRP)
    spread_taps(par_ref[pl.ds(here, block), :], pick_ref, e_ref)
    lane = lax.broadcasted_iota(jnp.int32, (GRP, 128), 1)
    inv_n = 1.0 / jnp.maximum(count_ref[0:1, 0:1], 1.0)
    for g in range(block // GRP):
        s = pl.ds(g * GRP, GRP)
        acc = conv_rows(field_ref, e_ref, s, rows, False)
        total = None
        for r in range(rows):
            out_ref[r, s, :] = acc[r]
            v = acc[r] * m_ref[r]
            total = v if total is None else total + v
        mean = jnp.sum(total, axis=-1, keepdims=True) * inv_n
        total = None
        for r in range(rows):
            d = acc[r] - mean
            v = d * d * m_ref[r]
            total = v if total is None else total + v
        dev = jnp.sum(total, axis=-1, keepdims=True)
        at = pl.multiple_of(step * block + g * GRP, GRP)
        cols_ref[pl.ds(at, GRP), :] = jnp.where(lane == 0, mean, dev)

    @pl.when(step == pl.num_programs(0) - 1)
    def _():
        st_ref[...] = jnp.broadcast_to(count_ref[0:1, :][None], st_ref.shape)
        copies_of(cols_ref[...], st_ref)


def conv_forward(x, up, dn, small, m16, copies, block):
    rows, channels, width = x.shape
    n_fs, given, share = small.shape
    padded = pl.cdiv(channels, 128) * 128
    return pl.pallas_call(
        functools.partial(conv_kernel, share=share),
        grid=(channels // block,),
        in_specs=[
            pl.BlockSpec((rows, block, width), lambda g: (0, g, 0)),
            pl.BlockSpec((REACH, block, width), lambda g: (0, g, 0)),
            pl.BlockSpec((REACH, block, width), lambda g: (0, g, 0)),
            whole((n_fs, given, share)),
            whole((rows, GRP, width)),
        ],
        out_specs=[
            pl.BlockSpec((rows, block, width), lambda g: (0, g, 0)),
            pl.BlockSpec((copies, 16, 128), lambda g: (0, 0, 0)),
            pl.BlockSpec((channels, 128), lambda g: (0, 0)),
        ],
        out_shape=[
            jax.ShapeDtypeStruct((rows, channels, width), F32),
            jax.ShapeDtypeStruct((copies, 16, 128), F32),
            jax.ShapeDtypeStruct((channels, 128), F32),
        ],
        scratch_shapes=[
            pltpu.VMEM((rows + 2 * REACH, block, width), BF16),
            pltpu.VMEM((padded, 128), F32),
            pltpu.VMEM((2, KS, block, 128), BF16),
            pltpu.VMEM((KS, 128, 128), BF16),
            pltpu.VMEM((8, 128), F32),
        ],
        compiler_params=params(),
        cost_estimate=cost(0.4),
        name="conv_forward",
    )(x, up, dn, small, m16)


def input_grad_kernel(
    g_ref, up_ref, dn_ref, par_ref, og_ref, m_ref, out_ref, field_ref, e_ref, pick_ref
):
    @pl.when(pl.program_id(0) == 0)
    def _():
        for j, pick in enumerate(tap_picker()):
            pick_ref[j] = pick

    rows, block = g_ref.shape[0], g_ref.shape[1]
    last = rows + 2 * REACH - 1
    for q in range(REACH):
        field_ref[last - q] = up_ref[q]
        field_ref[REACH - 1 - q] = dn_ref[q]
    for q in range(rows):
        field_ref[last - REACH - q] = g_ref[q]
    spread_taps(par_ref[...], pick_ref, e_ref)
    for g in range(block // GRP):
        s = pl.ds(g * GRP, GRP)
        acc = conv_rows(field_ref, e_ref, s, rows, True)
        for r in range(rows):
            out_ref[r, s, :] = og_ref[r, s, :].astype(F32) * m_ref[r] + acc[r]


def input_gradient(grad, up, dn, par, og, m16, block):
    rows, channels, width = grad.shape
    return pl.pallas_call(
        input_grad_kernel,
        grid=(channels // block,),
        in_specs=[
            pl.BlockSpec((rows, block, width), lambda g: (0, g, 0)),
            pl.BlockSpec((REACH, block, width), lambda g: (0, g, 0)),
            pl.BlockSpec((REACH, block, width), lambda g: (0, g, 0)),
            pl.BlockSpec((block, 128), lambda g: (g, 0)),
            pl.BlockSpec((rows, block, width), lambda g: (0, g, 0)),
            whole((rows, GRP, width)),
        ],
        out_specs=pl.BlockSpec((rows, block, width), lambda g: (0, g, 0)),
        out_shape=jax.ShapeDtypeStruct((rows, channels, width), F32),
        scratch_shapes=[
            pltpu.VMEM((rows + 2 * REACH, block, width), BF16),
            pltpu.VMEM((2, KS, block, 128), BF16),
            pltpu.VMEM((KS, 128, 128), BF16),
        ],
        compiler_params=params(),
        cost_estimate=cost(5),
        name="input_gradient",
    )(grad, up, dn, par, og, m16)


def tap_grad_kernel(
    bits_ref, x_ref, up_ref, dn_ref, g_ref, bg_ref, *refs, share
):
    out_ref, field_ref, cols_ref = refs[-3:]
    rows, block, width = x_ref.shape
    field_ref[0:REACH] = up_ref[...]
    field_ref[REACH : REACH + rows] = x_ref[...]
    field_ref[REACH + rows :] = dn_ref[...]
    lane = lax.broadcasted_iota(jnp.int32, (GRP, 128), 1)
    own = lax.broadcasted_iota(jnp.int32, (GRP, 128), 0) == lane % GRP
    for g in range(block // GRP):
        s = pl.ds(g * GRP, GRP)
        x = field_ref[:, s, :].reshape((rows + 2 * REACH) * GRP, width)
        fields = jnp.concatenate([x[r * GRP : (r + KS) * GRP] for r in range(rows)], axis=1)
        grads = []
        for j in range(KS):
            moved = [roll_lanes(g_ref[r, s, :], j - REACH) for r in range(rows)]
            grads.append(jnp.concatenate(moved, axis=1))
        grads = jnp.concatenate(grads, axis=0)
        sums = lax.dot_general(grads, fields, NT, preferred_element_type=F32)
        sums = jnp.concatenate([sums, jnp.zeros((KS * GRP, 128 - KS * GRP), F32)], axis=1)
        out = None
        for j in range(KS):
            acc = jnp.where(own, sums[j * GRP : (j + 1) * GRP], 0.0)
            for k in (8, 4, 2, 1):
                acc = acc + pltpu.roll(acc, 128 - k, 1)
            acc = roll_lanes(acc, j)
            out = acc if out is None else jnp.where(lane % GRP == j, acc, out)
        at = pl.multiple_of(pl.program_id(0) * block + g * GRP, GRP)
        cols_ref[pl.ds(at, GRP), :] = out

    @pl.when(pl.program_id(0) == pl.num_programs(0) - 1)
    def _():
        blocks = [cols_ref[k : k + 128, :].T for k in range(0, cols_ref.shape[0], 128)]
        wide = jnp.concatenate(blocks, axis=1)
        taps = jnp.concatenate([wide[GRP * i : GRP * i + KS] for i in range(KS)], axis=0)
        band = jnp.concatenate([bg_ref[0, k : k + 1, :] for k in range(wide.shape[1] // 128)], axis=1)
        own, peer = (jnp.concatenate([refs[q][...], refs[q + 1][...]], axis=1) for q in (0, 2))
        core = bits_ref[bits_ref.shape[0] - 2]
        units = jnp.concatenate(
            [jnp.where(core == 0, own, peer), jnp.where(core == 0, peer, own)], axis=1
        )
        ratio = out_ref.shape[1] - TAPS - 1
        for f in range(out_ref.shape[0]):
            out_ref[f, 0:TAPS, :] = taps[:, f * share : (f + 1) * share]
            out_ref[f, TAPS : TAPS + 1, :] = band[:, f * share : (f + 1) * share]
            for q in range(ratio):
                at = (f * ratio + q) * share
                out_ref[f, TAPS + 1 + q : TAPS + 2 + q, :] = units[:, at : at + share]


def tap_gradient(bits, x, up, dn, grad, bg_sum, eb_sums, units, block, share):
    rows, channels, width = x.shape
    padded = pl.cdiv(channels, 128) * 128
    height = TAPS + 1 + units // channels
    return pl.pallas_call(
        functools.partial(tap_grad_kernel, share=share),
        grid=(channels // block,),
        in_specs=[
            pl.BlockSpec(memory_space=pltpu.SMEM),
            pl.BlockSpec((rows, block, width), lambda g: (0, g, 0)),
            pl.BlockSpec((REACH, block, width), lambda g: (0, g, 0)),
            pl.BlockSpec((REACH, block, width), lambda g: (0, g, 0)),
            pl.BlockSpec((rows, block, width), lambda g: (0, g, 0)),
            whole(bg_sum.shape),
        ]
        + [whole(v.shape) for v in eb_sums],
        out_specs=pl.BlockSpec((channels // share, height, share), lambda g: (0, 0, 0)),
        out_shape=jax.ShapeDtypeStruct((channels // share, height, share), F32),
        scratch_shapes=[
            pltpu.VMEM((rows + 2 * REACH, block, width), BF16),
            pltpu.VMEM((padded, 128), F32),
        ],
        compiler_params=params(),
        cost_estimate=cost(15),
        name="tap_gradient",
    )(bits, x, up, dn, grad, bg_sum, *eb_sums)


def mask_grad_kernel(og_ref, m_ref, out_ref, sum_ref, cols_ref):
    row = pl.program_id(0)
    channels = og_ref.shape[1]
    v = og_ref[0].astype(F32) * m_ref[0, 0:1]
    out_ref[...] = v.astype(BF16)
    part = v[:, 0:128]
    for k in range(128, v.shape[1], 128):
        part = part + v[:, k : k + 128]

    @pl.when(row == 0)
    def _():
        cols_ref[...] = jnp.zeros(cols_ref.shape, F32)

    cols_ref[0:channels, :] += part

    @pl.when(row == pl.num_programs(0) - 1)
    def _():
        sums = jnp.broadcast_to(jnp.sum(cols_ref[...], axis=1, keepdims=True), cols_ref.shape)
        copies_of(sums, sum_ref)


def mask_gradient(og, m16):
    rows, channels, width = og.shape
    padded = pl.cdiv(channels, 128) * 128
    pixels = rows * width
    return pl.pallas_call(
        mask_grad_kernel,
        grid=(rows,),
        in_specs=[
            pl.BlockSpec((1, channels, width), lambda r: (r, 0, 0)),
            pl.BlockSpec((1, GRP, width), lambda r: (r, 0, 0)),
        ],
        out_specs=[
            pl.BlockSpec((channels, width), lambda r: (0, r)),
            pl.BlockSpec((1, 16, 128), lambda r: (0, 0, 0)),
        ],
        out_shape=[
            jax.ShapeDtypeStruct((channels, pixels), BF16),
            jax.ShapeDtypeStruct((1, 16, 128), F32),
        ],
        scratch_shapes=[pltpu.VMEM((padded, 128), F32)],
        compiler_params=params(),
        cost_estimate=cost(0.1),
        name="mask_gradient",
    )(og, m16)


def activate(conv_ref, all_ref, par_ref, act_ref, stat_ref):
    rows, channels, width = conv_ref.shape
    means, squares = all_ref[:, 0:8, :], all_ref[:, 8:16, :]
    counts = all_ref[:, 7:8, :]
    count = jnp.sum(counts, axis=0)
    mean = jnp.sum(counts * means, axis=0) / count
    apart = means - mean[None]
    variance = jnp.sum(squares + counts * apart * apart, axis=0) / count
    inv_std = lax.rsqrt(variance + EPS)
    stat_ref[0:8] = mean
    stat_ref[8:16] = inv_std
    stat_ref[16:24] = jnp.sqrt(variance + EPS)
    stat_ref[24:32] = jnp.broadcast_to(count, (8, 128))
    c, p = columns_of(mean[0:7], inv_std[0:7])[:channels], par_ref[...]
    centre = wide(c[:, 0:1])
    scale = wide(c[:, 1:2] * p[:, TAPS : TAPS + 1])
    shift = wide(p[:, TAPS + 1 : TAPS + 2])
    for r in range(rows):
        for k in range(0, width, 128):
            v = (conv_ref[r, :, k : k + 128] - centre) * scale + shift
            act_ref[:, r * width + k : r * width + k + 128] = v.astype(BF16)


def gelu_parts(v):
    v2 = v * v
    t = jnp.tanh(v * (GELU_A + (GELU_A * GELU_B) * v2))
    s = 0.5 * t + 0.5
    h = v * s
    return h, s + h * (1.0 - s) * (2 * GELU_A + (6 * GELU_A * GELU_B) * v2)


def halves(v, mine, piece):
    keep, send = [], []
    for o in range(0, v.shape[0], 2 * piece):
        first, second = v[o : o + piece], v[o + piece : o + 2 * piece]
        keep.append(jnp.where(mine == 0, first, second))
        send.append(jnp.where(mine == 0, second, first))
    return jnp.concatenate(keep, axis=0), jnp.concatenate(send, axis=0)


def hidden_kernel(bits_ref, bg_ref, we_ref, wp_ref, eb_ref, *refs, step, pieces, slots, leads):
    if leads:
        conv_ref, all_ref, par_ref, h_ref, g_ref, dwp_ref, dwe_ref, ebg_ref, act_ref, stat_ref = refs

        @pl.when(pl.program_id(0) == 0)
        def _():
            activate(conv_ref, all_ref, par_ref, act_ref, stat_ref)

    else:
        act_ref, refs = refs[0], refs[1:]
    if leads:
        pass
    elif pieces is None:
        h_ref, g_ref, dwp_ref, dwe_ref, ebg_ref = refs
    else:
        other_p, other_e, h_ref, g_ref, keep_p, send_p, keep_e, send_e, ebg_ref = refs
    we, wp, bias = we_ref[...], wp_ref[...], eb_ref[...]
    total = None
    for p in range(0, act_ref.shape[1], step):
        pre = lax.dot_general(act_ref[:, p : p + step], we, TN, preferred_element_type=F32) + bias
        pull = lax.dot_general(bg_ref[:, p : p + step], wp, TN, preferred_element_type=F32)
        h, slope = gelu_parts(pre)
        grad = (pull * slope).astype(BF16)
        h_ref[p : p + step, :] = h.astype(BF16)
        g_ref[p : p + step, :] = grad
        part = jnp.sum(grad.astype(F32), axis=0, keepdims=True)
        total = part if total is None else total + part
    ebg_ref[...] = total
    dwp = jnp.dot(bg_ref[...], h_ref[...], preferred_element_type=F32)
    dwe = jnp.dot(act_ref[...], g_ref[...], preferred_element_type=F32)
    if pieces is None:
        dwp_ref[...] = dwp.astype(BF16)
        dwe_ref[...] = dwe.astype(BF16)
    else:
        keep, send = halves(dwp + other_p[...].astype(F32), bits_ref[slots[0]], pieces[0])
        keep_p[...] = keep
        send_p[...] = send.astype(BF16)
        keep, send = halves(dwe + other_e[...].astype(F32), bits_ref[slots[1]], pieces[1])
        keep_e[...] = keep
        send_e[...] = send.astype(BF16)


def hidden_layer(act, bg, we, wp, eb, first, units, bits, others=None, pieces=None, slots=None, front=None):
    channels, pixels = bg.shape
    off = first // TILE
    column = lambda rows: pl.BlockSpec((rows, TILE), lambda g: (0, g))
    weight = pl.BlockSpec((channels, TILE), lambda g: (0, g + off))
    shape = lambda rows, dtype: jax.ShapeDtypeStruct((rows, units), dtype)
    in_specs = [pl.BlockSpec(memory_space=pltpu.SMEM), whole(bg.shape), weight, weight]
    in_specs.append(pl.BlockSpec((1, TILE), lambda g: (0, g + off)))
    made = [act] if front is None else list(front)
    operands = [bits, bg, we, wp, eb] + made
    in_specs += [whole(v.shape) for v in made]
    out_specs = [column(pixels), column(pixels)]
    out_shape = [shape(pixels, BF16), shape(pixels, BF16)]
    if others is None:
        out_specs += [column(channels), column(channels)]
        out_shape += [shape(channels, BF16), shape(channels, BF16)]
    else:
        in_specs += [column(channels), column(channels)]
        operands += list(others)
        out_specs += [column(channels // 2)] * 4
        out_shape += [shape(channels // 2, F32), shape(channels // 2, BF16)] * 2
    out_specs.append(column(1))
    out_shape.append(shape(1, F32))
    if front is not None:
        out_specs += [pl.BlockSpec((channels, pixels), lambda g: (0, 0)), pl.BlockSpec((32, 128), lambda g: (0, 0))]
        out_shape += [jax.ShapeDtypeStruct((channels, pixels), BF16), jax.ShapeDtypeStruct((32, 128), F32)]
    return pl.pallas_call(
        functools.partial(hidden_kernel, step=128, pieces=pieces, slots=slots, leads=front is not None),
        grid=(pl.cdiv(units, TILE),),
        in_specs=in_specs,
        out_specs=out_specs,
        out_shape=out_shape,
        compiler_params=params(),
        cost_estimate=cost(0.3),
        name="hidden_layer",
    )(*operands)


def split_kernel(bits_ref, *refs, pieces, slots):
    n = len(pieces)
    for k, (piece, slot) in enumerate(zip(pieces, slots, strict=True)):
        total = refs[2 * k][...] + refs[2 * k + 1][...].astype(F32)
        keep, send = halves(total, bits_ref[slot], piece)
        refs[2 * n + 2 * k][...] = keep
        refs[2 * n + 2 * k + 1][...] = send.astype(BF16)


def split_sums(bits, pairs, pieces, slots):
    rows, cols = pairs[0][0].shape
    shape = lambda dtype: jax.ShapeDtypeStruct((rows // 2, cols), dtype)
    spec = lambda height: pl.BlockSpec((height, cols), lambda: (0, 0))
    out = pl.pallas_call(
        functools.partial(split_kernel, pieces=pieces, slots=slots),
        in_specs=[pl.BlockSpec(memory_space=pltpu.SMEM)] + [spec(rows)] * (2 * len(pairs)),
        out_specs=[spec(rows // 2)] * (2 * len(pairs)),
        out_shape=[shape(F32), shape(BF16)] * len(pairs),
        compiler_params=params(),
        cost_estimate=cost(3),
        name="split_sums",
    )(bits, *[v for pair in pairs for v in pair])
    return [(out[2 * k], out[2 * k + 1]) for k in range(len(pairs))]


def band_split_kernel(bits_ref, *refs):
    keep_ref, send_ref = refs[-2:]
    rows = keep_ref.shape[1]
    band = bits_ref[bits_ref.shape[0] - 1]
    for k in range(keep_ref.shape[0]):
        total = refs[2 * k][...] + refs[2 * k + 1][...].astype(F32)
        low, high = total[:rows], total[total.shape[0] - rows :]
        keep_ref[k] = jnp.where(band == 0, low, high)
        send_ref[k] = jnp.where(band == 0, high, low).astype(BF16)


def band_split(bits, pairs):
    share, cols = pairs[0][0].shape
    rows = pl.cdiv(pl.cdiv(share, 2), 8) * 8
    spec = pl.BlockSpec((share, cols), lambda: (0, 0))
    out = pl.BlockSpec((len(pairs), rows, cols), lambda: (0, 0, 0))
    shape = lambda dtype: jax.ShapeDtypeStruct((len(pairs), rows, cols), dtype)
    return pl.pallas_call(
        band_split_kernel,
        in_specs=[pl.BlockSpec(memory_space=pltpu.SMEM)] + [spec] * (2 * len(pairs)),
        out_specs=[out, out],
        out_shape=[shape(F32), shape(BF16)],
        compiler_params=params(),
        cost_estimate=cost(3),
        name="band_split",
    )(bits, *[v for pair in pairs for v in pair])


def round_kernel(*refs):
    n = len(refs) // 3
    for k in range(n):
        total = refs[2 * k][...].astype(F32) + refs[2 * k + 1][...].astype(F32)
        refs[2 * n + k][...] = total.astype(BF16)


def round_sums(pairs):
    shape = pairs[0][0].shape
    spec = pl.BlockSpec(shape, lambda: (0,) * len(shape))
    return pl.pallas_call(
        round_kernel,
        in_specs=[spec] * (2 * len(pairs)),
        out_specs=[spec] * len(pairs),
        out_shape=[jax.ShapeDtypeStruct(pairs[0][0].shape, BF16)] * len(pairs),
        compiler_params=params(),
        cost_estimate=cost(3),
        name="round_sums",
    )(*[v for pair in pairs for v in pair])


def contract(weights, hiddens):
    total = None
    for (w_ref, first, units), h_ref in zip(weights, hiddens, strict=True):
        part = lax.dot_general(
            w_ref[:, first : first + units], h_ref[...], NT, preferred_element_type=F32
        )
        total = part if total is None else total + part
    return total


def act_grad_kernel(*refs, cuts):
    n = len(cuts)
    w_refs, h_refs = refs[0:2], refs[2 : 2 + n]
    conv_ref, stat_ref, out_ref, sum_ref, cols_ref, acc_ref = refs[2 + n :]
    channels = conv_ref.shape[1]
    row = pl.program_id(0)

    @pl.when(row == 0)
    def _():
        cols_ref[...] = columns_of(stat_ref[0:7], stat_ref[8:15])[: cols_ref.shape[0]]
        acc_ref[...] = jnp.zeros(acc_ref.shape, F32)

    grad = contract([(w_refs[w], first, units) for w, first, units in cuts], h_refs)
    out_ref[0] = grad
    c = cols_ref[0:channels, :]
    scaled = grad * ((conv_ref[0] - c[:, 0:1]) * c[:, 1:2])
    plain, weighted = grad[:, 0:128], scaled[:, 0:128]
    for k in range(128, grad.shape[1], 128):
        plain = plain + grad[:, k : k + 128]
        weighted = weighted + scaled[:, k : k + 128]
    acc_ref[0, 0:channels, :] += plain
    acc_ref[1, 0:channels, :] += weighted

    @pl.when(row == pl.num_programs(0) - 1)
    def _():
        lane = lax.broadcasted_iota(jnp.int32, cols_ref.shape, 1)
        plain = jnp.sum(acc_ref[0], axis=1, keepdims=True)
        weighted = jnp.sum(acc_ref[1], axis=1, keepdims=True)
        sum_ref[...] = jnp.zeros(sum_ref.shape, F32)
        copies_of(jnp.where(lane == 0, plain, weighted), sum_ref)


def activation_gradient(weights, hiddens, cuts, conv, stat, copies):
    rows, channels, width = conv.shape
    padded = pl.cdiv(channels, 128) * 128
    return pl.pallas_call(
        functools.partial(act_grad_kernel, cuts=cuts),
        grid=(rows,),
        in_specs=[whole(w.shape) for w in weights]
        + [pl.BlockSpec((width, h.shape[1]), lambda r: (r, 0)) for h in hiddens]
        + [pl.BlockSpec((1, channels, width), lambda r: (r, 0, 0)), whole(stat.shape)],
        out_specs=[
            pl.BlockSpec((1, channels, width), lambda r: (r, 0, 0)),
            pl.BlockSpec((copies, 16, 128), lambda r: (0, 0, 0)),
        ],
        out_shape=[
            jax.ShapeDtypeStruct((rows, channels, width), F32),
            jax.ShapeDtypeStruct((copies, 16, 128), F32),
        ],
        scratch_shapes=[pltpu.VMEM((padded, 128), F32), pltpu.VMEM((2, padded, 128), F32)],
        compiler_params=params(),
        cost_estimate=cost(0.3),
        name="activation_gradient",
    )(*weights, *hiddens, conv, stat)


def block_out_kernel(*refs, cuts):
    n = len(cuts)
    w_refs, h_refs = refs[0:2], refs[2 : 2 + n]
    x_ref, m_ref, par_ref = refs[2 + n : 5 + n]
    out_ref = refs[-1]
    branch = contract([(w_refs[w], first, units) for w, first, units in cuts], h_refs)
    branch = branch + par_ref[:, TAPS + 2 : TAPS + 3]
    out_ref[0] = ((x_ref[0].astype(F32) + branch) * m_ref[0, 0:1]).astype(BF16)


def block_output(weights, hiddens, cuts, x, m16, par):
    rows, channels, width = x.shape
    return pl.pallas_call(
        functools.partial(block_out_kernel, cuts=cuts),
        grid=(rows,),
        in_specs=[whole(w.shape) for w in weights]
        + [pl.BlockSpec((width, h.shape[1]), lambda r: (r, 0)) for h in hiddens]
        + [
            pl.BlockSpec((1, channels, width), lambda r: (r, 0, 0)),
            pl.BlockSpec((1, GRP, width), lambda r: (r, 0, 0)),
            whole(par.shape),
        ],
        out_specs=pl.BlockSpec((1, channels, width), lambda r: (r, 0, 0)),
        out_shape=jax.ShapeDtypeStruct((rows, channels, width), BF16),
        compiler_params=params(),
        cost_estimate=cost(5),
        name="block_output",
    )(*weights, *hiddens, x, m16, par)


def conv_grad_kernel(
    da_ref, conv_ref, m_ref, all_ref, stat_ref, par_ref, out_ref, top_ref, end_ref, sum_ref, cols_ref
):
    row = pl.program_id(0)
    channels = conv_ref.shape[1]

    @pl.when(pl.program_id(0) == 0)
    def _():
        sums = jnp.sum(all_ref[...], axis=0)
        sum_ref[...] = sums
        count = stat_ref[24:32]
        c = columns_of(
            stat_ref[0:7], stat_ref[8:15], (sums[0:8] / count)[0:7], (sums[8:16] / count)[0:7]
        )[:channels]
        factor = c[:, 1:2] * par_ref[:, TAPS : TAPS + 1]
        cols_ref[0] = wide(c[:, 0:1])
        cols_ref[1] = wide(factor)
        cols_ref[2] = wide(factor * c[:, 2:3])
        cols_ref[3] = wide(factor * c[:, 1:2] * c[:, 3:4])

    for r in range(out_ref.shape[0]):
        for k in range(0, out_ref.shape[2], 128):
            s = slice(k, k + 128)
            apart = conv_ref[r, :, s] - cols_ref[0]
            correction = m_ref[r, 0:1, s] * (cols_ref[2] + apart * cols_ref[3])
            out_ref[r, :, s] = (cols_ref[1] * da_ref[r, :, s] - correction).astype(BF16)

    @pl.when(row == 0)
    def _():
        top_ref[...] = out_ref[...]

    @pl.when(row == pl.num_programs(0) - 1)
    def _():
        end_ref[...] = out_ref[...]


def conv_gradient(da, conv, m16, sums, stat, par):
    rows, channels, width = conv.shape
    return pl.pallas_call(
        conv_grad_kernel,
        grid=(rows // REACH,),
        in_specs=[
            pl.BlockSpec((REACH, channels, width), lambda r: (r, 0, 0)),
            pl.BlockSpec((REACH, channels, width), lambda r: (r, 0, 0)),
            pl.BlockSpec((REACH, GRP, width), lambda r: (r, 0, 0)),
            whole(sums.shape),
            whole(stat.shape),
            whole(par.shape),
        ],
        out_specs=[
            pl.BlockSpec((REACH, channels, width), lambda r: (r, 0, 0)),
            pl.BlockSpec((REACH, channels, width), lambda r: (0, 0, 0)),
            pl.BlockSpec((REACH, channels, width), lambda r: (0, 0, 0)),
            pl.BlockSpec((16, 128), lambda r: (0, 0)),
        ],
        out_shape=[
            jax.ShapeDtypeStruct((rows, channels, width), BF16),
            jax.ShapeDtypeStruct((REACH, channels, width), BF16),
            jax.ShapeDtypeStruct((REACH, channels, width), BF16),
            jax.ShapeDtypeStruct((16, 128), F32),
        ],
        scratch_shapes=[pltpu.VMEM((4, channels, 128), F32)],
        compiler_params=params(),
        cost_estimate=cost(0.2),
        name="conv_gradient",
    )(da, conv, m16, sums, stat, par)


def join_kernel(index_ref, *refs, names, share):
    n = len(names)
    for index in names:

        @pl.when(index_ref[0] == index)
        def _(index=index):
            for w in range(2):
                for k, name in enumerate(names):
                    row = (index ^ name) * share
                    refs[2 * n + w][row : row + share, :] = refs[w * n + k][...]


def join_pieces(index, first, second):
    names = sorted(first)
    share, cols = first[0].shape
    channels = share * len(names)
    if share % 8:
        out = []
        for pieces in (first, second):
            whole_array = jnp.zeros((channels, cols), BF16)
            for name in names:
                start = (index ^ name) * share
                whole_array = lax.dynamic_update_slice_in_dim(whole_array, pieces[name], start, axis=0)
            out.append(whole_array)
        return out
    tile = 2 * TILE
    column = lambda height: pl.BlockSpec((height, tile), lambda g: (0, g))
    return pl.pallas_call(
        functools.partial(join_kernel, names=names, share=share),
        grid=(pl.cdiv(cols, tile),),
        in_specs=[pl.BlockSpec(memory_space=pltpu.SMEM)] + [column(share)] * (2 * len(names)),
        out_specs=[column(channels)] * 2,
        out_shape=[jax.ShapeDtypeStruct((channels, cols), BF16)] * 2,
        compiler_params=params(),
        cost_estimate=cost(0.1),
        name="join_pieces",
    )(index[None], *[first[k] for k in names], *[second[k] for k in names])


def place_kernel(flags_ref, *refs, starts):
    outs = refs[-2:]
    core, band = flags_ref[flags_ref.shape[0] - 2], flags_ref[flags_ref.shape[0] - 1]
    (low, high), (low_half, high_half) = starts

    def put(out_ref, rows, at, v):
        wide = min(v.shape[1], out_ref.shape[1] - at)
        out_ref[rows, at : at + wide] = v[:, :wide]

    for w, out_ref in enumerate(outs):
        share = out_ref.shape[0]
        mine, other = refs[2 * w][...].astype(F32), refs[2 * w + 1][...].astype(F32)
        put(out_ref, slice(0, share), low, jnp.where(core == 0, mine, other))
        put(out_ref, slice(0, share), high, jnp.where(core == 0, other, mine))
        own, far, own_other, far_other = (ref[w].astype(F32) for ref in refs[4:8])
        rows = own.shape[0]
        both = []
        for near, away in ((own, far), (own_other, far_other)):
            first = jnp.where(band == 0, near, away)
            last = jnp.where(band == 0, away, near)[2 * rows - share :]
            both.append((first, last))
        for part, at in ((slice(0, rows), 0), (slice(rows, share), 1)):
            put(out_ref, part, low_half, jnp.where(core == 0, both[0][at], both[1][at]))
            put(out_ref, part, high_half, jnp.where(core == 0, both[1][at], both[0][at]))


def place_columns(flags, whole_parts, half_parts, starts, share, units):
    operands = [v for pair in whole_parts for v in pair] + list(half_parts)
    return pl.pallas_call(
        functools.partial(place_kernel, starts=starts),
        in_specs=[pl.BlockSpec(memory_space=pltpu.SMEM)]
        + [pl.BlockSpec(v.shape, lambda n=v.ndim: (0,) * n) for v in operands],
        out_specs=[pl.BlockSpec((share, units), lambda: (0, 0))] * 2,
        out_shape=[jax.ShapeDtypeStruct((share, units), F32)] * 2,
        compiler_params=params(),
        cost_estimate=cost(0.1),
        name="place_columns",
    )(flags, *operands)


def halo(first, last):
    size = lax.axis_size("dp")
    up = [(i, i + 1) for i in range(size - 1)]
    down = [(j, i) for i, j in up]
    return (
        lax.ppermute(last, "dp", up),
        lax.ppermute(first, "dp", down),
    )


def after(value, *others):
    return lax.optimization_barrier((value,) + others)[0]


def from_all(values, axis):
    copies = jnp.broadcast_to(values[None], (lax.axis_size(axis),) + values.shape)
    return lax.all_to_all(copies, axis, 0, 0)


def flip_bit(values, axis, bit):
    size = lax.axis_size(axis)
    return lax.ppermute(values, axis, [(i, i ^ (1 << bit)) for i in range(size)])


def bit_of(axis, bit):
    return (lax.axis_index(axis) >> bit) & 1


def gather_pieces(own, order):
    return {0: own} | {1 << bit: flip_bit(own, "fsdp", bit) for bit in order}


def gather_others(have, order, *others):
    reached = {0: have[0]}
    for bit in order:
        for name, v in list(reached.items()):
            far = have.get(name | 1 << bit)
            reached[name | 1 << bit] = far if far is not None else flip_bit(after(v, *others), "fsdp", bit)
    return reached


def per_device(
    inputs,
    out_grad,
    ocean_mask,
    rollout_lengths,
    conv_weight,
    norm_gain,
    norm_bias,
    expand_weight,
    expand_bias,
    project_weight,
    project_bias,
):
    channels, rows, width = inputs.shape[1:]
    n_fs, n_dp = lax.axis_size("fsdp"), lax.axis_size("dp")
    devices = ("dp", "fsdp")
    share = conv_weight.shape[0]
    units = expand_weight.shape[1]
    half = pl.cdiv(units // 128, 2) * 128
    bits = list(range(n_fs.bit_length() - 1))
    core = bit_of("dp", 0)
    x = inputs[0].transpose(1, 0, 2)
    og = out_grad[0].transpose(1, 0, 2)
    block = 5 * GRP

    ratio = expand_bias.shape[0] // share
    x_first, x_last = x[:REACH], x[-REACH:]
    small = jnp.concatenate(
        [
            after(conv_weight, x_first, x_last).T,
            norm_gain[None],
            norm_bias[None],
            project_bias.astype(F32)[None],
            expand_bias.astype(F32).reshape(ratio, share),
        ],
        axis=0,
    )
    every = from_all(small, "fsdp")
    e_bias = jnp.pad(every[:, TAPS + 3 :].reshape(1, units), ((0, 0), (0, 2 * half - units)))
    x_up, x_dn = halo(x_first, x_last)

    def columns(weight):
        weight = after(weight, every)
        high = jnp.pad(weight[:, half:], ((0, 0), (0, 2 * half - units)))
        return jnp.where(core == 0, high, weight[:, :half])

    eb_own = lax.dynamic_slice_in_dim(e_bias, core * half, half, axis=1)
    eb_peer = lax.dynamic_slice_in_dim(e_bias, (1 - core) * half, half, axis=1)

    sample = lax.axis_index("fsdp")
    length = lax.dynamic_index_in_dim(rollout_lengths, sample, keepdims=False)
    live = jnp.where(sample % ROLLOUT < length, 1.0, 0.0).astype(F32)
    weight = live * ocean_mask.astype(F32)
    m16 = jnp.broadcast_to(weight[:, None, :], (rows, GRP, width))

    we_pieces = gather_pieces(columns(expand_weight), bits)
    wp_pieces = gather_pieces(columns(project_weight), bits[::-1])

    copies = n_fs * n_dp
    orders = (bits[::-1], bits)
    flags = jnp.stack([bit_of("fsdp", bit) for bit in bits] + [core, bit_of("dp", 1)]).astype(jnp.int32)
    bg, bg_sum = mask_gradient(og, after(m16, we_pieces[0], wp_pieces[0]))
    early = [p[1 << b] for p, b in ((we_pieces, bits[0]), (wp_pieces, bits[-1]))]
    we_pieces = gather_others(we_pieces, bits, bg)
    wp_pieces = gather_others(wp_pieces, bits[::-1], bg)
    ready, eb_own, eb_peer, flags, *_ = lax.optimization_barrier(
        (m16, eb_own, eb_peer, flags, bg, *early)
    )
    conv, stats, par = conv_forward(x, x_up, x_dn, every, ready, copies, block)
    stats = lax.all_to_all(stats, devices, 0, 0)
    index = lax.axis_index("fsdp")
    far = n_fs - 1
    we_pieces[far], wp_pieces[far], index, _ = lax.optimization_barrier(
        (we_pieces[far], wp_pieces[far], index, conv)
    )
    we_peer, wp_peer = join_pieces(index, we_pieces, wp_pieces)
    groups = [[i for i in range(n_dp) if i % 2 == c] for c in range(2)]
    first = half // (2 * TILE) * TILE
    second = half - first

    def piece(order, n):
        return share << len([b for b in order[n + 1 :] if b < order[n]])

    def other_core(grads):
        return [flip_bit(v, "dp", 0) for v in grads]

    def exchanged(pairs, n):
        return [(keep, flip_bit(send, "fsdp", o[n])) for (keep, send), o in zip(pairs, orders, strict=True)]

    def arrived(pairs, *cover):
        came = lax.optimization_barrier((*[came for _, came in pairs], *cover))
        return [(keep, v) for (keep, _), v in zip(pairs, came)]

    def split(pairs, n):
        slots = tuple(order[n] for order in orders)
        return split_sums(flags, pairs, tuple(piece(order, n) for order in orders), slots)

    def sends(pairs):
        return [send for _, send in pairs]

    def over_bands(sums, groups):
        return [lax.psum(v, "dp", axis_index_groups=groups) for v in sums]

    pieces = tuple(piece(o, 0) for o in orders)
    leads = tuple(o[0] for o in orders)
    front = (conv, after(stats, we_peer, wp_peer), par)
    *q1, act, stat = hidden_layer(None, bg, we_peer, wp_peer, eb_peer, 0, first, flags, front=front)
    we_own = flip_bit(after(we_peer, act), "dp", 0)
    wp_own = flip_bit(after(wp_peer, act), "dp", 0)
    c1 = other_core(q1[2:4])
    q2 = hidden_layer(act, bg, we_peer, wp_peer, after(eb_peer, q1[0]), first, second, flags)
    c2 = other_core(q2[2:4])
    o1 = hidden_layer(act, bg, we_own, wp_own, after(eb_own, q2[0]), 0, first, flags, c1, pieces, leads)
    s1 = exchanged([(o1[2], o1[3]), (o1[4], o1[5])], 0)
    o2 = hidden_layer(act, bg, we_own, wp_own, after(eb_own, o1[0]), first, second, flags, c2, pieces, leads)
    for n in range(1, len(bits)):
        s1 = split(arrived(s1, o2[0]), n)
        last = sends(s1)
        s1 = exchanged(s1, n)

    s2 = exchanged([(o2[2], after(o2[3], *last)), (o2[4], after(o2[5], *last))], 0)
    eb_sums = (o1[-1], o2[-1], q1[-1], q2[-1])
    cuts = ((1, 0, first), (0, 0, first), (1, first, second), (0, first, second))
    parts = (q1, o1, q2, o2)
    hidden = [p[0] for p in parts]
    da, sums = activation_gradient(
        (we_own, we_peer), [p[1] for p in parts], cuts, conv, after(stat, *last), copies
    )
    sums = lax.all_to_all(sums, devices, 0, 0)
    z_keep, z_send = band_split(flags, arrived(s1, da))
    z_came = flip_bit(z_send, "dp", 1)
    for n in range(1, len(bits)):
        s2 = split(arrived(s2, da, z_send), n)
        last = sends(s2)
        s2 = exchanged(s2, n)
    ready = after(sums, *last)
    conv_grad, g_first, g_last, totals = conv_gradient(da, conv, m16, ready, stat, par)
    g_up, g_dn = halo(g_first, g_last)
    z_came, *came = lax.optimization_barrier((z_came, *[v for _, v in s2], conv_grad))
    s2 = round_sums([(keep, v) for (keep, _), v in zip(s2, came)])
    b2 = over_bands(s2, groups)
    half_sum = round_sums([(z_keep, z_came)])[0]
    ready = after(conv_grad, half_sum, *s2)
    tap_local = tap_gradient(flags, x, x_up, x_dn, ready, bg_sum, eb_sums, units, block, share)
    g_up, g_dn, half_sum, _ = lax.optimization_barrier((g_up, g_dn, half_sum, tap_local))
    half_came = flip_bit(half_sum, "dp", 2)
    bands = n_dp.bit_length() - 1

    local = lax.all_to_all(tap_local, "fsdp", 0, 0)
    input_grad = input_gradient(conv_grad, g_up, g_dn, after(par, tap_local), og, m16, block)
    half_came, _ = lax.optimization_barrier((half_came, input_grad))
    half_sum = round_sums([(half_sum, half_came)])[0]
    for bit in range(3, bands):
        half_sum = (half_sum.astype(F32) + flip_bit(half_sum, "dp", bit).astype(F32)).astype(BF16)
    half_far = flip_bit(half_sum, "dp", 1)
    local = jnp.sum(after(local, input_grad), axis=0)
    block_out = block_output((wp_own, wp_peer), hidden, cuts, x, m16, after(par, input_grad, local, half_sum))
    local = jnp.sum(after(from_all(local, "dp"), block_out), axis=0)

    half_far, *b2 = lax.optimization_barrier((half_far, *b2, block_out))
    whole_parts = [(v, flip_bit(v, "dp", 0)) for v in b2[:2]]
    half_parts = (half_sum, half_far, flip_bit(half_sum, "dp", 0), flip_bit(half_far, "dp", 0))
    starts = ((first, half + first), (0, half))
    project_grad, expand_grad = place_columns(flags, whole_parts, half_parts, starts, share, units)

    start = lax.axis_index("fsdp") * share
    totals = totals.reshape(2, -1)
    per_channel = lambda v: v.reshape(-1)[:channels]
    return (
        block_out.transpose(1, 0, 2)[None],
        input_grad.transpose(1, 0, 2)[None],
        local[:TAPS].T,
        lax.dynamic_slice_in_dim(totals[1], start, share),
        lax.dynamic_slice_in_dim(totals[0], start, share),
        expand_grad,
        local[TAPS + 1 :].reshape(-1),
        project_grad,
        local[TAPS],
        per_channel(stat[0:8]),
        per_channel(stat[16:24]),
    )


def solution(mesh):
    rows = P("fsdp", None, "dp", None)
    return jax.shard_map(
        per_device,
        mesh=mesh,
        in_specs=(
            rows,
            rows,
            P("dp", None),
            P(),
            P("fsdp", None),
            P("fsdp"),
            P("fsdp"),
            P("fsdp", None),
            P("fsdp"),
            P("fsdp", None),
            P("fsdp"),
        ),
        out_specs=(
            rows,
            rows,
            P("fsdp", None),
            P("fsdp"),
            P("fsdp"),
            P("fsdp", None),
            P("fsdp"),
            P("fsdp", None),
            P("fsdp"),
            P(),
            P(),
        ),
        check_vma=False,
    )
```

```python
import functools

import jax
import jax.numpy as jnp
from jax import lax
from jax.experimental import pallas as pl
from jax.experimental.pallas import tpu as pltpu
from jax.sharding import PartitionSpec as P

KS = 7
REACH = KS // 2
TAPS = KS * KS
ROLLOUT = 8
EPS = 1e-05
F32, BF16 = jnp.float32, jnp.bfloat16
GRP = 16
TILE = 256
VMEM = 639 * 2**20 // 10
GELU_A = 0.7978845608028654
GELU_B = 0.044715
NT = (((1,), (1,)), ((), ()))
TN = (((0,), (0,)), ((), ()))


def params():
    return pltpu.CompilerParams(vmem_limit_bytes=VMEM)


def cost(us):
    return pl.CostEstimate(flops=int(us * 1.15e9), bytes_accessed=10**5, transcendentals=0)


def whole(shape):
    zeros = (0,) * len(shape)
    return pl.BlockSpec(shape, lambda *g: zeros, pipeline_mode=pl.Buffered(1))


def roll_lanes(v, shift):
    shift %= v.shape[-1]
    return v if shift == 0 else pltpu.roll(v, shift, v.ndim - 1)


def columns_of(*rows):
    pieces = []
    for k in range(rows[0].shape[0]):
        used = [v[k : k + 1, :] for v in rows]
        block = jnp.concatenate(used + [jnp.zeros((128 - len(rows), 128), F32)], axis=0)
        pieces.append(block.T)
    return jnp.concatenate(pieces, axis=0)


def wide(column):
    return jnp.broadcast_to(column, (column.shape[0], 128))


def copies_of(cols, out_ref):
    copies = out_ref.shape[0]
    for k in range(cols.shape[0] // 128):
        block = cols[k * 128 : (k + 1) * 128, :].T
        for q in range(2):
            row = jnp.broadcast_to(block[q : q + 1, :][None], (copies, 1, 128))
            out_ref[:, 8 * q + k : 8 * q + k + 1, :] = row


def spread_taps(cols, pick_ref, e_ref):
    count = cols.shape[0]
    lane = lax.broadcasted_iota(jnp.int32, (count, 128), 1)
    own = lax.broadcasted_iota(jnp.int32, (count, 128), 0) % GRP == lane % GRP
    high = cols.astype(BF16)
    low = (cols - high.astype(F32)).astype(BF16)
    for h, part in enumerate((high, low)):
        for j in range(KS):
            picked = jnp.dot(part, pick_ref[j], preferred_element_type=F32)
            e_ref[h, j] = jnp.where(own, picked, 0.0).astype(BF16)


def tap_picker():
    tap = lax.broadcasted_iota(jnp.int32, (128, 128), 0)
    lane = lax.broadcasted_iota(jnp.int32, (128, 128), 1)
    inside = lane < KS * GRP
    first = KS * (lane // GRP)
    return [jnp.where((tap == first + j) & inside, 1.0, 0.0).astype(BF16) for j in range(KS)]


def conv_rows(field_ref, taps_ref, s, rows, flip):
    x = field_ref[:, s, :].reshape((rows + 2 * REACH) * GRP, field_ref.shape[-1])
    parts = [taps_ref[h, :, s, :].reshape(KS * GRP, 128)[:, : KS * GRP] for h in range(2)]
    taps = jnp.concatenate(parts, axis=1)
    out = []
    for r in range(rows):
        src = rows - 1 - r if flip else r
        window = x[src * GRP : (src + KS) * GRP]
        sums = jnp.dot(taps, jnp.concatenate([window, window], axis=0), preferred_element_type=F32)
        acc = None
        for j in range(KS):
            moved = roll_lanes(sums[j * GRP : (j + 1) * GRP], j - REACH if flip else REACH - j)
            acc = moved if acc is None else acc + moved
        out.append(acc)
    return out


def conv_kernel(
    x_ref, up_ref, dn_ref, small_ref, m_ref, out_ref, st_ref, par_ref,
    field_ref, cols_ref, e_ref, pick_ref, count_ref, *, share
):
    rows, block = x_ref.shape[0], x_ref.shape[1]
    step = pl.program_id(0)

    @pl.when(step == 0)
    def _():
        for j, pick in enumerate(tap_picker()):
            pick_ref[j] = pick
        count = jnp.sum(jnp.sum(m_ref[...], axis=0), axis=1, keepdims=True)[0:8]
        count_ref[...] = jnp.broadcast_to(count, (8, 128))
        cols_ref[...] = jnp.zeros(cols_ref.shape, F32)
        given, wide = small_ref.shape[1], pl.cdiv(share, 128) * 128
        for f in range(small_ref.shape[0]):
            v = small_ref[f]
            v = jnp.concatenate([v, jnp.zeros((given, wide - share), F32)], axis=1)
            v = jnp.concatenate([v, jnp.zeros((128 - given, wide), F32)], axis=0)
            par_ref[f * share : (f + 1) * share, :] = v.T[:share]

    field_ref[0:REACH] = up_ref[...]
    field_ref[REACH : REACH + rows] = x_ref[...]
    field_ref[REACH + rows :] = dn_ref[...]
    here = pl.multiple_of(step * block, GRP)
    spread_taps(par_ref[pl.ds(here, block), :], pick_ref, e_ref)
    lane = lax.broadcasted_iota(jnp.int32, (GRP, 128), 1)
    inv_n = 1.0 / jnp.maximum(count_ref[0:1, 0:1], 1.0)
    for g in range(block // GRP):
        s = pl.ds(g * GRP, GRP)
        acc = conv_rows(field_ref, e_ref, s, rows, False)
        total = None
        for r in range(rows):
            out_ref[r, s, :] = acc[r]
            v = acc[r] * m_ref[r]
            total = v if total is None else total + v
        mean = jnp.sum(total, axis=-1, keepdims=True) * inv_n
        total = None
        for r in range(rows):
            d = acc[r] - mean
            v = d * d * m_ref[r]
            total = v if total is None else total + v
        dev = jnp.sum(total, axis=-1, keepdims=True)
        at = pl.multiple_of(step * block + g * GRP, GRP)
        cols_ref[pl.ds(at, GRP), :] = jnp.where(lane == 0, mean, dev)

    @pl.when(step == pl.num_programs(0) - 1)
    def _():
        st_ref[...] = jnp.broadcast_to(count_ref[0:1, :][None], st_ref.shape)
        copies_of(cols_ref[...], st_ref)


def conv_forward(x, up, dn, small, m16, copies, block):
    rows, channels, width = x.shape
    n_fs, given, share = small.shape
    padded = pl.cdiv(channels, 128) * 128
    return pl.pallas_call(
        functools.partial(conv_kernel, share=share),
        grid=(channels // block,),
        in_specs=[
            pl.BlockSpec((rows, block, width), lambda g: (0, g, 0)),
            pl.BlockSpec((REACH, block, width), lambda g: (0, g, 0)),
            pl.BlockSpec((REACH, block, width), lambda g: (0, g, 0)),
            whole((n_fs, given, share)),
            whole((rows, GRP, width)),
        ],
        out_specs=[
            pl.BlockSpec((rows, block, width), lambda g: (0, g, 0)),
            pl.BlockSpec((copies, 16, 128), lambda g: (0, 0, 0)),
            pl.BlockSpec((channels, 128), lambda g: (0, 0)),
        ],
        out_shape=[
            jax.ShapeDtypeStruct((rows, channels, width), F32),
            jax.ShapeDtypeStruct((copies, 16, 128), F32),
            jax.ShapeDtypeStruct((channels, 128), F32),
        ],
        scratch_shapes=[
            pltpu.VMEM((rows + 2 * REACH, block, width), BF16),
            pltpu.VMEM((padded, 128), F32),
            pltpu.VMEM((2, KS, block, 128), BF16),
            pltpu.VMEM((KS, 128, 128), BF16),
            pltpu.VMEM((8, 128), F32),
        ],
        compiler_params=params(),
        cost_estimate=cost(0.4),
        name="conv_forward",
    )(x, up, dn, small, m16)


def input_grad_kernel(
    g_ref, up_ref, dn_ref, par_ref, og_ref, m_ref, out_ref, field_ref, e_ref, pick_ref
):
    @pl.when(pl.program_id(0) == 0)
    def _():
        for j, pick in enumerate(tap_picker()):
            pick_ref[j] = pick

    rows, block = g_ref.shape[0], g_ref.shape[1]
    last = rows + 2 * REACH - 1
    for q in range(REACH):
        field_ref[last - q] = up_ref[q]
        field_ref[REACH - 1 - q] = dn_ref[q]
    for q in range(rows):
        field_ref[last - REACH - q] = g_ref[q]
    spread_taps(par_ref[...], pick_ref, e_ref)
    for g in range(block // GRP):
        s = pl.ds(g * GRP, GRP)
        acc = conv_rows(field_ref, e_ref, s, rows, True)
        for r in range(rows):
            out_ref[r, s, :] = og_ref[r, s, :].astype(F32) * m_ref[r] + acc[r]


def input_gradient(grad, up, dn, par, og, m16, block):
    rows, channels, width = grad.shape
    return pl.pallas_call(
        input_grad_kernel,
        grid=(channels // block,),
        in_specs=[
            pl.BlockSpec((rows, block, width), lambda g: (0, g, 0)),
            pl.BlockSpec((REACH, block, width), lambda g: (0, g, 0)),
            pl.BlockSpec((REACH, block, width), lambda g: (0, g, 0)),
            pl.BlockSpec((block, 128), lambda g: (g, 0)),
            pl.BlockSpec((rows, block, width), lambda g: (0, g, 0)),
            whole((rows, GRP, width)),
        ],
        out_specs=pl.BlockSpec((rows, block, width), lambda g: (0, g, 0)),
        out_shape=jax.ShapeDtypeStruct((rows, channels, width), F32),
        scratch_shapes=[
            pltpu.VMEM((rows + 2 * REACH, block, width), BF16),
            pltpu.VMEM((2, KS, block, 128), BF16),
            pltpu.VMEM((KS, 128, 128), BF16),
        ],
        compiler_params=params(),
        cost_estimate=cost(5),
        name="input_gradient",
    )(grad, up, dn, par, og, m16)


def tap_grad_kernel(
    bits_ref, x_ref, up_ref, dn_ref, g_ref, bg_ref, *refs, share
):
    out_ref, field_ref, cols_ref = refs[-3:]
    rows, block, width = x_ref.shape
    field_ref[0:REACH] = up_ref[...]
    field_ref[REACH : REACH + rows] = x_ref[...]
    field_ref[REACH + rows :] = dn_ref[...]
    lane = lax.broadcasted_iota(jnp.int32, (GRP, 128), 1)
    own = lax.broadcasted_iota(jnp.int32, (GRP, 128), 0) == lane % GRP
    for g in range(block // GRP):
        s = pl.ds(g * GRP, GRP)
        x = field_ref[:, s, :].reshape((rows + 2 * REACH) * GRP, width)
        fields = jnp.concatenate([x[r * GRP : (r + KS) * GRP] for r in range(rows)], axis=1)
        grads = []
        for j in range(KS):
            moved = [roll_lanes(g_ref[r, s, :], j - REACH) for r in range(rows)]
            grads.append(jnp.concatenate(moved, axis=1))
        grads = jnp.concatenate(grads, axis=0)
        sums = lax.dot_general(grads, fields, NT, preferred_element_type=F32)
        sums = jnp.concatenate([sums, jnp.zeros((KS * GRP, 128 - KS * GRP), F32)], axis=1)
        out = None
        for j in range(KS):
            acc = jnp.where(own, sums[j * GRP : (j + 1) * GRP], 0.0)
            for k in (8, 4, 2, 1):
                acc = acc + pltpu.roll(acc, 128 - k, 1)
            acc = roll_lanes(acc, j)
            out = acc if out is None else jnp.where(lane % GRP == j, acc, out)
        at = pl.multiple_of(pl.program_id(0) * block + g * GRP, GRP)
        cols_ref[pl.ds(at, GRP), :] = out

    @pl.when(pl.program_id(0) == pl.num_programs(0) - 1)
    def _():
        blocks = [cols_ref[k : k + 128, :].T for k in range(0, cols_ref.shape[0], 128)]
        wide = jnp.concatenate(blocks, axis=1)
        taps = jnp.concatenate([wide[GRP * i : GRP * i + KS] for i in range(KS)], axis=0)
        band = jnp.concatenate([bg_ref[0, k : k + 1, :] for k in range(wide.shape[1] // 128)], axis=1)
        own, peer = (jnp.concatenate([refs[q][...], refs[q + 1][...]], axis=1) for q in (0, 2))
        core = bits_ref[bits_ref.shape[0] - 2]
        units = jnp.concatenate(
            [jnp.where(core == 0, own, peer), jnp.where(core == 0, peer, own)], axis=1
        )
        ratio = out_ref.shape[1] - TAPS - 1
        for f in range(out_ref.shape[0]):
            out_ref[f, 0:TAPS, :] = taps[:, f * share : (f + 1) * share]
            out_ref[f, TAPS : TAPS + 1, :] = band[:, f * share : (f + 1) * share]
            for q in range(ratio):
                at = (f * ratio + q) * share
                out_ref[f, TAPS + 1 + q : TAPS + 2 + q, :] = units[:, at : at + share]


def tap_gradient(bits, x, up, dn, grad, bg_sum, eb_sums, units, block, share):
    rows, channels, width = x.shape
    padded = pl.cdiv(channels, 128) * 128
    height = TAPS + 1 + units // channels
    return pl.pallas_call(
        functools.partial(tap_grad_kernel, share=share),
        grid=(channels // block,),
        in_specs=[
            pl.BlockSpec(memory_space=pltpu.SMEM),
            pl.BlockSpec((rows, block, width), lambda g: (0, g, 0)),
            pl.BlockSpec((REACH, block, width), lambda g: (0, g, 0)),
            pl.BlockSpec((REACH, block, width), lambda g: (0, g, 0)),
            pl.BlockSpec((rows, block, width), lambda g: (0, g, 0)),
            whole(bg_sum.shape),
        ]
        + [whole(v.shape) for v in eb_sums],
        out_specs=pl.BlockSpec((channels // share, height, share), lambda g: (0, 0, 0)),
        out_shape=jax.ShapeDtypeStruct((channels // share, height, share), F32),
        scratch_shapes=[
            pltpu.VMEM((rows + 2 * REACH, block, width), BF16),
            pltpu.VMEM((padded, 128), F32),
        ],
        compiler_params=params(),
        cost_estimate=cost(15),
        name="tap_gradient",
    )(bits, x, up, dn, grad, bg_sum, *eb_sums)


def mask_grad_kernel(og_ref, m_ref, out_ref, sum_ref, cols_ref):
    row = pl.program_id(0)
    channels = og_ref.shape[1]
    width = og_ref.shape[2]
    part = None
    for r in range(og_ref.shape[0]):
        v = og_ref[r].astype(F32) * m_ref[r, 0:1]
        out_ref[:, r * width : (r + 1) * width] = v.astype(BF16)
        for k in range(0, width, 128):
            piece = v[:, k : k + 128]
            part = piece if part is None else part + piece

    @pl.when(row == 0)
    def _():
        cols_ref[...] = jnp.zeros(cols_ref.shape, F32)

    cols_ref[0:channels, :] += part

    @pl.when(row == pl.num_programs(0) - 1)
    def _():
        sums = jnp.broadcast_to(jnp.sum(cols_ref[...], axis=1, keepdims=True), cols_ref.shape)
        copies_of(sums, sum_ref)


def mask_gradient(og, m16):
    rows, channels, width = og.shape
    padded = pl.cdiv(channels, 128) * 128
    pixels = rows * width
    return pl.pallas_call(
        mask_grad_kernel,
        grid=(rows // REACH,),
        in_specs=[
            pl.BlockSpec((REACH, channels, width), lambda r: (r, 0, 0)),
            pl.BlockSpec((REACH, GRP, width), lambda r: (r, 0, 0)),
        ],
        out_specs=[
            pl.BlockSpec((channels, REACH * width), lambda r: (0, r)),
            pl.BlockSpec((1, 16, 128), lambda r: (0, 0, 0)),
        ],
        out_shape=[
            jax.ShapeDtypeStruct((channels, pixels), BF16),
            jax.ShapeDtypeStruct((1, 16, 128), F32),
        ],
        scratch_shapes=[pltpu.VMEM((padded, 128), F32)],
        compiler_params=params(),
        cost_estimate=cost(0.1),
        name="mask_gradient",
    )(og, m16)


def activate(conv_ref, all_ref, par_ref, act_ref, stat_ref):
    rows, channels, width = conv_ref.shape
    means, squares = all_ref[:, 0:8, :], all_ref[:, 8:16, :]
    counts = all_ref[:, 7:8, :]
    count = jnp.sum(counts, axis=0)
    mean = jnp.sum(counts * means, axis=0) / count
    apart = means - mean[None]
    variance = jnp.sum(squares + counts * apart * apart, axis=0) / count
    inv_std = lax.rsqrt(variance + EPS)
    stat_ref[0:8] = mean
    stat_ref[8:16] = inv_std
    stat_ref[16:24] = jnp.sqrt(variance + EPS)
    stat_ref[24:32] = jnp.broadcast_to(count, (8, 128))
    c, p = columns_of(mean[0:7], inv_std[0:7])[:channels], par_ref[...]
    centre = wide(c[:, 0:1])
    scale = wide(c[:, 1:2] * p[:, TAPS : TAPS + 1])
    shift = wide(p[:, TAPS + 1 : TAPS + 2])
    for r in range(rows):
        for k in range(0, width, 128):
            v = (conv_ref[r, :, k : k + 128] - centre) * scale + shift
            act_ref[:, r * width + k : r * width + k + 128] = v.astype(BF16)


def gelu_parts(v):
    v2 = v * v
    t = jnp.tanh(v * (GELU_A + (GELU_A * GELU_B) * v2))
    s = 0.5 * t + 0.5
    h = v * s
    return h, s + h * (1.0 - s) * (2 * GELU_A + (6 * GELU_A * GELU_B) * v2)


def halves(v, mine, piece):
    keep, send = [], []
    for o in range(0, v.shape[0], 2 * piece):
        first, second = v[o : o + piece], v[o + piece : o + 2 * piece]
        keep.append(jnp.where(mine == 0, first, second))
        send.append(jnp.where(mine == 0, second, first))
    return jnp.concatenate(keep, axis=0), jnp.concatenate(send, axis=0)


def hidden_kernel(bits_ref, bg_ref, we_ref, wp_ref, eb_ref, *refs, step, pieces, slots, leads):
    if leads:
        conv_ref, all_ref, par_ref, h_ref, g_ref, dwp_ref, dwe_ref, ebg_ref, act_ref, stat_ref = refs

        @pl.when(pl.program_id(0) == 0)
        def _():
            activate(conv_ref, all_ref, par_ref, act_ref, stat_ref)

    else:
        act_ref, refs = refs[0], refs[1:]
    if leads:
        pass
    elif pieces is None:
        h_ref, g_ref, dwp_ref, dwe_ref, ebg_ref = refs
    else:
        other_p, other_e, h_ref, g_ref, keep_p, send_p, keep_e, send_e, ebg_ref = refs
    we, wp, bias = we_ref[...], wp_ref[...], eb_ref[...]
    total = None
    for p in range(0, act_ref.shape[1], step):
        pre = lax.dot_general(act_ref[:, p : p + step], we, TN, preferred_element_type=F32) + bias
        pull = lax.dot_general(bg_ref[:, p : p + step], wp, TN, preferred_element_type=F32)
        h, slope = gelu_parts(pre)
        grad = (pull * slope).astype(BF16)
        h_ref[p : p + step, :] = h.astype(BF16)
        g_ref[p : p + step, :] = grad
        part = jnp.sum(grad.astype(F32), axis=0, keepdims=True)
        total = part if total is None else total + part
    ebg_ref[...] = total
    dwp = jnp.dot(bg_ref[...], h_ref[...], preferred_element_type=F32)
    dwe = jnp.dot(act_ref[...], g_ref[...], preferred_element_type=F32)
    if pieces is None:
        dwp_ref[...] = dwp.astype(BF16)
        dwe_ref[...] = dwe.astype(BF16)
    else:
        keep, send = halves(dwp + other_p[...].astype(F32), bits_ref[slots[0]], pieces[0])
        keep_p[...] = keep
        send_p[...] = send.astype(BF16)
        keep, send = halves(dwe + other_e[...].astype(F32), bits_ref[slots[1]], pieces[1])
        keep_e[...] = keep
        send_e[...] = send.astype(BF16)


def hidden_layer(act, bg, we, wp, eb, first, units, bits, others=None, pieces=None, slots=None, front=None):
    channels, pixels = bg.shape
    off = first // TILE
    column = lambda rows: pl.BlockSpec((rows, TILE), lambda g: (0, g))
    weight = pl.BlockSpec((channels, TILE), lambda g: (0, g + off))
    shape = lambda rows, dtype: jax.ShapeDtypeStruct((rows, units), dtype)
    in_specs = [pl.BlockSpec(memory_space=pltpu.SMEM), whole(bg.shape), weight, weight]
    in_specs.append(pl.BlockSpec((1, TILE), lambda g: (0, g + off)))
    made = [act] if front is None else list(front)
    operands = [bits, bg, we, wp, eb] + made
    in_specs += [whole(v.shape) for v in made]
    out_specs = [column(pixels), column(pixels)]
    out_shape = [shape(pixels, BF16), shape(pixels, BF16)]
    if others is None:
        out_specs += [column(channels), column(channels)]
        out_shape += [shape(channels, BF16), shape(channels, BF16)]
    else:
        in_specs += [column(channels), column(channels)]
        operands += list(others)
        out_specs += [column(channels // 2)] * 4
        out_shape += [shape(channels // 2, F32), shape(channels // 2, BF16)] * 2
    out_specs.append(column(1))
    out_shape.append(shape(1, F32))
    if front is not None:
        out_specs += [pl.BlockSpec((channels, pixels), lambda g: (0, 0)), pl.BlockSpec((32, 128), lambda g: (0, 0))]
        out_shape += [jax.ShapeDtypeStruct((channels, pixels), BF16), jax.ShapeDtypeStruct((32, 128), F32)]
    return pl.pallas_call(
        functools.partial(hidden_kernel, step=128, pieces=pieces, slots=slots, leads=front is not None),
        grid=(pl.cdiv(units, TILE),),
        in_specs=in_specs,
        out_specs=out_specs,
        out_shape=out_shape,
        compiler_params=params(),
        cost_estimate=cost(0.3),
        name="hidden_layer",
    )(*operands)


def split_kernel(bits_ref, *refs, pieces, slots):
    n = len(pieces)
    for k, (piece, slot) in enumerate(zip(pieces, slots, strict=True)):
        total = refs[2 * k][...] + refs[2 * k + 1][...].astype(F32)
        keep, send = halves(total, bits_ref[slot], piece)
        refs[2 * n + 2 * k][...] = keep
        refs[2 * n + 2 * k + 1][...] = send.astype(BF16)


def split_sums(bits, pairs, pieces, slots):
    rows, cols = pairs[0][0].shape
    shape = lambda dtype: jax.ShapeDtypeStruct((rows // 2, cols), dtype)
    spec = lambda height: pl.BlockSpec((height, cols), lambda: (0, 0))
    out = pl.pallas_call(
        functools.partial(split_kernel, pieces=pieces, slots=slots),
        in_specs=[pl.BlockSpec(memory_space=pltpu.SMEM)] + [spec(rows)] * (2 * len(pairs)),
        out_specs=[spec(rows // 2)] * (2 * len(pairs)),
        out_shape=[shape(F32), shape(BF16)] * len(pairs),
        compiler_params=params(),
        cost_estimate=cost(3),
        name="split_sums",
    )(bits, *[v for pair in pairs for v in pair])
    return [(out[2 * k], out[2 * k + 1]) for k in range(len(pairs))]


def band_split_kernel(bits_ref, *refs):
    keep_ref, send_ref = refs[-2:]
    rows = keep_ref.shape[1]
    band = bits_ref[bits_ref.shape[0] - 1]
    for k in range(keep_ref.shape[0]):
        total = refs[2 * k][...] + refs[2 * k + 1][...].astype(F32)
        low, high = total[:rows], total[total.shape[0] - rows :]
        keep_ref[k] = jnp.where(band == 0, low, high)
        send_ref[k] = jnp.where(band == 0, high, low).astype(BF16)


def band_split(bits, pairs):
    share, cols = pairs[0][0].shape
    rows = pl.cdiv(pl.cdiv(share, 2), 8) * 8
    spec = pl.BlockSpec((share, cols), lambda: (0, 0))
    out = pl.BlockSpec((len(pairs), rows, cols), lambda: (0, 0, 0))
    shape = lambda dtype: jax.ShapeDtypeStruct((len(pairs), rows, cols), dtype)
    return pl.pallas_call(
        band_split_kernel,
        in_specs=[pl.BlockSpec(memory_space=pltpu.SMEM)] + [spec] * (2 * len(pairs)),
        out_specs=[out, out],
        out_shape=[shape(F32), shape(BF16)],
        compiler_params=params(),
        cost_estimate=cost(3),
        name="band_split",
    )(bits, *[v for pair in pairs for v in pair])


def round_kernel(*refs):
    n = len(refs) // 3
    for k in range(n):
        total = refs[2 * k][...].astype(F32) + refs[2 * k + 1][...].astype(F32)
        refs[2 * n + k][...] = total.astype(BF16)


def round_sums(pairs):
    shape = pairs[0][0].shape
    spec = pl.BlockSpec(shape, lambda: (0,) * len(shape))
    return pl.pallas_call(
        round_kernel,
        in_specs=[spec] * (2 * len(pairs)),
        out_specs=[spec] * len(pairs),
        out_shape=[jax.ShapeDtypeStruct(pairs[0][0].shape, BF16)] * len(pairs),
        compiler_params=params(),
        cost_estimate=cost(3),
        name="round_sums",
    )(*[v for pair in pairs for v in pair])


def contract(weights, hiddens):
    total = None
    for (w_ref, first, units), h_ref in zip(weights, hiddens, strict=True):
        part = lax.dot_general(
            w_ref[:, first : first + units], h_ref[...], NT, preferred_element_type=F32
        )
        total = part if total is None else total + part
    return total


def act_grad_kernel(*refs, cuts):
    n = len(cuts)
    w_refs, h_refs = refs[0:2], refs[2 : 2 + n]
    conv_ref, stat_ref, out_ref, sum_ref, cols_ref, acc_ref = refs[2 + n :]
    channels = conv_ref.shape[1]
    row = pl.program_id(0)

    @pl.when(row == 0)
    def _():
        cols_ref[...] = columns_of(stat_ref[0:7], stat_ref[8:15])[: cols_ref.shape[0]]
        acc_ref[...] = jnp.zeros(acc_ref.shape, F32)

    grad = contract([(w_refs[w], first, units) for w, first, units in cuts], h_refs)
    out_ref[0] = grad
    c = cols_ref[0:channels, :]
    scaled = grad * ((conv_ref[0] - c[:, 0:1]) * c[:, 1:2])
    plain, weighted = grad[:, 0:128], scaled[:, 0:128]
    for k in range(128, grad.shape[1], 128):
        plain = plain + grad[:, k : k + 128]
        weighted = weighted + scaled[:, k : k + 128]
    acc_ref[0, 0:channels, :] += plain
    acc_ref[1, 0:channels, :] += weighted

    @pl.when(row == pl.num_programs(0) - 1)
    def _():
        lane = lax.broadcasted_iota(jnp.int32, cols_ref.shape, 1)
        plain = jnp.sum(acc_ref[0], axis=1, keepdims=True)
        weighted = jnp.sum(acc_ref[1], axis=1, keepdims=True)
        sum_ref[...] = jnp.zeros(sum_ref.shape, F32)
        copies_of(jnp.where(lane == 0, plain, weighted), sum_ref)


def activation_gradient(weights, hiddens, cuts, conv, stat, copies):
    rows, channels, width = conv.shape
    padded = pl.cdiv(channels, 128) * 128
    return pl.pallas_call(
        functools.partial(act_grad_kernel, cuts=cuts),
        grid=(rows,),
        in_specs=[whole(w.shape) for w in weights]
        + [pl.BlockSpec((width, h.shape[1]), lambda r: (r, 0)) for h in hiddens]
        + [pl.BlockSpec((1, channels, width), lambda r: (r, 0, 0)), whole(stat.shape)],
        out_specs=[
            pl.BlockSpec((1, channels, width), lambda r: (r, 0, 0)),
            pl.BlockSpec((copies, 16, 128), lambda r: (0, 0, 0)),
        ],
        out_shape=[
            jax.ShapeDtypeStruct((rows, channels, width), F32),
            jax.ShapeDtypeStruct((copies, 16, 128), F32),
        ],
        scratch_shapes=[pltpu.VMEM((padded, 128), F32), pltpu.VMEM((2, padded, 128), F32)],
        compiler_params=params(),
        cost_estimate=cost(0.3),
        name="activation_gradient",
    )(*weights, *hiddens, conv, stat)


def block_out_kernel(*refs, cuts):
    n = len(cuts)
    w_refs, h_refs = refs[0:2], refs[2 : 2 + n]
    x_ref, m_ref, par_ref = refs[2 + n : 5 + n]
    out_ref = refs[-1]
    branch = contract([(w_refs[w], first, units) for w, first, units in cuts], h_refs)
    branch = branch + par_ref[:, TAPS + 2 : TAPS + 3]
    out_ref[0] = ((x_ref[0].astype(F32) + branch) * m_ref[0, 0:1]).astype(BF16)


def block_output(weights, hiddens, cuts, x, m16, par):
    rows, channels, width = x.shape
    return pl.pallas_call(
        functools.partial(block_out_kernel, cuts=cuts),
        grid=(rows,),
        in_specs=[whole(w.shape) for w in weights]
        + [pl.BlockSpec((width, h.shape[1]), lambda r: (r, 0)) for h in hiddens]
        + [
            pl.BlockSpec((1, channels, width), lambda r: (r, 0, 0)),
            pl.BlockSpec((1, GRP, width), lambda r: (r, 0, 0)),
            whole(par.shape),
        ],
        out_specs=pl.BlockSpec((1, channels, width), lambda r: (r, 0, 0)),
        out_shape=jax.ShapeDtypeStruct((rows, channels, width), BF16),
        compiler_params=params(),
        cost_estimate=cost(5),
        name="block_output",
    )(*weights, *hiddens, x, m16, par)


def conv_grad_kernel(
    da_ref, conv_ref, m_ref, all_ref, stat_ref, par_ref, out_ref, top_ref, end_ref, sum_ref, cols_ref
):
    row = pl.program_id(0)
    channels = conv_ref.shape[1]

    @pl.when(pl.program_id(0) == 0)
    def _():
        sums = jnp.sum(all_ref[...], axis=0)
        sum_ref[...] = sums
        count = stat_ref[24:32]
        c = columns_of(
            stat_ref[0:7], stat_ref[8:15], (sums[0:8] / count)[0:7], (sums[8:16] / count)[0:7]
        )[:channels]
        factor = c[:, 1:2] * par_ref[:, TAPS : TAPS + 1]
        cols_ref[0] = wide(c[:, 0:1])
        cols_ref[1] = wide(factor)
        cols_ref[2] = wide(factor * c[:, 2:3])
        cols_ref[3] = wide(factor * c[:, 1:2] * c[:, 3:4])

    for r in range(out_ref.shape[0]):
        for k in range(0, out_ref.shape[2], 128):
            s = slice(k, k + 128)
            apart = conv_ref[r, :, s] - cols_ref[0]
            correction = m_ref[r, 0:1, s] * (cols_ref[2] + apart * cols_ref[3])
            out_ref[r, :, s] = (cols_ref[1] * da_ref[r, :, s] - correction).astype(BF16)

    @pl.when(row == 0)
    def _():
        top_ref[...] = out_ref[...]

    @pl.when(row == pl.num_programs(0) - 1)
    def _():
        end_ref[...] = out_ref[...]


def conv_gradient(da, conv, m16, sums, stat, par):
    rows, channels, width = conv.shape
    return pl.pallas_call(
        conv_grad_kernel,
        grid=(rows // REACH,),
        in_specs=[
            pl.BlockSpec((REACH, channels, width), lambda r: (r, 0, 0)),
            pl.BlockSpec((REACH, channels, width), lambda r: (r, 0, 0)),
            pl.BlockSpec((REACH, GRP, width), lambda r: (r, 0, 0)),
            whole(sums.shape),
            whole(stat.shape),
            whole(par.shape),
        ],
        out_specs=[
            pl.BlockSpec((REACH, channels, width), lambda r: (r, 0, 0)),
            pl.BlockSpec((REACH, channels, width), lambda r: (0, 0, 0)),
            pl.BlockSpec((REACH, channels, width), lambda r: (0, 0, 0)),
            pl.BlockSpec((16, 128), lambda r: (0, 0)),
        ],
        out_shape=[
            jax.ShapeDtypeStruct((rows, channels, width), BF16),
            jax.ShapeDtypeStruct((REACH, channels, width), BF16),
            jax.ShapeDtypeStruct((REACH, channels, width), BF16),
            jax.ShapeDtypeStruct((16, 128), F32),
        ],
        scratch_shapes=[pltpu.VMEM((4, channels, 128), F32)],
        compiler_params=params(),
        cost_estimate=cost(0.2),
        name="conv_gradient",
    )(da, conv, m16, sums, stat, par)


def join_kernel(index_ref, *refs, names, share):
    n = len(names)
    for index in names:

        @pl.when(index_ref[0] == index)
        def _(index=index):
            for w in range(2):
                for k, name in enumerate(names):
                    row = (index ^ name) * share
                    refs[2 * n + w][row : row + share, :] = refs[w * n + k][...]


def join_pieces(index, first, second):
    names = sorted(first)
    share, cols = first[0].shape
    channels = share * len(names)
    if share % 8:
        out = []
        for pieces in (first, second):
            whole_array = jnp.zeros((channels, cols), BF16)
            for name in names:
                start = (index ^ name) * share
                whole_array = lax.dynamic_update_slice_in_dim(whole_array, pieces[name], start, axis=0)
            out.append(whole_array)
        return out
    tile = 2 * TILE
    column = lambda height: pl.BlockSpec((height, tile), lambda g: (0, g))
    return pl.pallas_call(
        functools.partial(join_kernel, names=names, share=share),
        grid=(pl.cdiv(cols, tile),),
        in_specs=[pl.BlockSpec(memory_space=pltpu.SMEM)] + [column(share)] * (2 * len(names)),
        out_specs=[column(channels)] * 2,
        out_shape=[jax.ShapeDtypeStruct((channels, cols), BF16)] * 2,
        compiler_params=params(),
        cost_estimate=cost(0.1),
        name="join_pieces",
    )(index[None], *[first[k] for k in names], *[second[k] for k in names])


def place_kernel(flags_ref, *refs, starts):
    outs = refs[-2:]
    core, band = flags_ref[flags_ref.shape[0] - 2], flags_ref[flags_ref.shape[0] - 1]
    (low, high), (low_half, high_half) = starts

    def put(out_ref, rows, at, v):
        wide = min(v.shape[1], out_ref.shape[1] - at)
        out_ref[rows, at : at + wide] = v[:, :wide]

    for w, out_ref in enumerate(outs):
        share = out_ref.shape[0]
        mine, other = refs[2 * w][...].astype(F32), refs[2 * w + 1][...].astype(F32)
        put(out_ref, slice(0, share), low, jnp.where(core == 0, mine, other))
        put(out_ref, slice(0, share), high, jnp.where(core == 0, other, mine))
        own, far, own_other, far_other = (ref[w].astype(F32) for ref in refs[4:8])
        rows = own.shape[0]
        both = []
        for near, away in ((own, far), (own_other, far_other)):
            first = jnp.where(band == 0, near, away)
            last = jnp.where(band == 0, away, near)[2 * rows - share :]
            both.append((first, last))
        for part, at in ((slice(0, rows), 0), (slice(rows, share), 1)):
            put(out_ref, part, low_half, jnp.where(core == 0, both[0][at], both[1][at]))
            put(out_ref, part, high_half, jnp.where(core == 0, both[1][at], both[0][at]))


def place_columns(flags, whole_parts, half_parts, starts, share, units):
    operands = [v for pair in whole_parts for v in pair] + list(half_parts)
    return pl.pallas_call(
        functools.partial(place_kernel, starts=starts),
        in_specs=[pl.BlockSpec(memory_space=pltpu.SMEM)]
        + [pl.BlockSpec(v.shape, lambda n=v.ndim: (0,) * n) for v in operands],
        out_specs=[pl.BlockSpec((share, units), lambda: (0, 0))] * 2,
        out_shape=[jax.ShapeDtypeStruct((share, units), F32)] * 2,
        compiler_params=params(),
        cost_estimate=cost(0.1),
        name="place_columns",
    )(flags, *operands)


def halo(first, last):
    size = lax.axis_size("dp")
    up = [(i, i + 1) for i in range(size - 1)]
    down = [(j, i) for i, j in up]
    return (
        lax.ppermute(last, "dp", up),
        lax.ppermute(first, "dp", down),
    )


def after(value, *others):
    return lax.optimization_barrier((value,) + others)[0]


def from_all(values, axis):
    copies = jnp.broadcast_to(values[None], (lax.axis_size(axis),) + values.shape)
    return lax.all_to_all(copies, axis, 0, 0)


def flip_bit(values, axis, bit):
    size = lax.axis_size(axis)
    return lax.ppermute(values, axis, [(i, i ^ (1 << bit)) for i in range(size)])


def bit_of(axis, bit):
    return (lax.axis_index(axis) >> bit) & 1


def gather_pieces(own, order):
    return {0: own} | {1 << bit: flip_bit(own, "fsdp", bit) for bit in order}


def gather_others(have, order, *others):
    reached = {0: have[0]}
    for bit in order:
        for name, v in list(reached.items()):
            far = have.get(name | 1 << bit)
            reached[name | 1 << bit] = far if far is not None else flip_bit(after(v, *others), "fsdp", bit)
    return reached


def per_device(
    inputs,
    out_grad,
    ocean_mask,
    rollout_lengths,
    conv_weight,
    norm_gain,
    norm_bias,
    expand_weight,
    expand_bias,
    project_weight,
    project_bias,
):
    channels, rows, width = inputs.shape[1:]
    n_fs, n_dp = lax.axis_size("fsdp"), lax.axis_size("dp")
    devices = ("dp", "fsdp")
    share = conv_weight.shape[0]
    units = expand_weight.shape[1]
    half = pl.cdiv(units // 128, 2) * 128
    bits = list(range(n_fs.bit_length() - 1))
    core = bit_of("dp", 0)
    x = inputs[0].transpose(1, 0, 2)
    og = out_grad[0].transpose(1, 0, 2)
    block = 5 * GRP

    ratio = expand_bias.shape[0] // share
    x_first, x_last = x[:REACH], x[-REACH:]
    small = jnp.concatenate(
        [
            after(conv_weight, x_first, x_last).T,
            norm_gain[None],
            norm_bias[None],
            project_bias.astype(F32)[None],
            expand_bias.astype(F32).reshape(ratio, share),
        ],
        axis=0,
    )
    every = from_all(small, "fsdp")
    e_bias = jnp.pad(every[:, TAPS + 3 :].reshape(1, units), ((0, 0), (0, 2 * half - units)))
    x_up, x_dn = halo(x_first, x_last)

    def columns(weight):
        weight = after(weight, every)
        high = jnp.pad(weight[:, half:], ((0, 0), (0, 2 * half - units)))
        return jnp.where(core == 0, high, weight[:, :half])

    eb_own = lax.dynamic_slice_in_dim(e_bias, core * half, half, axis=1)
    eb_peer = lax.dynamic_slice_in_dim(e_bias, (1 - core) * half, half, axis=1)

    sample = lax.axis_index("fsdp")
    length = lax.dynamic_index_in_dim(rollout_lengths, sample, keepdims=False)
    live = jnp.where(sample % ROLLOUT < length, 1.0, 0.0).astype(F32)
    weight = live * ocean_mask.astype(F32)
    m16 = jnp.broadcast_to(weight[:, None, :], (rows, GRP, width))

    we_pieces = gather_pieces(columns(expand_weight), bits)
    wp_pieces = gather_pieces(columns(project_weight), bits[::-1])

    copies = n_fs * n_dp
    orders = (bits[::-1], bits)
    flags = jnp.stack([bit_of("fsdp", bit) for bit in bits] + [core, bit_of("dp", 1)]).astype(jnp.int32)
    bg, bg_sum = mask_gradient(og, after(m16, we_pieces[0], wp_pieces[0]))
    early = [p[1 << b] for p, b in ((we_pieces, bits[0]), (wp_pieces, bits[-1]))]
    we_pieces = gather_others(we_pieces, bits, bg)
    wp_pieces = gather_others(wp_pieces, bits[::-1], bg)
    ready, eb_own, eb_peer, flags, *_ = lax.optimization_barrier(
        (m16, eb_own, eb_peer, flags, bg, *early)
    )
    conv, stats, par = conv_forward(x, x_up, x_dn, every, ready, copies, block)
    stats = lax.all_to_all(stats, devices, 0, 0)
    index = lax.axis_index("fsdp")
    far = n_fs - 1
    we_pieces[far], wp_pieces[far], index, _ = lax.optimization_barrier(
        (we_pieces[far], wp_pieces[far], index, conv)
    )
    we_peer, wp_peer = join_pieces(index, we_pieces, wp_pieces)
    groups = [[i for i in range(n_dp) if i % 2 == c] for c in range(2)]
    first = half // (2 * TILE) * TILE
    second = half - first

    def piece(order, n):
        return share << len([b for b in order[n + 1 :] if b < order[n]])

    def other_core(grads):
        return [flip_bit(v, "dp", 0) for v in grads]

    def exchanged(pairs, n):
        return [(keep, flip_bit(send, "fsdp", o[n])) for (keep, send), o in zip(pairs, orders, strict=True)]

    def arrived(pairs, *cover):
        came = lax.optimization_barrier((*[came for _, came in pairs], *cover))
        return [(keep, v) for (keep, _), v in zip(pairs, came)]

    def split(pairs, n):
        slots = tuple(order[n] for order in orders)
        return split_sums(flags, pairs, tuple(piece(order, n) for order in orders), slots)

    def sends(pairs):
        return [send for _, send in pairs]

    def over_bands(sums, groups):
        return [lax.psum(v, "dp", axis_index_groups=groups) for v in sums]

    pieces = tuple(piece(o, 0) for o in orders)
    leads = tuple(o[0] for o in orders)
    front = (conv, after(stats, we_peer, wp_peer), par)
    *q1, act, stat = hidden_layer(None, bg, we_peer, wp_peer, eb_peer, 0, first, flags, front=front)
    we_own = flip_bit(after(we_peer, act), "dp", 0)
    wp_own = flip_bit(after(wp_peer, act), "dp", 0)
    c1 = other_core(q1[2:4])
    q2 = hidden_layer(act, bg, we_peer, wp_peer, after(eb_peer, q1[0]), first, second, flags)
    c2 = other_core(q2[2:4])
    o1 = hidden_layer(act, bg, we_own, wp_own, after(eb_own, q2[0]), 0, first, flags, c1, pieces, leads)
    s1 = exchanged([(o1[2], o1[3]), (o1[4], o1[5])], 0)
    o2 = hidden_layer(act, bg, we_own, wp_own, after(eb_own, o1[0]), first, second, flags, c2, pieces, leads)
    for n in range(1, len(bits)):
        s1 = split(arrived(s1, o2[0]), n)
        last = sends(s1)
        s1 = exchanged(s1, n)

    s2 = exchanged([(o2[2], after(o2[3], *last)), (o2[4], after(o2[5], *last))], 0)
    eb_sums = (o1[-1], o2[-1], q1[-1], q2[-1])
    cuts = ((1, 0, first), (0, 0, first), (1, first, second), (0, first, second))
    parts = (q1, o1, q2, o2)
    hidden = [p[0] for p in parts]
    da, sums = activation_gradient(
        (we_own, we_peer), [p[1] for p in parts], cuts, conv, after(stat, *last), copies
    )
    sums = lax.all_to_all(sums, devices, 0, 0)
    z_keep, z_send = band_split(flags, arrived(s1, da))
    z_came = flip_bit(z_send, "dp", 1)
    for n in range(1, len(bits)):
        s2 = split(arrived(s2, da, z_send), n)
        last = sends(s2)
        s2 = exchanged(s2, n)
    ready = after(sums, *last)
    conv_grad, g_first, g_last, totals = conv_gradient(da, conv, m16, ready, stat, par)
    g_up, g_dn = halo(g_first, g_last)
    z_came, *came = lax.optimization_barrier((z_came, *[v for _, v in s2], conv_grad))
    s2 = round_sums([(keep, v) for (keep, _), v in zip(s2, came)])
    b2 = over_bands(s2, groups)
    half_sum = round_sums([(z_keep, z_came)])[0]
    ready = after(conv_grad, half_sum, *s2)
    tap_local = tap_gradient(flags, x, x_up, x_dn, ready, bg_sum, eb_sums, units, block, share)
    g_up, g_dn, half_sum, _ = lax.optimization_barrier((g_up, g_dn, half_sum, tap_local))
    half_came = flip_bit(half_sum, "dp", 2)
    bands = n_dp.bit_length() - 1

    local = lax.all_to_all(tap_local, "fsdp", 0, 0)
    input_grad = input_gradient(conv_grad, g_up, g_dn, after(par, tap_local), og, m16, block)
    half_came, _ = lax.optimization_barrier((half_came, input_grad))
    half_sum = round_sums([(half_sum, half_came)])[0]
    for bit in range(3, bands):
        half_sum = (half_sum.astype(F32) + flip_bit(half_sum, "dp", bit).astype(F32)).astype(BF16)
    half_far = flip_bit(half_sum, "dp", 1)
    local = jnp.sum(after(local, input_grad), axis=0)
    block_out = block_output((wp_own, wp_peer), hidden, cuts, x, m16, after(par, input_grad, local, half_sum))
    local = jnp.sum(after(from_all(local, "dp"), block_out), axis=0)

    half_far, *b2 = lax.optimization_barrier((half_far, *b2, block_out))
    whole_parts = [(v, flip_bit(v, "dp", 0)) for v in b2[:2]]
    half_parts = (half_sum, half_far, flip_bit(half_sum, "dp", 0), flip_bit(half_far, "dp", 0))
    starts = ((first, half + first), (0, half))
    project_grad, expand_grad = place_columns(flags, whole_parts, half_parts, starts, share, units)

    start = lax.axis_index("fsdp") * share
    totals = totals.reshape(2, -1)
    per_channel = lambda v: v.reshape(-1)[:channels]
    return (
        block_out.transpose(1, 0, 2)[None],
        input_grad.transpose(1, 0, 2)[None],
        local[:TAPS].T,
        lax.dynamic_slice_in_dim(totals[1], start, share),
        lax.dynamic_slice_in_dim(totals[0], start, share),
        expand_grad,
        local[TAPS + 1 :].reshape(-1),
        project_grad,
        local[TAPS],
        per_channel(stat[0:8]),
        per_channel(stat[16:24]),
    )


def solution(mesh):
    rows = P("fsdp", None, "dp", None)
    return jax.shard_map(
        per_device,
        mesh=mesh,
        in_specs=(
            rows,
            rows,
            P("dp", None),
            P(),
            P("fsdp", None),
            P("fsdp"),
            P("fsdp"),
            P("fsdp", None),
            P("fsdp"),
            P("fsdp", None),
            P("fsdp"),
        ),
        out_specs=(
            rows,
            rows,
            P("fsdp", None),
            P("fsdp"),
            P("fsdp"),
            P("fsdp", None),
            P("fsdp"),
            P("fsdp", None),
            P("fsdp"),
            P(),
            P(),
        ),
        check_vma=False,
    )
```
